32 devices in a mesh: dp: 16 (over z, y, x), mp: 2 (over core).
Axes of the slice: x: 2, y: 2, z: 4, core: 2. Of those that a mesh axis runs over, the one named last changes fastest.
Arguments:
- tokens: bfloat16 [32, 512, 768], P('dp'), may hold values from -6 to 6
- segment_ids: int32 [32, 512], P('dp'), may hold values from 0 to 3, never falling along the last dimension, each value on 1 to 256 neighbouring positions
- cotangent: bfloat16 [32, 512, 768], P('dp'), may hold values from -6 to 6
- attention_master: float32 [4, 768, 768], P(None, 'dp', 'mp'), may hold values from -2 to 2
- attention_first: float32 [4, 768, 768], P(None, 'dp', 'mp'), may hold values from -320 to 320
- attention_second: float32 [4, 768, 768], P(None, 'dp', 'mp'), may hold values from 1310.72 to 20971.52
- dense_master: float32 [2, 768, 3072], P(None, 'dp', 'mp'), may hold values from -0.21875 to 0.21875
- dense_first: float32 [2, 768, 3072], P(None, 'dp', 'mp'), may hold values from -320 to 320
- dense_second: float32 [2, 768, 3072], P(None, 'dp', 'mp'), may hold values from 1310.72 to 20971.52
- head_bias: float32 [2, 768], P(None, 'mp'), may hold values from -3 to 3
- head_bias_first: float32 [2, 768], P(None, 'mp'), may hold values from -448 to 448
- head_bias_second: float32 [2, 768], P(None, 'mp'), may hold values from 2949.12 to 47185.92
- dense_bias: float32 [3072], P('mp'), may hold values from -3 to 3
- dense_bias_first: float32 [3072], P('mp'), may hold values from -224 to 224
- dense_bias_second: float32 [3072], P('mp'), may hold values from 737.28 to 11796.48
- small_vectors: float32 [6, 768], replicated, may hold values from -1 to 2
- small_first: float32 [6, 768], replicated, may hold values from -768 to 768
- small_second: float32 [6, 768], replicated, may hold values from 8192 to 131072
Outputs:
- layer_out: bfloat16 [32, 512, 768], P('dp')
- input_grad: float32 [32, 512, 768], P('dp')
- attention_new: float32 [4, 768, 768], P(None, 'dp', 'mp')
- attention_first_new: float32 [4, 768, 768], P(None, 'dp', 'mp')
- attention_second_new: float32 [4, 768, 768], P(None, 'dp', 'mp')
- attention_copy: bfloat16 [4, 768, 768], P(None, 'dp', 'mp')
- dense_new: float32 [2, 768, 3072], P(None, 'dp', 'mp')
- dense_first_new: float32 [2, 768, 3072], P(None, 'dp', 'mp')
- dense_second_new: float32 [2, 768, 3072], P(None, 'dp', 'mp')
- dense_copy: bfloat16 [2, 768, 3072], P(None, 'dp', 'mp')
- head_bias_new: float32 [2, 768], P(None, 'mp')
- head_bias_first_new: float32 [2, 768], P(None, 'mp')
- head_bias_second_new: float32 [2, 768], P(None, 'mp')
- dense_bias_new: float32 [3072], P('mp')
- dense_bias_first_new: float32 [3072], P('mp')
- dense_bias_second_new: float32 [3072], P('mp')
- small_new: float32 [6, 768], replicated
- small_first_new: float32 [6, 768], replicated
- small_second_new: float32 [6, 768], replicated
The draws below stay inside these ranges and needn't reach their ends.
Inputs may be any that keep to these rules, and one draw needn't show every extreme that they name: `segment_ids`: within each sequence the ids never fall and each id covers one run of positions; a segment holds at most 256 positions.
All inputs are finite; a program needn't handle non-finite values.
Results may differ from the reference program's by a relative error of at most 0.02.
The reference program's roundings to bfloat16 on the way count: a program that leaves them out, or rounds other values in their place, can miss the bound.
Values may be sent and summed in bfloat16 or wider, within the bound.
A program may use at most 128 MiB of HBM per device.

```python
import math
import jax
import jax.numpy as jnp
import numpy as np
from jax import lax

D = 768
HEADS = 12
HEAD_DIM = 64
FF = 3072
LEN = 512
STEP = 5
SEQ_DEV = 2
SEQS = 32
TOKENS = 16384
N_MP = 2


def draw_attention_master(key, part):
    scales = jnp.array([1.3, 1.3, 1.0, 4.0], jnp.float32) * D ** (-0.5)
    normal = jnp.clip(jax.random.normal(key, (4, D, D), jnp.float32), -4.0, 4.0)
    return normal * scales[:, None, None]


def draw_small_vectors(key, part):
    normal = jnp.clip(jax.random.normal(key, (6, D), jnp.float32), -2.0, 2.0) * 0.5
    offset = jnp.array([0.0, 0.0, 1.0, 0.0, 1.0, 0.0], jnp.float32)
    return normal + offset[:, None]


def block_levels(rng, dims, shards, least, largest):
    def one(axis_at, blocks):
        draws = jax.random.uniform(jax.random.fold_in(jax.random.fold_in(rng, 6), axis_at), (blocks,), jnp.float32, least / len(shards), largest / len(shards))
        return jnp.repeat(jnp.exp(draws), dims[axis_at] // blocks).reshape((-1,) + (1,) * (len(dims) - axis_at - 1))

    gain = one(*shards[0])
    for cut in shards[1:]:
        gain = gain * one(*cut)
    return gain


def profile(amount, total, bound, slope):
    weights = [(1 << 20) // math.isqrt(standing ** slope) + 1 for standing in range(2, amount + 1)]
    surplus, counts = total - bound - (amount - 1), [1] * (amount - 1)
    while surplus > 0:
        movable = [i for i in range(amount - 1) if counts[i] < bound]
        whole, budget = sum([weights[i] for i in movable]), surplus
        for i in movable:
            addition = min(bound - counts[i], max(1, budget * weights[i] // whole), surplus)
            counts[i] = counts[i] + addition
            surplus = surplus - addition
    return np.array([bound] + counts)


def uneven_parts(stream_key, number_of, total, most, slope):
    if number_of == 2:
        one = jax.random.randint(stream_key, (), max(1, total - most), min(most, total - 1) + 1)
        return jnp.stack([one, total - one])
    lengths = jnp.asarray(profile(number_of, total, most, slope), jnp.int32)
    couples = (number_of - 1) // 2
    donor, sink = lengths[1:1 + 2 * couples:2], lengths[2:2 + 2 * couples:2]
    room = jnp.minimum(donor - 1, most - sink)
    passed = jax.random.randint(jax.random.fold_in(stream_key, 1), (couples,), 0, 1 << 20) % (room + 1)
    lengths = lengths.at[1:1 + 2 * couples:2].set(donor - passed).at[2:2 + 2 * couples:2].set(sink + passed)
    return lengths[jax.random.permutation(jax.random.fold_in(stream_key, 2), number_of)]


def scatter_about(own_key, shape, width, bound, cuts=(), dtype=jnp.bfloat16):
    entries = jax.random.normal(own_key, shape, jnp.float32) * width
    if len(cuts) > 0:
        entries = block_levels(own_key, shape, cuts, -0.22, 0.18) * entries
    return jnp.clip(entries, min=-bound, max=bound).astype(dtype)


def setup_inputs(seed: int = 0) -> dict:
    key_of = jax.random.split(jax.random.key(seed), 19)
    return {
        "tokens": scatter_about(key_of[0], (SEQS, LEN, D), 1.0, 6.0, ((0, 16),)),
        "segment_ids": jax.vmap(lambda own: jnp.searchsorted(jnp.cumsum(uneven_parts(own, 4, LEN, LEN // 2, 0)), jnp.arange(LEN), side="right"))(jax.random.split(key_of[1], SEQS)).reshape((SEQS, LEN)).astype(jnp.int32),
        "cotangent": scatter_about(key_of[2], (SEQS, LEN, D), 1.0, 6.0, ((0, 16),)),
        "attention_master": draw_attention_master(jax.random.fold_in(key_of[18], 71), 0),
        "attention_first": scatter_about(key_of[4], (4, D, D), (0.4 * TOKENS ** 0.5), 320.0, ((1, 16), (2, 2)), jnp.float32),
        "attention_second": jnp.clip(jnp.exp(math.log(20971.52) - 2.7725887 * jax.random.uniform(key_of[5], (4, D, D), jnp.float32) ** block_levels(key_of[5], (4, D, D), ((1, 16), (2, 2)), -0.2, 0.2)), 1310.72, 20971.52),
        "dense_master": scatter_about(key_of[6], (2, D, FF), D ** -0.5, 0.21875, ((1, 16), (2, 2)), jnp.float32),
        "dense_first": scatter_about(key_of[7], (2, D, FF), (0.4 * TOKENS ** 0.5), 320.0, ((1, 16), (2, 2)), jnp.float32),
        "dense_second": jnp.clip(jnp.exp(math.log(20971.52) - 2.7725887 * jax.random.uniform(key_of[8], (2, D, FF), jnp.float32) ** block_levels(key_of[8], (2, D, FF), ((1, 16), (2, 2)), -0.2, 0.2)), 1310.72, 20971.52),
        "head_bias": scatter_about(key_of[9], (2, D), 0.5, 3.0, ((1, 2),), jnp.float32),
        "head_bias_first": scatter_about(key_of[10], (2, D), (0.6 * TOKENS ** 0.5), 448.0, ((1, 2),), jnp.float32),
        "head_bias_second": jnp.clip(jnp.exp(math.log(47185.92) - 2.7725887 * jax.random.uniform(key_of[11], (2, D), jnp.float32) ** block_levels(key_of[11], (2, D), ((1, 2),), -0.2, 0.2)), 2949.12, 47185.92),
        "dense_bias": scatter_about(key_of[12], (FF,), 0.5, 3.0, ((0, 2),), jnp.float32),
        "dense_bias_first": scatter_about(key_of[13], (FF,), (0.3 * TOKENS ** 0.5), 224.0, ((0, 2),), jnp.float32),
        "dense_bias_second": jnp.clip(jnp.exp(math.log(11796.48) - 2.7725887 * jax.random.uniform(key_of[14], (FF,), jnp.float32) ** block_levels(key_of[14], (FF,), ((0, 2),), -0.2, 0.2)), 737.28, 11796.48),
        "small_vectors": draw_small_vectors(jax.random.fold_in(key_of[18], 71), 0),
        "small_first": scatter_about(key_of[16], (6, D), (1.0 * TOKENS ** 0.5), 768.0, (), jnp.float32),
        "small_second": jnp.clip(jnp.exp(jax.random.uniform(key_of[17], (6, D), jnp.float32, math.log(8192.0), math.log(131072.0))), 8192.0, 131072.0),
    }


highest = lax.Precision.HIGHEST

@jax.custom_vjp
def low(v):
    return lax.optimization_barrier(v.astype(jnp.bfloat16)).astype(jnp.float32)

@jax.custom_vjp
def low_back(v):
    return v

def low_keep(v):
    return (low(v), None)

def low_pass(kept, grad):
    return (grad,)

def back_keep(v):
    return (v, None)

def back_low(kept, grad):
    return (low(grad),)
low.defvjp(low_keep, low_pass)
low_back.defvjp(back_keep, back_low)

def layer_norm(row_values, gain_row, shift_row):
    center = row_values - lax.optimization_barrier(jnp.mean(row_values, axis=-1, keepdims=True))
    spread = lax.optimization_barrier(jnp.mean(center * center, axis=-1, keepdims=True))
    return center * lax.rsqrt(spread + 1e-06) * gain_row + shift_row

def forward(param_set, token_rows, segment_rows):
    attention, dense, head_terms, dense_terms, small_terms = param_set
    weights = low(attention)
    dense_weights = low(dense)
    groups = token_rows.shape[0]
    queries = low_back(low(0.125 * (jnp.einsum('gtd,dc->gtc', token_rows, weights[0], precision=highest) + head_terms[0])))
    key_rows = low_back(low(jnp.einsum('gtd,dc->gtc', token_rows, weights[1], precision=highest)))
    value_rows = low_back(low(jnp.einsum('gtd,dc->gtc', token_rows, weights[2], precision=highest) + head_terms[1]))
    head_shape = (groups, LEN, HEADS, HEAD_DIM)
    scores = low_back(jnp.einsum('gqhd,gkhd->ghqk', queries.reshape(head_shape), key_rows.reshape(head_shape), precision=highest))
    allowed = (segment_rows[:, :, None] == segment_rows[:, None, :])[:, None, :, :]
    scores = jnp.where(allowed, scores, -1000000000.0)
    attend = jax.nn.softmax(scores, axis=-1)
    mixed_heads = jnp.einsum('ghqk,gkhd->gqhd', low(attend), value_rows.reshape(head_shape), precision=highest)
    mixed_heads = low_back(low(mixed_heads.reshape(groups, LEN, D)))
    part_cols = D // N_MP
    out_parts = jnp.einsum('gtmc,emc->mgte', mixed_heads.reshape(groups, LEN, N_MP, part_cols), weights[3].reshape(D, N_MP, part_cols), precision=highest)
    branch = low_back(lax.optimization_barrier(jnp.sum(low(out_parts), axis=0)))
    hidden = layer_norm(token_rows + branch + small_terms[0], small_terms[2], small_terms[3])
    hidden_pre = low_back(jnp.einsum('gtd,df->gtf', low(hidden), dense_weights[0], precision=highest) + dense_terms)
    activated = low(jax.nn.gelu(hidden_pre, approximate=False))
    dense_cols = FF // N_MP
    down_parts = jnp.einsum('gtmf,emf->mgte', activated.reshape(groups, LEN, N_MP, dense_cols), dense_weights[1].reshape(D, N_MP, dense_cols), precision=highest)
    result = hidden + low_back(lax.optimization_barrier(jnp.sum(low(down_parts), axis=0))) + small_terms[1]
    return layer_norm(result, small_terms[4], small_terms[5])

def adamw(parameter, gradient, moment_one, moment_two, learn_rate, weight_decay):
    first_new = 0.5 * moment_one + 0.5 * gradient
    second_new = 0.5 * moment_two + 0.5 * gradient * gradient
    correction = 1.0 - jnp.power(jnp.float32(0.5), jnp.float32(STEP))
    update = first_new / correction / (jnp.sqrt(second_new / correction) + 1e-08)
    return (parameter - learn_rate * update - learn_rate * weight_decay * parameter, first_new, second_new)

def reference(tokens, segment_ids, cotangent, attention_master, attention_first, attention_second, dense_master, dense_first, dense_second, head_bias, head_bias_first, head_bias_second, dense_bias, dense_bias_first, dense_bias_second, small_vectors, small_first, small_second):
    param_set = (attention_master, dense_master, head_bias, dense_bias, small_vectors)
    group_count = SEQS // SEQ_DEV
    token_groups = tokens.astype(jnp.float32).reshape(group_count, SEQ_DEV, LEN, D)
    segment_groups = segment_ids.reshape(group_count, SEQ_DEV, LEN)
    cotangent_groups = cotangent.astype(jnp.float32).reshape(group_count, SEQ_DEV, LEN, D)
    zero_grads = jax.tree.map(jnp.zeros_like, param_set)

    def one_group(totals, pieces):
        token_group, segment_group, cotangent_group = pieces

        def apply_layer(param_values, token_values):
            return forward(param_values, token_values, segment_group)
        output, pullback = jax.vjp(apply_layer, param_set, token_group)
        param_grads, token_grad = pullback(cotangent_group)
        totals = jax.tree.map(jnp.add, totals, param_grads)
        return (totals, (output, token_grad))
    totals, (outputs, token_grads) = lax.scan(one_group, zero_grads, (token_groups, segment_groups, cotangent_groups))
    attention_new, attention_first_new, attention_second_new = adamw(attention_master, totals[0], attention_first, attention_second, 0.03, 0.01)
    dense_new, dense_first_new, dense_second_new = adamw(dense_master, totals[1], dense_first, dense_second, 0.03, 0.01)
    head_new, head_first_new, head_second_new = adamw(head_bias, totals[2], head_bias_first, head_bias_second, 0.2, 0.0)
    dbias_new, dbias_first_new, dbias_second_new = adamw(dense_bias, totals[3], dense_bias_first, dense_bias_second, 0.2, 0.0)
    small_new, small_first_new, small_second_new = adamw(small_vectors, totals[4], small_first, small_second, 0.2, 0.0)
    layer_out = outputs.reshape(SEQS, LEN, D).astype(jnp.bfloat16)
    input_grad = token_grads.reshape(SEQS, LEN, D)
    return (layer_out, input_grad, attention_new, attention_first_new, attention_second_new, attention_new.astype(jnp.bfloat16), dense_new, dense_first_new, dense_second_new, dense_new.astype(jnp.bfloat16), head_new, head_first_new, head_second_new, dbias_new, dbias_first_new, dbias_second_new, small_new, small_first_new, small_second_new)
```

```python
import functools

import jax
import jax.numpy as jnp
from jax import lax
from jax.experimental import pallas as pl
from jax.experimental.pallas import tpu as pltpu
from jax.sharding import PartitionSpec as P

HEAD_DIM = 64
STEP = 5
MESH_ID = pl.DeviceIdType.MESH

first_dims = (((0,), (0,)), ((), ()))
last_dims = (((1,), (1,)), ((), ()))


def norm_forward(row_values, gain_row, shift_row):
    center = row_values - jnp.mean(row_values, axis=-1, keepdims=True)
    inverse = lax.rsqrt(jnp.mean(center * center, axis=-1, keepdims=True) + 1e-06)
    normed = center * inverse
    return (normed * gain_row + shift_row, normed, inverse)


def norm_backward(upstream, normed, inverse, gain_row):
    scaled = upstream * gain_row
    back_rows = inverse * (
        scaled
        - jnp.mean(scaled, axis=-1, keepdims=True)
        - normed * jnp.mean(scaled * normed, axis=-1, keepdims=True)
    )
    return (back_rows, jnp.sum(upstream * normed, axis=0), jnp.sum(upstream, axis=0))


def gelu_value(hidden_pre):
    return 0.5 * hidden_pre * (1.0 + lax.erf(hidden_pre * 0.7071067811865476))


def gelu_slope(hidden_pre):
    return (
        0.5 * (1.0 + lax.erf(hidden_pre * 0.7071067811865476))
        + hidden_pre * jnp.exp(-0.5 * hidden_pre * hidden_pre) * 0.3989422804014327
    )


def masked_scores(queries, key_rows, allowed):
    scores = jnp.einsum("qhd,khd->hqk", queries, key_rows, preferred_element_type=jnp.float32)
    return jnp.where(allowed, scores, -1000000000.0)


def adamw(parameter, gradient, moment_one, moment_two, learn_rate, weight_decay):
    first_new = 0.5 * moment_one + 0.5 * gradient
    second_new = 0.5 * moment_two + 0.5 * gradient * gradient
    correction = 1.0 - jnp.power(jnp.float32(0.5), jnp.float32(STEP))
    update = first_new / correction / (jnp.sqrt(second_new / correction) + 1e-08)
    return (
        parameter - learn_rate * update - learn_rate * weight_decay * parameter,
        first_new,
        second_new,
    )


class Place:
    def __init__(self):
        self.dp = lax.axis_index("dp")
        self.mp = lax.axis_index("mp")
        self.x = self.dp % 2
        self.y = (self.dp // 2) % 2
        self.z = self.dp // 4
        self.z_low = self.z % 2
        self.z_high = self.z // 2
        on_x = self.dp + 1 - 2 * self.x
        on_y = self.dp + 2 - 4 * self.y
        self.near_x = (on_x, self.mp)
        self.near_y = (on_y, self.mp)
        self.near_z = (self.dp + 4 - 8 * self.z_low, self.mp)
        self.far_z = (self.dp + 8 - 16 * self.z_high, self.mp)
        self.core = (self.dp, 1 - self.mp)
        self.one = (on_x + (on_y - on_x) * self.mp, self.mp)
        self.two = (on_y + (on_x - on_y) * self.mp, self.mp)
        self.one_at = (self.y + (1 - 2 * self.y) * self.mp, self.x + (1 - 2 * self.x) * (1 - self.mp))
        self.two_at = (self.y + (1 - 2 * self.y) * (1 - self.mp), self.x + (1 - 2 * self.x) * self.mp)
        self.own_at = (self.y, self.x)
        self.cross_at = (1 - self.y, 1 - self.x)

    def greet(self):
        barrier = pltpu.get_barrier_semaphore()
        partners = (self.near_x, self.near_y, self.near_z, self.far_z, self.core)
        for partner in partners:
            pl.semaphore_signal(barrier, inc=1, device_id=partner, device_id_type=MESH_ID)
        pl.semaphore_wait(barrier, len(partners))


class Sender:
    def __init__(self, send_sems, recv_sems):
        self.send_sems, self.recv_sems, self.used, self.open = send_sems, recv_sems, 0, []

    def start(self, source, target, device):
        copy = pltpu.make_async_remote_copy(
            src_ref=source,
            dst_ref=target,
            send_sem=self.send_sems.at[self.used],
            recv_sem=self.recv_sems.at[self.used],
            device_id=device,
            device_id_type=MESH_ID,
        )
        self.used += 1
        copy.start()
        self.open.append(copy)
        return copy

    def finish(self):
        for copy in self.open:
            copy.wait_send()


def run_pipelined(pieces):
    waiting, running = list(pieces), []
    while waiting or running:
        if waiting:
            running.append(waiting.pop(0))
        for piece in list(running):
            try:
                next(piece)
            except StopIteration:
                running.remove(piece)


def gather_piece(place, sender, local_sem, source, target, other):
    z, (y, x) = place.z, place.own_at
    local = pltpu.make_async_copy(source, target.at[z, y, x], local_sem)
    local.start()
    near = sender.start(source, target.at[z, y, x], place.near_z)
    yield
    local.wait()
    near.wait_recv()
    pair = pl.ds(2 * place.z_high, 2)
    far = sender.start(target.at[pair, y, x], target.at[pair, y, x], place.far_z)
    yield
    far.wait_recv()
    own = target.at[:, y, x]
    to_one = sender.start(own, own, place.one)
    to_two = sender.start(own, own, place.two)
    cores = [sender.start(own, own, place.core)]
    yield
    to_one.wait_recv()
    first = target.at[:, place.one_at[0], place.one_at[1]]
    cross = sender.start(first, first, place.two)
    cores.append(sender.start(first, first, place.core))
    yield
    to_two.wait_recv()
    second = target.at[:, place.two_at[0], place.two_at[1]]
    cores.append(sender.start(second, second, place.core))
    cross.wait_recv()
    last = target.at[:, place.cross_at[0], place.cross_at[1]]
    cores.append(sender.start(last, last, place.core))
    yield
    for copy in cores:
        copy.wait_recv()


GATHER_COPIES = 9


def gather_kernel(attention_ref, dense_ref, attention_out, dense_out, send_sems, recv_sems, local_sems):
    place = Place()
    place.greet()
    sender = Sender(send_sems, recv_sems)
    pieces = []
    for matrix in range(attention_ref.shape[0]):
        pieces.append((attention_ref.at[matrix], attention_out.at[place.mp, matrix]))
    for matrix in range(dense_ref.shape[0]):
        pieces.append((dense_ref.at[matrix], dense_out.at[place.mp, matrix]))
    run_pipelined(
        gather_piece(place, sender, local_sems.at[at], source, target, None)
        for at, (source, target) in enumerate(pieces)
    )
    sender.finish()


def gather_weights(attention_low, dense_low):
    def blocks(shard):
        return jax.ShapeDtypeStruct((2, shard.shape[0], 4, 2, 2) + shard.shape[1:], shard.dtype)

    count = attention_low.shape[0] + dense_low.shape[0]
    anywhere = pl.BlockSpec(memory_space=pl.ANY)
    attention_full, dense_full = pl.pallas_call(
        gather_kernel,
        name="gather_weights",
        out_shape=(blocks(attention_low), blocks(dense_low)),
        in_specs=[anywhere, anywhere],
        out_specs=(anywhere, anywhere),
        scratch_shapes=[
            pltpu.SemaphoreType.DMA((count * GATHER_COPIES,)),
            pltpu.SemaphoreType.DMA((count * GATHER_COPIES,)),
            pltpu.SemaphoreType.DMA((count,)),
        ],
        compiler_params=pltpu.CompilerParams(collective_id=0, has_side_effects=True),
    )(attention_low, dense_low)
    return (
        attention_full.reshape(2, attention_low.shape[0], -1, attention_low.shape[2]),
        dense_full.reshape(2, dense_low.shape[0], -1, dense_low.shape[2]),
    )


def add_blocks(count, store, *loads):
    def body(at, carry):
        total = loads[0](at).astype(jnp.float32)
        for load in loads[1:]:
            total = total + load(at).astype(jnp.float32)
        store(at, total)
        return carry

    lax.fori_loop(0, count, body, 0)


def scatter_piece(place, sender, gradient, other_gradient, held, out):
    from_core, summed, from_cross, from_one, from_two, to_one, grouped, from_far, pair, from_near, to_near = held
    to_core = sender.start(other_gradient, from_core, place.core)
    yield
    to_core.wait_recv()

    def store_sum(at, total):
        summed[at // 4, (at // 2) % 2, at % 2] = total.astype(jnp.bfloat16)

    def at_block(ref):
        return lambda at: ref[at // 4, (at // 2) % 2, at % 2]

    add_blocks(16, store_sum, at_block(gradient), at_block(from_core))
    cross = sender.start(summed.at[:, place.cross_at[0], place.cross_at[1]], from_cross, place.two)
    straight = sender.start(summed.at[:, place.two_at[0], place.two_at[1]], from_two, place.two)
    yield
    cross.wait_recv()

    def store_one(at, total):
        to_one[at] = total.astype(jnp.bfloat16)

    add_blocks(
        4, store_one, lambda at: summed[at, place.one_at[0], place.one_at[1]], lambda at: from_cross[at]
    )
    turned = sender.start(to_one, from_one, place.one)
    yield
    straight.wait_recv()
    turned.wait_recv()

    def store_group(at, total):
        grouped[at] = total.astype(jnp.bfloat16)

    add_blocks(
        4,
        store_group,
        lambda at: summed[at, place.y, place.x],
        lambda at: from_one[at],
        lambda at: from_two[at],
    )
    far = sender.start(grouped.at[pl.ds(2 - 2 * place.z_high, 2)], from_far, place.far_z)
    yield
    far.wait_recv()

    def store_pair(at, total):
        pair[at] = total

    add_blocks(2, store_pair, lambda at: grouped[2 * place.z_high + at], lambda at: from_far[at])
    to_near[...] = pair[1 - place.z_low].astype(jnp.bfloat16)
    near = sender.start(to_near, from_near, place.near_z)
    yield
    near.wait_recv()
    out[...] = pair[place.z_low] + from_near[...].astype(jnp.float32)


SCATTER_COPIES = 6


def scatter_held(rows, cols):
    def low(*lead):
        return pltpu.VMEM(lead + (rows, cols), jnp.bfloat16)

    return [
        low(4, 2, 2),
        low(4, 2, 2),
        low(4),
        low(4),
        low(4),
        low(4),
        low(4),
        low(2),
        pltpu.VMEM((2, rows, cols), jnp.float32),
        low(),
        low(),
    ]


def sum_small(place, sender, small_ref, small_out, slots):
    small_out[...] = small_ref[...]
    for at, partner in enumerate((place.core, place.near_x, place.near_y, place.near_z, place.far_z)):
        slots[2 * at] = small_out[...]
        copy = sender.start(slots.at[2 * at], slots.at[2 * at + 1], partner)
        yield
        copy.wait_recv()
        small_out[...] = slots[2 * at] + slots[2 * at + 1]


HELD = 11


def scatter_kernel(attention_ref, dense_ref, small_ref, attention_out, dense_out, small_out, *scratch):
    send_sems, recv_sems, slots = scratch[:3]
    held = scratch[3:]
    place = Place()
    place.greet()
    sender = Sender(send_sems, recv_sems)
    pieces = []
    at = 0
    for ref, out in ((dense_ref, dense_out), (attention_ref, attention_out)):
        for matrix in range(ref.shape[1]):
            pieces.append(
                scatter_piece(
                    place,
                    sender,
                    ref.at[place.mp, matrix],
                    ref.at[1 - place.mp, matrix],
                    held[at : at + HELD],
                    out.at[matrix],
                )
            )
            at += HELD
    pieces.insert(1, sum_small(place, sender, small_ref, small_out, slots))
    run_pipelined(pieces)
    sender.finish()


def scatter_gradients(attention_gradient, dense_gradient, small):
    def blocks(gradient):
        matrices, rows, cols = gradient.shape[1:]
        return gradient.reshape(2, matrices, 4, 2, 2, rows // 16, cols)

    attention_gradient, dense_gradient = blocks(attention_gradient), blocks(dense_gradient)
    count = attention_gradient.shape[1] + dense_gradient.shape[1]
    copies = count * SCATTER_COPIES + 5

    def share(gradient):
        return jax.ShapeDtypeStruct((gradient.shape[1],) + gradient.shape[5:], jnp.float32)

    scratch = [
        pltpu.SemaphoreType.DMA((copies,)),
        pltpu.SemaphoreType.DMA((copies,)),
        pltpu.VMEM((10,) + small.shape, jnp.float32),
    ]
    for gradient in (dense_gradient, attention_gradient):
        for _ in range(gradient.shape[1]):
            scratch.extend(scatter_held(*gradient.shape[5:]))
    whole = pl.BlockSpec(memory_space=pltpu.VMEM)
    return pl.pallas_call(
        scatter_kernel,
        name="scatter_gradients",
        out_shape=(
            share(attention_gradient),
            share(dense_gradient),
            jax.ShapeDtypeStruct(small.shape, jnp.float32),
        ),
        in_specs=[whole] * 3,
        out_specs=(whole,) * 3,
        scratch_shapes=scratch,
        compiler_params=pltpu.CompilerParams(
            collective_id=1, has_side_effects=True, vmem_limit_bytes=56 * 2**20
        ),
    )(attention_gradient, dense_gradient, small)


def plain_gather(attention_low, dense_low):
    def both(shard):
        return lax.all_gather(lax.all_gather(shard, "dp", axis=1, tiled=True), "mp", axis=0)

    return both(attention_low), both(dense_low)


def plain_scatter(attention_gradient, dense_gradient, small):
    def share(gradient):
        half = lax.psum_scatter(gradient.astype(jnp.float32), "mp", scatter_dimension=0)
        return lax.psum_scatter(half, "dp", scatter_dimension=1, tiled=True)

    return share(attention_gradient), share(dense_gradient), lax.psum(small, ("dp", "mp"))


def layer(row_tokens, segment_row, upstream, attention_full, dense_full, head_bias, dense_bias, small_vectors):
    groups = attention_full.shape[0]
    length = row_tokens.shape[0]
    local_cols = attention_full.shape[3]
    local_heads = local_cols // HEAD_DIM
    allowed = (segment_row[:, None] == segment_row[None, :])[None]
    saved = []
    branch = 0.0
    for group in range(groups):
        weights = attention_full[group]
        queries = (
            (jnp.dot(row_tokens, weights[0], preferred_element_type=jnp.float32) + head_bias[group, 0]) * 0.125
        ).astype(jnp.bfloat16)
        key_rows = jnp.dot(row_tokens, weights[1], preferred_element_type=jnp.float32).astype(jnp.bfloat16)
        value_rows = (
            jnp.dot(row_tokens, weights[2], preferred_element_type=jnp.float32) + head_bias[group, 1]
        ).astype(jnp.bfloat16)
        query_heads = queries.reshape(length, local_heads, HEAD_DIM)
        key_heads = key_rows.reshape(length, local_heads, HEAD_DIM)
        value_heads = value_rows.reshape(length, local_heads, HEAD_DIM)
        scores = masked_scores(query_heads, key_heads, allowed)
        row_peak = jnp.max(scores, axis=-1, keepdims=True)
        shifted_exp = jnp.exp(scores - row_peak)
        exp_total = jnp.sum(shifted_exp, axis=-1, keepdims=True)
        attend_low = (shifted_exp / exp_total).astype(jnp.bfloat16)
        log_total = row_peak + jnp.log(exp_total)
        mixed_heads = (
            jnp.einsum("hqk,khd->qhd", attend_low, value_heads, preferred_element_type=jnp.float32)
            .reshape(length, local_cols)
            .astype(jnp.bfloat16)
        )
        partial_value = lax.dot_general(mixed_heads, weights[3], last_dims, preferred_element_type=jnp.float32)
        branch = branch + partial_value.astype(jnp.bfloat16).astype(jnp.float32)
        saved.append((query_heads, key_heads, value_heads, log_total, mixed_heads))
    hidden, normed_one, inverse_one = norm_forward(
        row_tokens.astype(jnp.float32) + branch + small_vectors[0], small_vectors[2], small_vectors[3]
    )
    hidden_low = hidden.astype(jnp.bfloat16)
    down_out = 0.0
    dense_saved = []
    for group in range(groups):
        hidden_pre = (
            jnp.dot(hidden_low, dense_full[group, 0], preferred_element_type=jnp.float32) + dense_bias[group]
        )
        activated = gelu_value(hidden_pre).astype(jnp.bfloat16)
        down_partial = lax.dot_general(
            activated, dense_full[group, 1], last_dims, preferred_element_type=jnp.float32
        )
        down_out = down_out + down_partial.astype(jnp.bfloat16).astype(jnp.float32)
        dense_saved.append((hidden_pre, activated))
    final, normed_two, inverse_two = norm_forward(
        hidden + down_out + small_vectors[1], small_vectors[4], small_vectors[5]
    )
    back_two, gain_two, shift_two = norm_backward(upstream, normed_two, inverse_two, small_vectors[4])
    down_grad = back_two.astype(jnp.bfloat16)
    hidden_grad = back_two
    dense_grads, dense_bias_grads = [], []
    for group in range(groups):
        hidden_pre, activated = dense_saved[group]
        grad_down_weight = lax.dot_general(down_grad, activated, first_dims, preferred_element_type=jnp.float32)
        pre_grad = (
            jnp.dot(down_grad, dense_full[group, 1], preferred_element_type=jnp.float32) * gelu_slope(hidden_pre)
        ).astype(jnp.bfloat16)
        grad_up_weight = lax.dot_general(hidden_low, pre_grad, first_dims, preferred_element_type=jnp.float32)
        hidden_grad = hidden_grad + lax.dot_general(
            pre_grad, dense_full[group, 0], last_dims, preferred_element_type=jnp.float32
        )
        dense_grads.append(jnp.stack([grad_up_weight, grad_down_weight]))
        dense_bias_grads.append(jnp.sum(pre_grad.astype(jnp.float32), axis=0))
    back_one, gain_one, shift_one = norm_backward(hidden_grad, normed_one, inverse_one, small_vectors[2])
    small_grad = jnp.stack(
        [jnp.sum(back_one, axis=0), jnp.sum(back_two, axis=0), gain_one, shift_one, gain_two, shift_two]
    )
    branch_grad = back_one.astype(jnp.bfloat16)
    input_rows = back_one
    attention_grads, head_grads = [], []
    for group in range(groups):
        weights = attention_full[group]
        query_heads, key_heads, value_heads, log_total, mixed_heads = saved[group]
        grad_out_weight = lax.dot_general(branch_grad, mixed_heads, first_dims, preferred_element_type=jnp.float32)
        mixed_grad = (
            jnp.dot(branch_grad, weights[3], preferred_element_type=jnp.float32)
            .astype(jnp.bfloat16)
            .reshape(length, local_heads, HEAD_DIM)
        )
        attend = jnp.exp(masked_scores(query_heads, key_heads, allowed) - log_total)
        attend_low = attend.astype(jnp.bfloat16)
        prob_grad = jnp.einsum("qhd,khd->hqk", mixed_grad, value_heads, preferred_element_type=jnp.float32)
        value_grad = jnp.einsum(
            "hqk,qhd->khd", attend_low, mixed_grad, preferred_element_type=jnp.float32
        ).astype(jnp.bfloat16)
        inner_total = jnp.sum(attend * prob_grad, axis=-1, keepdims=True)
        score_grad = (attend * (prob_grad - inner_total)).astype(jnp.bfloat16)
        query_grad = (
            jnp.einsum("hqk,khd->qhd", score_grad, key_heads, preferred_element_type=jnp.float32).astype(jnp.bfloat16)
            * 0.125
        )
        key_grad = jnp.einsum(
            "hqk,qhd->khd", score_grad, query_heads, preferred_element_type=jnp.float32
        ).astype(jnp.bfloat16)
        stacked = [each.reshape(length, local_cols) for each in (query_grad, key_grad, value_grad)]
        grads = [
            lax.dot_general(row_tokens, each, first_dims, preferred_element_type=jnp.float32) for each in stacked
        ]
        for each, weight in zip(stacked, weights[:3]):
            input_rows = input_rows + lax.dot_general(each, weight, last_dims, preferred_element_type=jnp.float32)
        attention_grads.append(jnp.stack(grads + [grad_out_weight]))
        head_grads.append(
            jnp.stack(
                [jnp.sum(stacked[0].astype(jnp.float32), axis=0), jnp.sum(stacked[2].astype(jnp.float32), axis=0)]
            )
        )
    return (
        final.astype(jnp.bfloat16),
        input_rows,
        jnp.stack(attention_grads).astype(jnp.bfloat16),
        jnp.stack(dense_grads).astype(jnp.bfloat16),
        jnp.stack(head_grads),
        jnp.stack(dense_bias_grads),
        small_grad,
    )


def make_local(mesh):
    n_dp, n_mp = mesh.shape["dp"], mesh.shape["mp"]
    square = n_dp == 16 and n_mp == 2

    def local(
        tokens,
        segment_ids,
        cotangent,
        attention_master,
        attention_first,
        attention_second,
        dense_master,
        dense_first,
        dense_second,
        head_bias,
        head_bias_first,
        head_bias_second,
        dense_bias,
        dense_bias_first,
        dense_bias_second,
        small_vectors,
        small_first,
        small_second,
    ):
        gather, scatter = (gather_weights, scatter_gradients) if square else (plain_gather, plain_scatter)
        attention_full, dense_full = gather(
            attention_master.astype(jnp.bfloat16), dense_master.astype(jnp.bfloat16)
        )
        head_full = lax.all_gather(head_bias, "mp", axis=0)
        dense_bias_full = lax.all_gather(dense_bias, "mp", axis=0)
        mine = lax.axis_index("mp")
        row_tokens = lax.dynamic_index_in_dim(tokens, mine, 0, keepdims=False)
        segment_row = lax.dynamic_index_in_dim(segment_ids, mine, 0, keepdims=False)
        upstream = lax.dynamic_index_in_dim(cotangent, mine, 0, keepdims=False).astype(jnp.float32)
        final, input_rows, attention_grad, dense_grad, head_grad, dense_bias_grad, small_grad = layer(
            row_tokens, segment_row, upstream, attention_full, dense_full, head_full, dense_bias_full, small_vectors
        )
        parts = (head_grad, dense_bias_grad, small_grad)
        packed = jnp.concatenate([part.reshape(-1) for part in parts]).reshape(-1, 128)
        attention_share, dense_share, packed = scatter(attention_grad, dense_grad, packed)
        sums, start = [], 0
        flat = packed.reshape(-1)
        for part in parts:
            sums.append(flat[start : start + part.size].reshape(part.shape))
            start += part.size
        head_sum = lax.dynamic_index_in_dim(sums[0], mine, 0, keepdims=False)
        dense_bias_sum = lax.dynamic_index_in_dim(sums[1], mine, 0, keepdims=False)
        small_sum = sums[2]

        swap = [(at, (at + 1) % n_mp) for at in range(n_mp)]

        def both(rows):
            other = lax.ppermute(rows, "mp", swap)
            first = mine == 0
            return jnp.stack([jnp.where(first, rows, other), jnp.where(first, other, rows)])

        out_rows, grad_rows = both(final), both(input_rows)
        attention_new = adamw(attention_master, attention_share, attention_first, attention_second, 0.03, 0.01)
        dense_new = adamw(dense_master, dense_share, dense_first, dense_second, 0.03, 0.01)
        head_new = adamw(head_bias, head_sum, head_bias_first, head_bias_second, 0.2, 0.0)
        dbias_new = adamw(dense_bias, dense_bias_sum, dense_bias_first, dense_bias_second, 0.2, 0.0)
        small_new = adamw(small_vectors, small_sum, small_first, small_second, 0.2, 0.0)
        return (
            out_rows,
            grad_rows,
            *attention_new,
            attention_new[0].astype(jnp.bfloat16),
            *dense_new,
            dense_new[0].astype(jnp.bfloat16),
            *head_new,
            *dbias_new,
            *small_new,
        )

    return local


def solution(mesh):
    rows, matrix, halves, units = P("dp", None, None), P(None, "dp", "mp"), P(None, "mp"), P("mp")
    return jax.shard_map(
        make_local(mesh),
        mesh=mesh,
        in_specs=(rows, P("dp", None), rows) + (matrix,) * 6 + (halves,) * 3 + (units,) * 3 + (P(),) * 3,
        out_specs=(rows,) * 2 + (matrix,) * 8 + (halves,) * 3 + (units,) * 3 + (P(),) * 3,
        check_vma=False,
    )
```

```python
import functools

import jax
import jax.numpy as jnp
from jax import lax
from jax.experimental import pallas as pl
from jax.experimental.pallas import tpu as pltpu
from jax.sharding import PartitionSpec as P

HEAD_DIM = 64
PAIR = 2 * HEAD_DIM
STEP = 5
MESH_ID = pl.DeviceIdType.MESH

last_dims = (((1,), (1,)), ((), ()))


def adamw(parameter, gradient, moment_one, moment_two, learn_rate, weight_decay):
    first_new = 0.5 * moment_one + 0.5 * gradient
    second_new = 0.5 * moment_two + 0.5 * gradient * gradient
    correction = 1.0 - jnp.power(jnp.float32(0.5), jnp.float32(STEP))
    update = first_new / correction / (jnp.sqrt(second_new / correction) + 1e-08)
    return (
        parameter - learn_rate * update - learn_rate * weight_decay * parameter,
        first_new,
        second_new,
    )


class Place:
    def __init__(self):
        self.dp = lax.axis_index("dp")
        self.mp = lax.axis_index("mp")
        self.x = self.dp % 2
        self.y = (self.dp // 2) % 2
        self.z = self.dp // 4
        self.z_low = self.z % 2
        self.z_high = self.z // 2
        on_x = self.dp + 1 - 2 * self.x
        on_y = self.dp + 2 - 4 * self.y
        self.near_x = (on_x, self.mp)
        self.near_y = (on_y, self.mp)
        self.near_z = (self.dp + 4 - 8 * self.z_low, self.mp)
        self.far_z = (self.dp + 8 - 16 * self.z_high, self.mp)
        self.core = (self.dp, 1 - self.mp)
        self.one = (on_x + (on_y - on_x) * self.mp, self.mp)
        self.two = (on_y + (on_x - on_y) * self.mp, self.mp)
        self.one_at = (self.y + (1 - 2 * self.y) * self.mp, self.x + (1 - 2 * self.x) * (1 - self.mp))
        self.two_at = (self.y + (1 - 2 * self.y) * (1 - self.mp), self.x + (1 - 2 * self.x) * self.mp)
        self.own_at = (self.y, self.x)
        self.cross_at = (1 - self.y, 1 - self.x)

    def greet(self):
        barrier = pltpu.get_barrier_semaphore()
        partners = (self.near_x, self.near_y, self.near_z, self.far_z, self.core)
        for partner in partners:
            pl.semaphore_signal(barrier, inc=1, device_id=partner, device_id_type=MESH_ID)
        pl.semaphore_wait(barrier, len(partners))


class Sender:
    def __init__(self, send_sems, recv_sems):
        self.send_sems, self.recv_sems, self.used, self.open = send_sems, recv_sems, 0, []

    def start(self, source, target, device):
        copy = pltpu.make_async_remote_copy(
            src_ref=source,
            dst_ref=target,
            send_sem=self.send_sems.at[self.used],
            recv_sem=self.recv_sems.at[self.used],
            device_id=device,
            device_id_type=MESH_ID,
        )
        self.used += 1
        copy.start()
        self.open.append(copy)
        return copy

    def finish(self):
        for copy in self.open:
            copy.wait_send()


def run_pipelined(pieces):
    waiting, running = list(pieces), []
    while waiting or running:
        if waiting:
            running.append(waiting.pop(0))
        for piece in list(running):
            try:
                next(piece)
            except StopIteration:
                running.remove(piece)


def gather_piece(place, sender, local_sem, source, target, other):
    z, (y, x) = place.z, place.own_at
    local = pltpu.make_async_copy(source, target.at[z, y, x], local_sem)
    local.start()
    near = sender.start(source, target.at[z, y, x], place.near_z)
    yield
    local.wait()
    near.wait_recv()
    pair = pl.ds(2 * place.z_high, 2)
    far = sender.start(target.at[pair, y, x], target.at[pair, y, x], place.far_z)
    yield
    far.wait_recv()
    own = target.at[:, y, x]
    to_one = sender.start(own, own, place.one)
    to_two = sender.start(own, own, place.two)
    cores = [sender.start(own, own, place.core)]
    yield
    to_one.wait_recv()
    first = target.at[:, place.one_at[0], place.one_at[1]]
    cross = sender.start(first, first, place.two)
    cores.append(sender.start(first, first, place.core))
    yield
    to_two.wait_recv()
    second = target.at[:, place.two_at[0], place.two_at[1]]
    cores.append(sender.start(second, second, place.core))
    cross.wait_recv()
    last = target.at[:, place.cross_at[0], place.cross_at[1]]
    cores.append(sender.start(last, last, place.core))
    yield
    for copy in cores:
        copy.wait_recv()


GATHER_COPIES = 9


def gather_kernel(attention_ref, dense_ref, attention_out, dense_out, send_sems, recv_sems, local_sems):
    place = Place()
    place.greet()
    sender = Sender(send_sems, recv_sems)
    pieces = []
    for matrix in range(attention_ref.shape[0]):
        pieces.append((attention_ref.at[matrix], attention_out.at[place.mp, matrix]))
    for matrix in range(dense_ref.shape[0]):
        pieces.append((dense_ref.at[matrix], dense_out.at[place.mp, matrix]))
    run_pipelined(
        gather_piece(place, sender, local_sems.at[at], source, target, None)
        for at, (source, target) in enumerate(pieces)
    )
    sender.finish()


def gather_weights(attention_low, dense_low):
    def blocks(shard):
        return jax.ShapeDtypeStruct((2, shard.shape[0], 4, 2, 2) + shard.shape[1:], shard.dtype)

    count = attention_low.shape[0] + dense_low.shape[0]
    anywhere = pl.BlockSpec(memory_space=pl.ANY)
    attention_full, dense_full = pl.pallas_call(
        gather_kernel,
        name="gather_weights",
        out_shape=(blocks(attention_low), blocks(dense_low)),
        in_specs=[anywhere, anywhere],
        out_specs=(anywhere, anywhere),
        scratch_shapes=[
            pltpu.SemaphoreType.DMA((count * GATHER_COPIES,)),
            pltpu.SemaphoreType.DMA((count * GATHER_COPIES,)),
            pltpu.SemaphoreType.DMA((count,)),
        ],
        compiler_params=pltpu.CompilerParams(collective_id=0, has_side_effects=True),
    )(attention_low, dense_low)
    return (
        attention_full.reshape(2, attention_low.shape[0], -1, attention_low.shape[2]),
        dense_full.reshape(2, dense_low.shape[0], -1, dense_low.shape[2]),
    )


def add_blocks(count, store, *loads):
    def body(at, carry):
        total = loads[0](at).astype(jnp.float32)
        for load in loads[1:]:
            total = total + load(at).astype(jnp.float32)
        store(at, total)
        return carry

    lax.fori_loop(0, count, body, 0)


def scatter_piece(place, sender, gradient, other_gradient, held, out):
    from_core, summed, from_cross, from_one, from_two, to_one, grouped, from_far, pair, from_near, to_near = held
    to_core = sender.start(other_gradient, from_core, place.core)
    yield
    to_core.wait_recv()

    def store_sum(at, total):
        summed[at // 4, (at // 2) % 2, at % 2] = total.astype(jnp.bfloat16)

    def at_block(ref):
        return lambda at: ref[at // 4, (at // 2) % 2, at % 2]

    add_blocks(16, store_sum, at_block(gradient), at_block(from_core))
    cross = sender.start(summed.at[:, place.cross_at[0], place.cross_at[1]], from_cross, place.two)
    straight = sender.start(summed.at[:, place.two_at[0], place.two_at[1]], from_two, place.two)
    yield
    cross.wait_recv()

    def store_one(at, total):
        to_one[at] = total.astype(jnp.bfloat16)

    add_blocks(
        4, store_one, lambda at: summed[at, place.one_at[0], place.one_at[1]], lambda at: from_cross[at]
    )
    turned = sender.start(to_one, from_one, place.one)
    yield
    straight.wait_recv()
    turned.wait_recv()

    def store_group(at, total):
        grouped[at] = total.astype(jnp.bfloat16)

    add_blocks(
        4,
        store_group,
        lambda at: summed[at, place.y, place.x],
        lambda at: from_one[at],
        lambda at: from_two[at],
    )
    far = sender.start(grouped.at[pl.ds(2 - 2 * place.z_high, 2)], from_far, place.far_z)
    yield
    far.wait_recv()

    def store_pair(at, total):
        pair[at] = total

    add_blocks(2, store_pair, lambda at: grouped[2 * place.z_high + at], lambda at: from_far[at])
    to_near[...] = pair[1 - place.z_low].astype(jnp.bfloat16)
    near = sender.start(to_near, from_near, place.near_z)
    yield
    near.wait_recv()
    out[...] = pair[place.z_low] + from_near[...].astype(jnp.float32)


SCATTER_COPIES = 6


def scatter_held(rows, cols):
    def low(*lead):
        return pltpu.VMEM(lead + (rows, cols), jnp.bfloat16)

    return [
        low(4, 2, 2),
        low(4, 2, 2),
        low(4),
        low(4),
        low(4),
        low(4),
        low(4),
        low(2),
        pltpu.VMEM((2, rows, cols), jnp.float32),
        low(),
        low(),
    ]


def sum_small(place, sender, small_ref, small_out, slots):
    small_out[...] = small_ref[...]
    for at, partner in enumerate((place.core, place.near_x, place.near_y, place.near_z, place.far_z)):
        slots[2 * at] = small_out[...]
        copy = sender.start(slots.at[2 * at], slots.at[2 * at + 1], partner)
        yield
        copy.wait_recv()
        small_out[...] = slots[2 * at] + slots[2 * at + 1]


HELD = 11


def scatter_kernel(attention_ref, dense_ref, small_ref, attention_out, dense_out, small_out, *scratch):
    send_sems, recv_sems, slots = scratch[:3]
    held = scratch[3:]
    place = Place()
    place.greet()
    sender = Sender(send_sems, recv_sems)
    pieces = []
    at = 0
    for ref, out in ((dense_ref, dense_out), (attention_ref, attention_out)):
        for matrix in range(ref.shape[1]):
            pieces.append(
                scatter_piece(
                    place,
                    sender,
                    ref.at[place.mp, matrix],
                    ref.at[1 - place.mp, matrix],
                    held[at : at + HELD],
                    out.at[matrix],
                )
            )
            at += HELD
    pieces.insert(1, sum_small(place, sender, small_ref, small_out, slots))
    run_pipelined(pieces)
    sender.finish()


def scatter_gradients(attention_gradient, dense_gradient, small):
    def blocks(gradient):
        matrices, rows, cols = gradient.shape[1:]
        return gradient.reshape(2, matrices, 4, 2, 2, rows // 16, cols)

    attention_gradient, dense_gradient = blocks(attention_gradient), blocks(dense_gradient)
    count = attention_gradient.shape[1] + dense_gradient.shape[1]
    copies = count * SCATTER_COPIES + 5

    def share(gradient):
        return jax.ShapeDtypeStruct((gradient.shape[1],) + gradient.shape[5:], jnp.float32)

    scratch = [
        pltpu.SemaphoreType.DMA((copies,)),
        pltpu.SemaphoreType.DMA((copies,)),
        pltpu.VMEM((10,) + small.shape, jnp.float32),
    ]
    for gradient in (dense_gradient, attention_gradient):
        for _ in range(gradient.shape[1]):
            scratch.extend(scatter_held(*gradient.shape[5:]))
    whole = pl.BlockSpec(memory_space=pltpu.VMEM)
    return pl.pallas_call(
        scatter_kernel,
        name="scatter_gradients",
        out_shape=(
            share(attention_gradient),
            share(dense_gradient),
            jax.ShapeDtypeStruct(small.shape, jnp.float32),
        ),
        in_specs=[whole] * 3,
        out_specs=(whole,) * 3,
        scratch_shapes=scratch,
        compiler_params=pltpu.CompilerParams(
            collective_id=1, has_side_effects=True, vmem_limit_bytes=56 * 2**20
        ),
    )(attention_gradient, dense_gradient, small)


def plain_gather(attention_low, dense_low):
    def both(shard):
        return lax.all_gather(lax.all_gather(shard, "dp", axis=1, tiled=True), "mp", axis=0)

    return both(attention_low), both(dense_low)


def plain_scatter(attention_gradient, dense_gradient, small):
    def share(gradient):
        half = lax.psum_scatter(gradient.astype(jnp.float32), "mp", scatter_dimension=0)
        return lax.psum_scatter(half, "dp", scatter_dimension=1, tiled=True)

    return share(attention_gradient), share(dense_gradient), lax.psum(small, ("dp", "mp"))


def dot(left, right):
    return jnp.dot(left, right, preferred_element_type=jnp.float32)


def dot_last(left, right):
    return lax.dot_general(left, right, last_dims, preferred_element_type=jnp.float32)


def rows_at(at, count):
    return pl.ds(pl.multiple_of(at * count, count), count)


def fold(values):
    return jnp.sum(values.reshape(values.shape[0] // 8, 8, values.shape[1]), axis=0)


class Layer:
    NORM_ROWS = 64
    SOFT_ROWS = 128

    def __init__(self, **refs):
        self.__dict__.update(refs)
        self.length, self.width = self.tokens.shape
        self.groups = self.dense_weights.shape[0]
        self.cols = self.attention_weights.shape[-1]
        self.units = self.dense_weights.shape[-1]
        self.pairs = self.cols // PAIR

    def weight(self, ref, group, matrix, cols=None):
        value = ref[group, matrix] if cols is None else ref[group, matrix, ..., cols]
        return value.reshape(self.width, value.shape[-1])

    def put_gradient(self, ref, group, matrix, cols, value):
        shape = ref.shape[2:-1] + (value.shape[-1],)
        ref[group, matrix, ..., cols] = value.astype(jnp.bfloat16).reshape(shape)


    def project(self, group, matrix):
        out = (self.queries, self.keys, self.values)[matrix]
        value = dot(self.tokens[...], self.weight(self.attention_weights, group, matrix))
        if matrix == 0:
            value = (value + self.head_bias[group, 0:1]) * 0.125
        elif matrix == 2:
            value = value + self.head_bias[group, 1:2]
        value = value.astype(jnp.bfloat16)
        for pair in range(self.pairs):
            out[group * self.pairs + pair] = value[:, pair * PAIR : (pair + 1) * PAIR]

    def attend(self, group, pair):
        at = group * self.pairs + pair
        cols = slice(pair * PAIR, (pair + 1) * PAIR)
        keys, values = self.keys[at], self.values[at]
        first = lax.broadcasted_iota(jnp.int32, (self.SOFT_ROWS, PAIR), 1) < HEAD_DIM
        segment_row = self.segment_row[...]

        def chunk(block, carry):
            rows = rows_at(block, self.SOFT_ROWS)
            queries = self.queries[at, rows]
            allowed = self.segment_column[rows] == segment_row
            mixed, totals = [], []
            for side in range(2):
                mine = jnp.where(first if side == 0 else ~first, queries, jnp.bfloat16(0))
                scores = jnp.where(allowed, dot_last(mine, keys), -1000000000.0)
                peak = jnp.max(scores, axis=-1, keepdims=True)
                shifted = jnp.exp(scores - peak)
                total = jnp.sum(shifted, axis=-1, keepdims=True)
                attend_low = (shifted * (1.0 / total)).astype(jnp.bfloat16)
                mixed.append(dot(attend_low, values))
                totals.append(peak + jnp.log(total))
            self.mixed[group, rows, cols] = jnp.where(first, mixed[0], mixed[1]).astype(jnp.bfloat16)
            self.log_totals[at, rows] = jnp.where(first, totals[0], totals[1])
            return carry

        lax.fori_loop(0, self.length // self.SOFT_ROWS, chunk, 0)

    def add_branch(self, group):
        step = 256
        for start in range(0, self.width, step):
            cols = slice(start, start + step)
            weight = self.weight(self.attention_weights, group, 3)[cols]
            part = dot_last(self.mixed[group], weight).astype(jnp.bfloat16).astype(jnp.float32)
            self.wide[:, cols] = part if group == 0 else self.wide[:, cols] + part

    def norm_one(self):
        out_bias, gain, shift = self.small[0:1], self.small[2:3], self.small[3:4]

        def chunk(block, carry):
            rows = rows_at(block, self.NORM_ROWS)
            values = self.tokens[rows].astype(jnp.float32) + self.wide[rows] + out_bias
            center = values - jnp.mean(values, axis=-1, keepdims=True)
            inverse = lax.rsqrt(jnp.mean(center * center, axis=-1, keepdims=True) + 1e-06)
            normed = center * inverse
            self.normed[rows] = normed
            self.inverse[rows] = inverse
            self.hidden_low[rows] = (normed * gain + shift).astype(jnp.bfloat16)
            return carry

        lax.fori_loop(0, self.length // self.NORM_ROWS, chunk, 0)

    def expand(self, group, start, count=256):
        cols = slice(start, start + count)
        pre = dot(self.hidden_low[...], self.weight(self.dense_weights, group, 0, cols))
        pre = pre + self.dense_bias[group, :, cols]
        half = 0.5 * (1.0 + lax.erf(pre * 0.7071067811865476))
        self.activated[group, :, cols] = (pre * half).astype(jnp.bfloat16)
        self.slope[group, :, cols] = half + pre * jnp.exp(-0.5 * pre * pre) * 0.3989422804014327

    def add_down(self, group):
        step = 256
        for start in range(0, self.width, step):
            weight = self.dense_weights[group, 1].reshape(self.width, self.units)[start : start + step]
            part = dot_last(self.activated[group], weight).astype(jnp.bfloat16).astype(jnp.float32)
            cols = slice(start, start + step)
            self.wide[:, cols] = part if group == 0 else self.wide[:, cols] + part

    def norm_two(self):
        down_bias, gain, shift = self.small[1:2], self.small[4:5], self.small[5:6]
        gain_one, shift_one = self.small[2:3], self.small[3:4]

        def chunk(block, sums):
            rows = rows_at(block, self.NORM_ROWS)
            hidden = self.normed[rows] * gain_one + shift_one
            values = hidden + self.wide[rows] + down_bias
            center = values - jnp.mean(values, axis=-1, keepdims=True)
            inverse = lax.rsqrt(jnp.mean(center * center, axis=-1, keepdims=True) + 1e-06)
            normed = center * inverse
            self.final[rows] = (normed * gain + shift).astype(jnp.bfloat16)
            upstream = self.cotangent[rows].astype(jnp.float32)
            scaled = upstream * gain
            back = inverse * (
                scaled
                - jnp.mean(scaled, axis=-1, keepdims=True)
                - normed * jnp.mean(scaled * normed, axis=-1, keepdims=True)
            )
            self.wide[rows] = back
            self.back_low[rows] = back.astype(jnp.bfloat16)
            return (sums[0] + fold(back), sums[1] + fold(upstream * normed), sums[2] + fold(upstream))

        zero = jnp.zeros((8, self.width), jnp.float32)
        sums = lax.fori_loop(0, self.length // self.NORM_ROWS, chunk, (zero, zero, zero))
        for row, total in zip((1, 4, 5), sums):
            self.small_grad[row : row + 1] = jnp.sum(total, axis=0, keepdims=True)


    def turn(self, source, target):
        step = 128
        for start in range(0, self.length, step):
            target[:, start : start + step] = source[start : start + step].T

    def down_gradient(self, group, start, count=256):
        cols = slice(start, start + count)
        self.put_gradient(self.dense_grad, group, 1, cols, dot(self.turned[...], self.activated[group, :, cols]))

    def pre_gradient(self, group, start, count=256):
        cols = slice(start, start + count)
        grad = dot(self.back_low[...], self.weight(self.dense_weights, group, 1, cols)) * self.slope[group, :, cols]
        grad = grad.astype(jnp.bfloat16)
        self.activated[group, :, cols] = grad
        self.dense_bias_grad[group, :, cols] = jnp.sum(fold(grad.astype(jnp.float32)), axis=0, keepdims=True)

    def up_gradient(self, group, start, count=256):
        cols = slice(start, start + count)
        self.put_gradient(self.dense_grad, group, 0, cols, dot(self.turned[...], self.activated[group, :, cols]))

    def add_hidden_gradient(self):
        step = 256
        for start in range(0, self.width, step):
            cols = slice(start, start + step)
            total = self.wide[:, cols]
            for group in range(self.groups):
                weight = self.dense_weights[group, 0].reshape(self.width, self.units)[cols]
                total = total + dot_last(self.activated[group], weight)
            self.wide[:, cols] = total

    def norm_one_back(self):
        gain = self.small[2:3]

        def chunk(block, sums):
            rows = rows_at(block, self.NORM_ROWS)
            upstream, normed = self.wide[rows], self.normed[rows]
            scaled = upstream * gain
            back = self.inverse[rows] * (
                scaled
                - jnp.mean(scaled, axis=-1, keepdims=True)
                - normed * jnp.mean(scaled * normed, axis=-1, keepdims=True)
            )
            self.wide[rows] = back
            self.back_low[rows] = back.astype(jnp.bfloat16)
            return (sums[0] + fold(back), sums[1] + fold(upstream * normed), sums[2] + fold(upstream))

        zero = jnp.zeros((8, self.width), jnp.float32)
        sums = lax.fori_loop(0, self.length // self.NORM_ROWS, chunk, (zero, zero, zero))
        for row, total in zip((0, 2, 3), sums):
            self.small_grad[row : row + 1] = jnp.sum(total, axis=0, keepdims=True)

    def out_gradient(self, group):
        self.put_gradient(self.attention_grad, group, 3, slice(0, self.cols), dot(self.turned[...], self.mixed[group]))

    def mix_gradient(self, group):
        grad = dot(self.back_low[...], self.weight(self.attention_weights, group, 3)).astype(jnp.bfloat16)
        for pair in range(self.pairs):
            self.mixed_grad[group * self.pairs + pair] = grad[:, pair * PAIR : (pair + 1) * PAIR]

    def attend_back(self, group, pair):
        at = group * self.pairs + pair
        cols = slice(pair * PAIR, (pair + 1) * PAIR)
        keys, values = self.keys[at], self.values[at]
        first = lax.broadcasted_iota(jnp.int32, (self.SOFT_ROWS, PAIR), 1) < HEAD_DIM
        segment_row = self.segment_row[...]

        def chunk(block, carry):
            rows = rows_at(block, self.SOFT_ROWS)
            queries, mixed_grad = self.queries[at, rows], self.mixed_grad[at, rows]
            allowed = self.segment_column[rows] == segment_row
            query_grads = []
            for side in range(2):
                here = first if side == 0 else ~first
                scores = dot_last(jnp.where(here, queries, jnp.bfloat16(0)), keys)
                prob_grad = dot_last(jnp.where(here, mixed_grad, jnp.bfloat16(0)), values)
                total = self.log_totals[at, rows, side * HEAD_DIM : side * HEAD_DIM + 1]
                attend = jnp.exp(jnp.where(allowed, scores, -1000000000.0) - total)
                inner = jnp.sum(attend * prob_grad, axis=-1, keepdims=True)
                score_grad = (attend * (prob_grad - inner)).astype(jnp.bfloat16)
                self.attend_low[side, rows] = attend.astype(jnp.bfloat16)
                self.score_grad[side, rows] = score_grad
                query_grads.append(dot(score_grad, keys))
            grad = jnp.where(first, query_grads[0], query_grads[1]).astype(jnp.bfloat16)
            self.query_grad[group, rows, cols] = grad * jnp.bfloat16(0.125)
            return carry

        lax.fori_loop(0, self.length // self.SOFT_ROWS, chunk, 0)
        mixed_turned, query_turned = self.mixed_grad[at].T, self.queries[at].T
        value_grads, key_grads = [], []
        for side in range(2):
            own = slice(side * HEAD_DIM, (side + 1) * HEAD_DIM)
            value_grads.append(dot(mixed_turned[own], self.attend_low[side]))
            key_grads.append(dot(query_turned[own], self.score_grad[side]))
        self.value_grad[group, :, cols] = jnp.concatenate(value_grads, axis=0).T.astype(jnp.bfloat16)
        self.key_grad[group, :, cols] = jnp.concatenate(key_grads, axis=0).T.astype(jnp.bfloat16)

    def project_gradient(self, group, matrix):
        grad = (self.query_grad, self.key_grad, self.value_grad)[matrix][group]
        self.put_gradient(self.attention_grad, group, matrix, slice(0, self.cols), dot(self.turned[...], grad))
        if matrix != 1:
            row = 0 if matrix == 0 else 1
            total = jnp.sum(fold(grad.astype(jnp.float32)), axis=0, keepdims=True)
            self.head_bias_grad[group, row : row + 1] = total

    def input_gradient(self):
        step = 256
        for start in range(0, self.width, step):
            cols = slice(start, start + step)
            total = self.wide[:, cols]
            for group in range(self.groups):
                for matrix, ref in enumerate((self.query_grad, self.key_grad, self.value_grad)):
                    weight = self.weight(self.attention_weights, group, matrix)[cols]
                    total = total + dot_last(ref[group], weight)
            self.wide[:, cols] = total


    def forward(self, tick):
        for group in range(self.groups):
            for matrix in range(3):
                self.project(group, matrix)
        for group in range(self.groups):
            for pair in range(self.pairs):
                self.attend(group, pair)
                tick()
            self.add_branch(group)
        self.norm_one()
        for group in range(self.groups):
            for start in range(0, self.units, 256):
                self.expand(group, start)
                tick()
            self.add_down(group)
            tick()
        self.norm_two()

    def backward(self, tick):
        self.turn(self.back_low, self.turned)
        for group in range(self.groups):
            for start in range(0, self.units, 256):
                self.down_gradient(group, start)
                self.pre_gradient(group, start)
                tick()
        self.turn(self.hidden_low, self.turned)
        for group in range(self.groups):
            for start in range(0, self.units, 256):
                self.up_gradient(group, start)
                tick()
        self.add_hidden_gradient()
        tick()
        self.norm_one_back()
        self.turn(self.back_low, self.turned)
        for group in range(self.groups):
            self.out_gradient(group)
            self.mix_gradient(group)
            tick()
        for group in range(self.groups):
            for pair in range(self.pairs):
                self.attend_back(group, pair)
                tick()
        self.turn(self.tokens, self.turned)
        for group in range(self.groups):
            for matrix in range(3):
                self.project_gradient(group, matrix)
                tick()
        self.input_gradient()


def layer_scratch(length, width, groups, cols, units):
    low, wide = jnp.bfloat16, jnp.float32
    pairs = groups * cols // PAIR
    return {
        "queries": pltpu.VMEM((pairs, length, PAIR), low),
        "keys": pltpu.VMEM((pairs, length, PAIR), low),
        "values": pltpu.VMEM((pairs, length, PAIR), low),
        "mixed": pltpu.VMEM((groups, length, cols), low),
        "log_totals": pltpu.VMEM((pairs, length, PAIR), wide),
        "normed": pltpu.VMEM((length, width), wide),
        "inverse": pltpu.VMEM((length, 1), wide),
        "hidden_low": pltpu.VMEM((length, width), low),
        "activated": pltpu.VMEM((groups, length, units), low),
        "slope": pltpu.VMEM((groups, length, units), wide),
        "back_low": pltpu.VMEM((length, width), low),
        "turned": pltpu.VMEM((width, length), low),
        "mixed_grad": pltpu.VMEM((pairs, length, PAIR), low),
        "attend_low": pltpu.VMEM((2, length, length), low),
        "score_grad": pltpu.VMEM((2, length, length), low),
        "query_grad": pltpu.VMEM((groups, length, cols), low),
        "key_grad": pltpu.VMEM((groups, length, cols), low),
        "value_grad": pltpu.VMEM((groups, length, cols), low),
    }


LAYER_INPUTS = (
    "tokens",
    "segment_column",
    "segment_row",
    "cotangent",
    "attention_weights",
    "dense_weights",
    "head_bias",
    "dense_bias",
    "small",
)
LAYER_OUTPUTS = (
    "final",
    "wide",
    "attention_grad",
    "dense_grad",
    "head_bias_grad",
    "dense_bias_grad",
    "small_grad",
)


def layer_kernel(names, *refs):
    step = Layer(**dict(zip(names, refs)))
    step.forward(lambda: None)
    step.backward(lambda: None)


def layer(row_tokens, segment_row, upstream, attention_full, dense_full, head_bias, dense_bias, small_vectors):
    length, width = row_tokens.shape
    groups, _, _, cols = attention_full.shape
    units = dense_full.shape[-1]
    scratch = layer_scratch(length, width, groups, cols, units)
    whole = pl.BlockSpec(memory_space=pltpu.VMEM)
    wide = jnp.float32
    inputs = (
        row_tokens,
        segment_row[:, None],
        segment_row[None, :],
        upstream,
        attention_full,
        dense_full,
        head_bias,
        dense_bias[:, None, :],
        small_vectors,
    )
    results = pl.pallas_call(
        functools.partial(layer_kernel, LAYER_INPUTS + LAYER_OUTPUTS + tuple(scratch)),
        name="layer",
        out_shape=(
            jax.ShapeDtypeStruct((length, width), jnp.bfloat16),
            jax.ShapeDtypeStruct((length, width), wide),
            jax.ShapeDtypeStruct(attention_full.shape, jnp.bfloat16),
            jax.ShapeDtypeStruct(dense_full.shape, jnp.bfloat16),
            jax.ShapeDtypeStruct(head_bias.shape, wide),
            jax.ShapeDtypeStruct((groups, 1, units), wide),
            jax.ShapeDtypeStruct(small_vectors.shape, wide),
        ),
        in_specs=[whole] * len(inputs),
        out_specs=(whole,) * len(LAYER_OUTPUTS),
        scratch_shapes=list(scratch.values()),
        compiler_params=pltpu.CompilerParams(vmem_limit_bytes=62 * 2**20),
    )(*inputs)
    return results[:5] + (results[5].reshape(groups, units), results[6])


def make_local(mesh):
    n_dp, n_mp = mesh.shape["dp"], mesh.shape["mp"]
    square = n_dp == 16 and n_mp == 2

    def local(
        tokens,
        segment_ids,
        cotangent,
        attention_master,
        attention_first,
        attention_second,
        dense_master,
        dense_first,
        dense_second,
        head_bias,
        head_bias_first,
        head_bias_second,
        dense_bias,
        dense_bias_first,
        dense_bias_second,
        small_vectors,
        small_first,
        small_second,
    ):
        gather, scatter = (gather_weights, scatter_gradients) if square else (plain_gather, plain_scatter)
        attention_full, dense_full = gather(
            attention_master.astype(jnp.bfloat16), dense_master.astype(jnp.bfloat16)
        )
        head_full = lax.all_gather(head_bias, "mp", axis=0)
        dense_bias_full = lax.all_gather(dense_bias, "mp", axis=0)
        mine = lax.axis_index("mp")
        row_tokens = lax.dynamic_index_in_dim(tokens, mine, 0, keepdims=False)
        segment_row = lax.dynamic_index_in_dim(segment_ids, mine, 0, keepdims=False)
        upstream = lax.dynamic_index_in_dim(cotangent, mine, 0, keepdims=False)
        final, input_rows, attention_grad, dense_grad, head_grad, dense_bias_grad, small_grad = layer(
            row_tokens, segment_row, upstream, attention_full, dense_full, head_full, dense_bias_full, small_vectors
        )
        parts = (head_grad, dense_bias_grad, small_grad)
        packed = jnp.concatenate([part.reshape(-1) for part in parts]).reshape(-1, 128)
        attention_share, dense_share, packed = scatter(attention_grad, dense_grad, packed)
        sums, start = [], 0
        flat = packed.reshape(-1)
        for part in parts:
            sums.append(flat[start : start + part.size].reshape(part.shape))
            start += part.size
        head_sum = lax.dynamic_index_in_dim(sums[0], mine, 0, keepdims=False)
        dense_bias_sum = lax.dynamic_index_in_dim(sums[1], mine, 0, keepdims=False)
        small_sum = sums[2]

        swap = [(at, (at + 1) % n_mp) for at in range(n_mp)]

        def both(rows):
            other = lax.ppermute(rows, "mp", swap)
            first = mine == 0
            return jnp.stack([jnp.where(first, rows, other), jnp.where(first, other, rows)])

        out_rows, grad_rows = both(final), both(input_rows)
        attention_new = adamw(attention_master, attention_share, attention_first, attention_second, 0.03, 0.01)
        dense_new = adamw(dense_master, dense_share, dense_first, dense_second, 0.03, 0.01)
        head_new = adamw(head_bias, head_sum, head_bias_first, head_bias_second, 0.2, 0.0)
        dbias_new = adamw(dense_bias, dense_bias_sum, dense_bias_first, dense_bias_second, 0.2, 0.0)
        small_new = adamw(small_vectors, small_sum, small_first, small_second, 0.2, 0.0)
        return (
            out_rows,
            grad_rows,
            *attention_new,
            attention_new[0].astype(jnp.bfloat16),
            *dense_new,
            dense_new[0].astype(jnp.bfloat16),
            *head_new,
            *dbias_new,
            *small_new,
        )

    return local


def solution(mesh):
    rows, matrix, halves, units = P("dp", None, None), P(None, "dp", "mp"), P(None, "mp"), P("mp")
    return jax.shard_map(
        make_local(mesh),
        mesh=mesh,
        in_specs=(rows, P("dp", None), rows) + (matrix,) * 6 + (halves,) * 3 + (units,) * 3 + (P(),) * 3,
        out_specs=(rows,) * 2 + (matrix,) * 8 + (halves,) * 3 + (units,) * 3 + (P(),) * 3,
        check_vma=False,
    )
```

```python
import functools

import jax
import jax.numpy as jnp
from jax import lax
from jax.experimental import pallas as pl
from jax.experimental.pallas import tpu as pltpu
from jax.sharding import PartitionSpec as P

HEAD_DIM = 64
PAIR = 2 * HEAD_DIM
STEP = 5
MESH_ID = pl.DeviceIdType.MESH

first_dims = (((0,), (0,)), ((), ()))
last_dims = (((1,), (1,)), ((), ()))


def norm_forward(row_values, gain_row, shift_row):
    center = row_values - jnp.mean(row_values, axis=-1, keepdims=True)
    inverse = lax.rsqrt(jnp.mean(center * center, axis=-1, keepdims=True) + 1e-06)
    normed = center * inverse
    return (normed * gain_row + shift_row, normed, inverse)


def norm_backward(upstream, normed, inverse, gain_row):
    scaled = upstream * gain_row
    back_rows = inverse * (
        scaled
        - jnp.mean(scaled, axis=-1, keepdims=True)
        - normed * jnp.mean(scaled * normed, axis=-1, keepdims=True)
    )
    return (back_rows, jnp.sum(upstream * normed, axis=0), jnp.sum(upstream, axis=0))


def gelu_value(hidden_pre):
    return 0.5 * hidden_pre * (1.0 + lax.erf(hidden_pre * 0.7071067811865476))


def gelu_slope(hidden_pre):
    return (
        0.5 * (1.0 + lax.erf(hidden_pre * 0.7071067811865476))
        + hidden_pre * jnp.exp(-0.5 * hidden_pre * hidden_pre) * 0.3989422804014327
    )


def masked_scores(queries, key_rows, allowed):
    scores = jnp.einsum("qhd,khd->hqk", queries, key_rows, preferred_element_type=jnp.float32)
    return jnp.where(allowed, scores, -1000000000.0)


def adamw(parameter, gradient, moment_one, moment_two, learn_rate, weight_decay):
    first_new = 0.5 * moment_one + 0.5 * gradient
    second_new = 0.5 * moment_two + 0.5 * gradient * gradient
    correction = 1.0 - jnp.power(jnp.float32(0.5), jnp.float32(STEP))
    update = first_new / correction / (jnp.sqrt(second_new / correction) + 1e-08)
    return (
        parameter - learn_rate * update - learn_rate * weight_decay * parameter,
        first_new,
        second_new,
    )


def dot(left, right):
    return jnp.dot(left, right, preferred_element_type=jnp.float32)


def dot_last(left, right):
    return lax.dot_general(left, right, last_dims, preferred_element_type=jnp.float32)


def aligned(at, count):
    return pl.ds(pl.multiple_of(at * count, count), count)


def fold(values):
    return jnp.sum(values.reshape(values.shape[0] // 8, 8, values.shape[1]), axis=0)


def loop(count, body):
    def step(at, carry):
        body(at)
        return carry

    lax.fori_loop(0, count, step, 0)


class Place:
    def __init__(self):
        self.dp = lax.axis_index("dp")
        self.mp = lax.axis_index("mp")
        self.x = self.dp % 2
        self.y = (self.dp // 2) % 2
        self.z = self.dp // 4
        self.z_low = self.z % 2
        self.z_high = self.z // 2
        on_x = self.dp + 1 - 2 * self.x
        on_y = self.dp + 2 - 4 * self.y
        self.near_x = (on_x, self.mp)
        self.near_y = (on_y, self.mp)
        self.near_z = (self.dp + 4 - 8 * self.z_low, self.mp)
        self.opposite_z = (self.dp + 12 - 8 * self.z, self.mp)
        self.inner = (self.z_low + self.z_high) == 1
        self.core = (self.dp, 1 - self.mp)
        self.one = (on_x + (on_y - on_x) * self.mp, self.mp)
        self.two = (on_y + (on_x - on_y) * self.mp, self.mp)
        self.one_at = (self.y + (1 - 2 * self.y) * self.mp, self.x + (1 - 2 * self.x) * (1 - self.mp))
        self.two_at = (self.y + (1 - 2 * self.y) * (1 - self.mp), self.x + (1 - 2 * self.x) * self.mp)
        self.own_at = (self.y, self.x)
        self.cross_at = (1 - self.y, 1 - self.x)
        self.near_at = 2 * self.z_high + 1 - self.z_low
        self.these, self.those = pl.ds(2 * self.z_high, 2), pl.ds(2 - 2 * self.z_high, 2)

    def greet(self):
        barrier = pltpu.get_barrier_semaphore()
        partners = (self.near_x, self.near_y, self.near_z, self.opposite_z, self.core)
        for partner in partners:
            pl.semaphore_signal(barrier, inc=1, device_id=partner, device_id_type=MESH_ID)
        pl.semaphore_wait(barrier, len(partners))


class Sender:
    def __init__(self, send_sems, recv_sems, local_sems):
        self.send_sems, self.recv_sems, self.local_sems = send_sems, recv_sems, local_sems
        self.used, self.used_local, self.open = 0, 0, []

    def plan(self, source, target, device, only=None):
        copy = pltpu.make_async_remote_copy(
            src_ref=source,
            dst_ref=target,
            send_sem=self.send_sems.at[self.used],
            recv_sem=self.recv_sems.at[self.used],
            device_id=device,
            device_id_type=MESH_ID,
        )
        self.used += 1
        self.open.append((copy, only))
        return copy

    def start(self, source, target, device):
        copy = self.plan(source, target, device)
        copy.start()
        return copy

    def start_local(self, source, target):
        copy = pltpu.make_async_copy(source, target, self.local_sems.at[self.used_local])
        self.used_local += 1
        copy.start()
        return copy

    def sent(self, copy):
        self.open = [each for each in self.open if each[0] is not copy]
        copy.wait_send()

    def finish(self):
        for copy, only in self.open:
            if only is None:
                copy.wait_send()
            else:
                pl.when(only)(copy.wait_send)


class Flow:
    def __init__(self, newest_first):
        self.newest_first = newest_first
        self.waiting, self.running, self.done = [], [], set()

    def queue(self, name, piece):
        self.waiting.append((name, piece))

    def add(self, name, piece):
        self.running.append((name, piece))
        next(piece)

    def tick(self):
        for entry in self.running[::-1] if self.newest_first else list(self.running):
            try:
                next(entry[1])
            except StopIteration:
                self.running.remove(entry)
                self.done.add(entry[0])
        if self.waiting:
            self.add(*self.waiting.pop(0))

    def until(self, name):
        while name not in self.done:
            self.tick()

    def finish(self):
        while self.waiting or self.running:
            self.tick()


def spread_square(place, sender, at, cores):
    own, first, second, last = (at(*where) for where in (place.own_at, place.one_at, place.two_at, place.cross_at))
    to_one = sender.start(own, own, place.one)
    to_two = sender.start(own, own, place.two)
    if cores is not None:
        cores.append(sender.start(own, own, place.core))
    yield
    to_one.wait_recv()
    cross = sender.start(first, first, place.two)
    if cores is not None:
        cores.append(sender.start(first, first, place.core))
    yield
    to_two.wait_recv()
    if cores is not None:
        cores.append(sender.start(second, second, place.core))
    yield
    cross.wait_recv()
    if cores is not None:
        cores.append(sender.start(last, last, place.core))


def spread_line(place, sender, at, cores, source=None):
    own = at(place.z)
    near = sender.start(own if source is None else source, own, place.near_z)
    yield
    near.wait_recv()
    these, those = at(place.these), at(place.those)
    across = sender.plan(these, these, place.opposite_z, place.inner)
    onward = sender.plan(those, those, place.near_z, place.inner)
    pl.when(place.inner)(across.start)
    if cores is not None:
        cores.append(sender.start(these, these, place.core))
    yield

    @pl.when(place.inner)
    def _():
        across.wait_recv()
        onward.start()

    yield
    pl.when(jnp.logical_not(place.inner))(onward.wait_recv)
    if cores is not None:
        cores.append(sender.start(those, those, place.core))


def gather_piece(place, sender, source, target, line_first):
    z, (y, x) = place.z, place.own_at
    local = sender.start_local(source, target.at[z, y, x])
    cores = []
    if line_first:
        stage = spread_line(place, sender, lambda at: target.at[at, y, x], None, source)
        next(stage)
        yield
        local.wait()
        yield from stage
        yield from spread_square(place, sender, lambda *at: target.at[:, at[0], at[1]], cores)
    else:
        local.wait()
        yield from spread_square(place, sender, lambda *at: target.at[z, at[0], at[1]], None)
        yield from spread_line(place, sender, lambda at: target.at[at], cores)
    yield
    for copy in cores:
        copy.wait_recv()


GATHER_COPIES = 10


def add_blocks(out, *others):
    lead = out.shape[:-2]
    count = 1
    for size in lead:
        count *= size

    def body(at):
        index = []
        for size in lead[::-1]:
            index.insert(0, at % size)
            at = at // size
        index = tuple(index)
        total = others[0][index].astype(jnp.float32)
        for other in others[1:]:
            total = total + other[index].astype(jnp.float32)
        out[index] = total.astype(out.dtype)

    if lead:
        loop(count, body)
    else:
        total = others[0][...].astype(jnp.float32)
        for other in others[1:]:
            total = total + other[...].astype(jnp.float32)
        out[...] = total.astype(out.dtype)


def reduce_square(place, sender, at, held, out):
    from_cross, from_one, from_two = held
    own, first, second, last = (at(*where) for where in (place.own_at, place.one_at, place.two_at, place.cross_at))
    cross = sender.start(last, from_cross, place.two)
    straight = sender.start(second, from_two, place.two)
    yield
    cross.wait_recv()
    add_blocks(first, first, from_cross)
    turned = sender.start(first, from_one, place.one)
    yield
    straight.wait_recv()
    turned.wait_recv()
    add_blocks(own if out is None else out, own, from_one, from_two)


def reduce_line(place, sender, at, held, out):
    from_end, from_across, from_near = held
    these, those = at(place.these), at(place.those)
    outer = jnp.logical_not(place.inner)
    inward = sender.plan(those, from_end, place.near_z, outer)
    across = sender.plan(those, from_across, place.opposite_z, place.inner)
    pl.when(outer)(inward.start)
    yield

    @pl.when(place.inner)
    def _():
        inward.wait_recv()
        add_blocks(those, those, from_end)
        across.start()

    yield

    @pl.when(place.inner)
    def _():
        across.wait_recv()
        add_blocks(these, these, from_across)

    near = sender.start(at(place.near_at), from_near, place.near_z)
    yield
    near.wait_recv()
    own = at(place.z)
    add_blocks(own if out is None else out, own, from_near)


def scatter_piece(place, sender, gradient, held, out, line_first):
    z, (y, x) = place.z, place.own_at
    if line_first:
        yield from reduce_line(place, sender, lambda at: gradient.at[at], held[3:], None)
        yield from reduce_square(place, sender, lambda *at: gradient.at[z, at[0], at[1]], held[:3], out)
    else:
        yield from reduce_square(place, sender, lambda *at: gradient.at[:, at[0], at[1]], held[:3], None)
        yield from reduce_line(place, sender, lambda at: gradient.at[at, y, x], held[3:], out)


SCATTER_COPIES = 6


def scatter_held(rows, cols, line_first):
    leads = ((),) * 3 + ((2, 2, 2), (2, 2, 2), (2, 2)) if line_first else ((4,),) * 3 + ((2,), (2,), ())
    return [pltpu.VMEM(lead + (rows, cols), jnp.bfloat16) for lead in leads]


def sum_small(place, sender, total, slots):
    for at, partner in enumerate((place.core, place.near_x, place.near_y, place.near_z, place.opposite_z)):
        slots[2 * at] = total[...]
        copy = sender.start(slots.at[2 * at], slots.at[2 * at + 1], partner)
        yield
        copy.wait_recv()
        total[...] = slots[2 * at] + slots[2 * at + 1]


SMALL_HOPS = 5
SMALL_ROWS = 16
DENSE_PARTS = 3
STEP_COLS = 256


def by_square(matrix, part):
    return part == 1


class Layer:
    NORM_ROWS = 128

    def __init__(self, own, refs):
        self.__dict__.update(refs)
        self.own, self.other = own, 1 - own
        self.length, self.width = self.wide.shape
        self.groups = self.dense_weights.shape[0]
        self.cols = self.attention_weights.shape[-1]
        self.units = self.dense_weights.shape[-1]
        self.pairs = self.cols // PAIR
        views = [self.activated.at[:, :, at * self.cols : (at + 1) * self.cols] for at in range(4)]
        self.query_grad, self.key_grad, self.value_grad, self.mixed_grad = views
        self.projected_other = [self.pre_other.at[:, at * self.cols : (at + 1) * self.cols] for at in range(3)]
        self.final = self.tokens.at[self.other]

    def weight(self, ref, group, matrix, cols=None):
        value = ref[group, matrix] if cols is None else ref[group, matrix, ..., cols]
        return value.reshape(self.width, value.shape[-1])

    def weight_rows(self, ref, group, matrix, rows):
        return ref[group, matrix].reshape(self.width, ref.shape[-1])[rows]

    def put_gradient(self, ref, matrix, cols, value):
        ref[matrix, ..., cols] = value.astype(jnp.bfloat16).reshape(ref.shape[1:-1] + (value.shape[-1],))

    def steps(self, part, body):
        size = self.units // DENSE_PARTS
        step = min(STEP_COLS, size)
        loop(size // step, lambda at: body(pl.ds(pl.multiple_of(part * size + at * step, step), step)))


    def project(self, matrix):
        out = (self.queries, self.keys, self.values)[matrix]
        for group in range(self.groups):
            value = dot(self.tokens[self.own], self.weight(self.attention_weights, group, matrix))
            if matrix == 0:
                value = (value + self.head_bias[group, 0:1]) * 0.125
            elif matrix == 2:
                value = value + self.head_bias[group, 1:2]
            value = value.astype(jnp.bfloat16)
            for pair in range(self.pairs):
                out[group * self.pairs + pair] = value[:, pair * PAIR : (pair + 1) * PAIR]

    def attend(self, group, pair):
        at = group * self.pairs + pair
        cols = slice(pair * PAIR, (pair + 1) * PAIR)
        queries, keys, value_turned = self.queries[at], self.keys[at], self.values[at].T
        first = lax.broadcasted_iota(jnp.int32, queries.shape, 1) < HEAD_DIM
        allowed = self.segment_column[...] == self.segment_row[...]
        mixed = []
        for side in range(2):
            mine = jnp.where(first if side == 0 else ~first, queries, jnp.bfloat16(0))
            scores = jnp.where(allowed, dot_last(keys, mine), -1000000000.0)
            peak = jnp.max(scores, axis=0, keepdims=True)
            shifted = jnp.exp(scores - peak)
            total = jnp.sum(shifted, axis=0, keepdims=True)
            attend_low = (shifted * (1.0 / total)).astype(jnp.bfloat16)
            mixed.append(dot(value_turned[side * HEAD_DIM : (side + 1) * HEAD_DIM], attend_low))
            self.log_totals[group, 2 * pair + side : 2 * pair + side + 1] = peak + jnp.log(total)
        self.mixed[group, :, cols] = jnp.concatenate(mixed, axis=0).T.astype(jnp.bfloat16)

    def add_branch(self, group):
        for start in range(0, self.width, STEP_COLS):
            cols = slice(start, start + STEP_COLS)
            part = dot_last(self.mixed[group], self.weight_rows(self.attention_weights, group, 3, cols))
            part = part.astype(jnp.bfloat16).astype(jnp.float32)
            self.wide[:, cols] = part if group == 0 else self.wide[:, cols] + part

    def norm_one(self):
        out_bias, gain, shift = self.small[0:1], self.small[2:3], self.small[3:4]

        def chunk(block):
            rows = aligned(block, self.NORM_ROWS)
            values = self.tokens[self.own, rows].astype(jnp.float32) + self.wide[rows] + out_bias
            center = values - jnp.mean(values, axis=-1, keepdims=True)
            inverse = lax.rsqrt(jnp.mean(center * center, axis=-1, keepdims=True) + 1e-06)
            normed = center * inverse
            self.normed[rows] = normed
            self.inverse[rows] = inverse
            self.hidden_low[rows] = (normed * gain + shift).astype(jnp.bfloat16)

        loop(self.length // self.NORM_ROWS, chunk)

    def expand(self, part):
        def body(cols):
            for group in range(self.groups):
                pre = dot(self.hidden_low[...], self.weight(self.dense_weights, group, 0, cols))
                pre = pre + self.dense_bias[group, :, cols]
                half = 0.5 * (1.0 + lax.erf(pre * 0.7071067811865476))
                self.activated[group, :, cols] = (pre * half).astype(jnp.bfloat16)
                self.slope[group, :, cols] = half + pre * jnp.exp(-0.5 * pre * pre) * 0.3989422804014327

        self.steps(part, body)

    def add_down(self, group):
        for start in range(0, self.width, STEP_COLS):
            cols = slice(start, start + STEP_COLS)
            part = dot_last(self.activated[group], self.weight_rows(self.dense_weights, group, 1, cols))
            part = part.astype(jnp.bfloat16).astype(jnp.float32)
            self.wide[:, cols] = part if group == 0 else self.wide[:, cols] + part

    def norm_two(self):
        down_bias, gain, shift = self.small[1:2], self.small[4:5], self.small[5:6]
        gain_one, shift_one = self.small[2:3], self.small[3:4]

        def chunk(block, sums):
            rows = aligned(block, self.NORM_ROWS)
            hidden = self.normed[rows] * gain_one + shift_one
            values = hidden + self.wide[rows] + down_bias
            center = values - jnp.mean(values, axis=-1, keepdims=True)
            inverse = lax.rsqrt(jnp.mean(center * center, axis=-1, keepdims=True) + 1e-06)
            normed = center * inverse
            self.final[rows] = (normed * gain + shift).astype(jnp.bfloat16)
            upstream = self.back_low[rows].astype(jnp.float32)
            scaled = upstream * gain
            back = inverse * (
                scaled
                - jnp.mean(scaled, axis=-1, keepdims=True)
                - normed * jnp.mean(scaled * normed, axis=-1, keepdims=True)
            )
            self.wide[rows] = back
            self.back_low[rows] = back.astype(jnp.bfloat16)
            return (sums[0] + fold(back), sums[1] + fold(upstream * normed), sums[2] + fold(upstream))

        self.norm_sums(chunk, (1, 4, 5))

    def norm_sums(self, chunk, places):
        zero = jnp.zeros((8, self.width), jnp.float32)
        sums = lax.fori_loop(0, self.length // self.NORM_ROWS, chunk, (zero, zero, zero))
        for row, total in zip(places, sums):
            self.sums[row : row + 1] = jnp.sum(total, axis=0, keepdims=True)


    def turn(self, source, target):
        step = 128
        for start in range(0, self.length, step):
            target[:, start : start + step] = source[start : start + step].T

    def both(self, turned, own, other):
        return dot(turned[self.own], own) + dot(turned[self.other], other)

    def down_gradient(self, part):
        def body(cols):
            value = self.both(self.back_turned, self.activated[self.own, :, cols], self.activated_other[:, cols])
            self.put_gradient(self.dense_grad, 1, cols, value)

        self.steps(part, body)

    def pre_gradient(self, group, part):
        def body(cols):
            grad = dot(self.back_low[...], self.weight(self.dense_weights, group, 1, cols)) * self.slope[group, :, cols]
            grad = grad.astype(jnp.bfloat16)
            self.activated[group, :, cols] = grad
            self.unit_sums[pl.ds(group, 1), cols] = jnp.sum(fold(grad.astype(jnp.float32)), axis=0, keepdims=True)

        self.steps(part, body)

    def up_gradient(self, part):
        def body(cols):
            value = self.both(self.hidden_turned, self.activated[self.own, :, cols], self.pre_other[:, cols])
            self.put_gradient(self.dense_grad, 0, cols, value)

        self.steps(part, body)

    def add_hidden_gradient(self):
        for start in range(0, self.width, STEP_COLS):
            cols = slice(start, start + STEP_COLS)
            total = self.wide[:, cols]
            for group in range(self.groups):
                total = total + dot_last(self.activated[group], self.weight_rows(self.dense_weights, group, 0, cols))
            self.wide[:, cols] = total

    def norm_one_back(self):
        gain = self.small[2:3]

        def chunk(block, sums):
            rows = aligned(block, self.NORM_ROWS)
            upstream, normed = self.wide[rows], self.normed[rows]
            scaled = upstream * gain
            back = self.inverse[rows] * (
                scaled
                - jnp.mean(scaled, axis=-1, keepdims=True)
                - normed * jnp.mean(scaled * normed, axis=-1, keepdims=True)
            )
            self.wide[rows] = back
            self.back_low[rows] = back.astype(jnp.bfloat16)
            return (sums[0] + fold(back), sums[1] + fold(upstream * normed), sums[2] + fold(upstream))

        self.norm_sums(chunk, (0, 2, 3))

    def out_gradient(self):
        value = self.both(self.branch_turned, self.mixed[self.own], self.mixed_other[...])
        self.put_gradient(self.attention_grad, 3, slice(0, self.cols), value)

    def mix_gradient(self, group):
        grad = dot(self.back_low[...], self.weight(self.attention_weights, group, 3)).astype(jnp.bfloat16)
        self.mixed_grad[group] = grad

    def attend_back(self, group, pair):
        at = group * self.pairs + pair
        cols = slice(pair * PAIR, (pair + 1) * PAIR)
        queries, keys, values = self.queries[at], self.keys[at], self.values[at]
        mixed_grad, key_turned = self.mixed_grad[group, :, cols], keys.T
        first = lax.broadcasted_iota(jnp.int32, queries.shape, 1) < HEAD_DIM
        allowed = self.segment_column[...] == self.segment_row[...]
        query_grads, key_grads, value_grads = [], [], []
        for side in range(2):
            here = first if side == 0 else ~first
            scores = dot_last(keys, jnp.where(here, queries, jnp.bfloat16(0)))
            prob_grad = dot_last(values, jnp.where(here, mixed_grad, jnp.bfloat16(0)))
            total = self.log_totals[group, 2 * pair + side : 2 * pair + side + 1]
            attend = jnp.exp(jnp.where(allowed, scores, -1000000000.0) - total)
            inner = jnp.sum(attend * prob_grad, axis=0, keepdims=True)
            score_grad = (attend * (prob_grad - inner)).astype(jnp.bfloat16)
            value_grads.append(dot(attend.astype(jnp.bfloat16), mixed_grad))
            key_grads.append(dot(score_grad, queries))
            query_grads.append(dot(key_turned[side * HEAD_DIM : (side + 1) * HEAD_DIM], score_grad))
        self.value_grad[group, :, cols] = jnp.where(first, *value_grads).astype(jnp.bfloat16)
        self.key_grad[group, :, cols] = jnp.where(first, *key_grads).astype(jnp.bfloat16)
        grad = jnp.concatenate(query_grads, axis=0).T.astype(jnp.bfloat16)
        self.query_grad[group, :, cols] = grad * jnp.bfloat16(0.125)

    def project_gradient(self, matrix):
        ref = (self.query_grad, self.key_grad, self.value_grad)[matrix]
        value = self.both(self.token_turned, ref[self.own], self.projected_other[matrix][...])
        self.put_gradient(self.attention_grad, matrix, slice(0, self.cols), value)

    def head_sums(self):
        for group in range(self.groups):
            for at, ref in enumerate((self.query_grad, self.value_grad)):
                total = jnp.sum(fold(ref[group].astype(jnp.float32)), axis=0, keepdims=True)
                self.sums[10 + group : 11 + group, at * self.cols : (at + 1) * self.cols] = total

    def unit_totals(self):
        for group in range(self.groups):
            for half in range(2):
                row, start = 6 + 2 * group + half, half * self.width
                self.sums[row : row + 1] = self.unit_sums[group : group + 1, start : start + self.width]

    def input_gradient(self):
        for start in range(0, self.width, STEP_COLS):
            cols = slice(start, start + STEP_COLS)
            total = self.wide[:, cols]
            for group in range(self.groups):
                for matrix, ref in enumerate((self.query_grad, self.key_grad, self.value_grad)):
                    weight = self.weight_rows(self.attention_weights, group, matrix, cols)
                    total = total + dot_last(ref[group], weight)
            self.wide[:, cols] = total


def step_kernel(names, *refs):
    refs = dict(zip(names, refs))
    place = Place()
    layer = Layer(place.mp, refs)
    own, other = layer.own, layer.other
    sender = Sender(refs["send_sems"], refs["recv_sems"], refs["local_sems"])
    size = layer.units // DENSE_PARTS

    def part_cols(part):
        return slice(part * size, (part + 1) * size)

    def to_core(source, target):
        return sender.start(source, target, place.core)

    place.greet()
    flow = Flow(True)
    for matrix in range(4):
        source, target = refs["attention_shard"].at[matrix], layer.attention_weights.at[own, matrix]
        flow.queue(("attention", matrix), gather_piece(place, sender, source, target, True))
    for matrix in range(2):
        for part in range(DENSE_PARTS):
            source = refs["dense_shard"].at[matrix, :, part_cols(part)]
            target = layer.dense_weights.at[own, matrix, :, :, :, :, part_cols(part)]
            flow.queue(("dense", matrix, part), gather_piece(place, sender, source, target, not by_square(matrix, part)))
    flow.tick()
    token_copy = sender.start_local(refs["all_tokens"], layer.tokens)
    cotangent_copy = sender.start_local(refs["cotangent"].at[own], layer.back_low)
    layer.head_bias[own] = refs["head_shard"][...]
    layer.dense_bias[own] = refs["dense_bias_shard"][...]
    biases = [to_core(ref.at[own], ref.at[own]) for ref in (layer.head_bias, layer.dense_bias)]
    layer.sums[...] = jnp.zeros_like(layer.sums)
    flow.tick()
    token_copy.wait()
    for core in range(2):
        layer.turn(layer.tokens.at[core], layer.token_turned.at[core])
        flow.tick()
    for copy in biases:
        copy.wait_recv()
    for matrix in range(3):
        flow.until(("attention", matrix))
        layer.project(matrix)
    for group in range(layer.groups):
        for pair in range(layer.pairs):
            layer.attend(group, pair)
            if pair % 3 == 2:
                flow.tick()
    mixed_copy = to_core(layer.mixed.at[other], layer.mixed_other)
    flow.until(("attention", 3))
    for group in range(layer.groups):
        layer.add_branch(group)
    layer.norm_one()
    layer.turn(layer.hidden_low, layer.hidden_turned.at[own])
    hidden_copy = to_core(layer.hidden_turned.at[own], layer.hidden_turned.at[own])
    flow.tick()
    for part in range(DENSE_PARTS):
        flow.until(("dense", 0, part))
        layer.expand(part)
    activated_copy = to_core(layer.activated.at[other], layer.activated_other)
    flow.finish()
    for group in range(layer.groups):
        layer.add_down(group)
    cotangent_copy.wait()
    layer.norm_two()

    out_copies = [
        sender.start_local(layer.final, refs["out_rows"].at[own]),
        to_core(layer.final, refs["out_rows"].at[own]),
    ]
    layer.turn(layer.back_low, layer.back_turned.at[own])
    back_copy = to_core(layer.back_turned.at[own], layer.back_turned.at[own])
    sender.sent(activated_copy)
    for part in range(DENSE_PARTS):
        layer.pre_gradient(other, part)
    pre_copy = to_core(layer.activated.at[other], layer.pre_other)
    activated_copy.wait_recv()
    back_copy.wait_recv()
    held = iter(refs["held"])
    flow = Flow(False)

    def scatter(name, gradient, out, line_first=False):
        flow.add(name, scatter_piece(place, sender, gradient, next(held), out, line_first))

    def scatter_dense(matrix, part):
        gradient = layer.dense_grad.at[matrix, :, :, :, :, part_cols(part)]
        out = refs["dense_share"].at[matrix, :, part_cols(part)]
        scatter(("dense", matrix, part), gradient, out, by_square(matrix, part))

    for part in range(DENSE_PARTS):
        layer.down_gradient(part)
        scatter_dense(1, part)
    for part in range(DENSE_PARTS):
        layer.pre_gradient(own, part)
    flow.tick()
    pre_copy.wait_recv()
    hidden_copy.wait_recv()
    for part in range(DENSE_PARTS):
        layer.up_gradient(part)
        scatter_dense(0, part)
    layer.unit_totals()
    layer.add_hidden_gradient()
    flow.tick()
    layer.norm_one_back()
    layer.turn(layer.back_low, layer.branch_turned.at[own])
    branch_copy = to_core(layer.branch_turned.at[own], layer.branch_turned.at[own])
    sender.sent(pre_copy)
    for group in range(layer.groups):
        layer.mix_gradient(group)
    mixed_copy.wait_recv()
    branch_copy.wait_recv()
    layer.out_gradient()
    scatter(("attention", 3), layer.attention_grad.at[3], refs["attention_share"].at[3])
    flow.tick()
    projected = []
    for group in (other, own):
        for pair in range(layer.pairs):
            layer.attend_back(group, pair)
            flow.tick()
        if group is other:
            for matrix, ref in enumerate((layer.query_grad, layer.key_grad, layer.value_grad)):
                projected.append(to_core(ref.at[other], layer.projected_other[matrix]))
    for matrix in range(3):
        projected[matrix].wait_recv()
        layer.project_gradient(matrix)
        scatter(("attention", matrix), layer.attention_grad.at[matrix], refs["attention_share"].at[matrix])
    layer.head_sums()
    flow.add("small", sum_small(place, sender, layer.sums, refs["slots"]))
    layer.input_gradient()
    out_copies += [
        sender.start_local(layer.wide, refs["grad_rows"].at[own]),
        to_core(layer.wide, refs["grad_rows"].at[own]),
    ]
    flow.finish()
    for copy in out_copies[1::2]:
        copy.wait_recv()
    for copy in out_copies[0::2]:
        copy.wait()
    sender.finish()


def whole_step(tokens, segment_ids, cotangent, attention_shard, dense_shard, head_bias, dense_bias, small):
    _, length, width = tokens.shape
    groups = 2
    rows, cols = attention_shard.shape[1:]
    units = dense_shard.shape[2]
    pairs = groups * cols // PAIR
    low, wide = jnp.bfloat16, jnp.float32
    vmem, anywhere = pl.BlockSpec(memory_space=pltpu.VMEM), pl.BlockSpec(memory_space=pl.ANY)
    mine = lax.axis_index("mp")
    segments = lax.dynamic_index_in_dim(segment_ids, mine, 0, keepdims=False)
    inputs = {
        "all_tokens": (tokens, anywhere),
        "segment_column": (segments[:, None], vmem),
        "segment_row": (segments[None, :], vmem),
        "cotangent": (cotangent, anywhere),
        "attention_shard": (attention_shard, anywhere),
        "dense_shard": (dense_shard, anywhere),
        "head_shard": (head_bias, vmem),
        "dense_bias_shard": (dense_bias[None], vmem),
        "small": (small, vmem),
    }
    outputs = {
        "out_rows": ((tokens.shape, low), anywhere),
        "grad_rows": ((tokens.shape, wide), anywhere),
        "attention_share": ((attention_shard.shape, wide), vmem),
        "dense_share": ((dense_shard.shape, wide), vmem),
        "sums": (((SMALL_ROWS, width), wide), vmem),
    }
    buffers = {
        "attention_weights": ((groups, 4, 4, 2, 2, rows, cols), low),
        "dense_weights": ((groups, 2, 4, 2, 2, rows, units), low),
        "head_bias": ((groups, 2, cols), wide),
        "dense_bias": ((groups, 1, units), wide),
        "attention_grad": ((4, 4, 2, 2, rows, cols), low),
        "dense_grad": ((2, 4, 2, 2, rows, units), low),
        "tokens": (tokens.shape, low),
        "token_turned": ((groups, width, length), low),
        "hidden_turned": ((groups, width, length), low),
        "back_turned": ((groups, width, length), low),
        "branch_turned": ((groups, width, length), low),
        "activated_other": ((length, units), low),
        "pre_other": ((length, units), low),
        "mixed_other": ((length, cols), low),
        "queries": ((pairs, length, PAIR), low),
        "keys": ((pairs, length, PAIR), low),
        "values": ((pairs, length, PAIR), low),
        "mixed": ((groups, length, cols), low),
        "log_totals": ((groups, pl.cdiv(cols // HEAD_DIM, 8) * 8, length), wide),
        "normed": ((length, width), wide),
        "inverse": ((length, 1), wide),
        "hidden_low": ((length, width), low),
        "activated": ((groups, length, units), low),
        "slope": ((groups, length, units), wide),
        "back_low": ((length, width), low),
        "wide": ((length, width), wide),
        "unit_sums": ((groups, units), wide),
        "slots": ((2 * SMALL_HOPS, SMALL_ROWS, width), wide),
    }
    scratch = {name: pltpu.VMEM(*what) for name, what in buffers.items()}
    pieces = 4 + 2 * DENSE_PARTS
    copies = pieces * (GATHER_COPIES + SCATTER_COPIES) + SMALL_HOPS + 2 + 9 + 2
    scratch["send_sems"] = pltpu.SemaphoreType.DMA((copies,))
    scratch["recv_sems"] = pltpu.SemaphoreType.DMA((copies,))
    scratch["local_sems"] = pltpu.SemaphoreType.DMA((pieces + 4,))
    held = [
        scatter_held(rows, units // DENSE_PARTS, by_square(matrix, part)) for matrix in (1, 0) for part in range(DENSE_PARTS)
    ]
    held += [scatter_held(rows, cols, False) for _ in range(4)]
    scratch["held"] = held
    return pl.pallas_call(
        functools.partial(step_kernel, tuple(inputs) + tuple(outputs) + tuple(scratch)),
        name="whole_step",
        out_shape=tuple(jax.ShapeDtypeStruct(*what) for what, _ in outputs.values()),
        in_specs=[spec for _, spec in inputs.values()],
        out_specs=tuple(spec for _, spec in outputs.values()),
        scratch_shapes=list(scratch.values()),
        compiler_params=pltpu.CompilerParams(
            collective_id=0, has_side_effects=True, vmem_limit_bytes=63 * 2**20
        ),
    )(*(value for value, _ in inputs.values()))


def plain_gather(attention_low, dense_low):
    def both(shard):
        return lax.all_gather(lax.all_gather(shard, "dp", axis=1, tiled=True), "mp", axis=0)

    return both(attention_low), both(dense_low)


def plain_scatter(attention_gradient, dense_gradient, small):
    def share(gradient):
        half = lax.psum_scatter(gradient.astype(jnp.float32), "mp", scatter_dimension=0)
        return lax.psum_scatter(half, "dp", scatter_dimension=1, tiled=True)

    return share(attention_gradient), share(dense_gradient), lax.psum(small, ("dp", "mp"))


def plain_layer(row_tokens, segment_row, upstream, attention_full, dense_full, head_bias, dense_bias, small_vectors):
    groups = attention_full.shape[0]
    length = row_tokens.shape[0]
    local_cols = attention_full.shape[3]
    local_heads = local_cols // HEAD_DIM
    allowed = (segment_row[:, None] == segment_row[None, :])[None]
    saved = []
    branch = 0.0
    for group in range(groups):
        weights = attention_full[group]
        queries = (
            (jnp.dot(row_tokens, weights[0], preferred_element_type=jnp.float32) + head_bias[group, 0]) * 0.125
        ).astype(jnp.bfloat16)
        key_rows = jnp.dot(row_tokens, weights[1], preferred_element_type=jnp.float32).astype(jnp.bfloat16)
        value_rows = (
            jnp.dot(row_tokens, weights[2], preferred_element_type=jnp.float32) + head_bias[group, 1]
        ).astype(jnp.bfloat16)
        query_heads = queries.reshape(length, local_heads, HEAD_DIM)
        key_heads = key_rows.reshape(length, local_heads, HEAD_DIM)
        value_heads = value_rows.reshape(length, local_heads, HEAD_DIM)
        scores = masked_scores(query_heads, key_heads, allowed)
        row_peak = jnp.max(scores, axis=-1, keepdims=True)
        shifted_exp = jnp.exp(scores - row_peak)
        exp_total = jnp.sum(shifted_exp, axis=-1, keepdims=True)
        attend_low = (shifted_exp / exp_total).astype(jnp.bfloat16)
        log_total = row_peak + jnp.log(exp_total)
        mixed_heads = (
            jnp.einsum("hqk,khd->qhd", attend_low, value_heads, preferred_element_type=jnp.float32)
            .reshape(length, local_cols)
            .astype(jnp.bfloat16)
        )
        partial_value = lax.dot_general(mixed_heads, weights[3], last_dims, preferred_element_type=jnp.float32)
        branch = branch + partial_value.astype(jnp.bfloat16).astype(jnp.float32)
        saved.append((query_heads, key_heads, value_heads, log_total, mixed_heads))
    hidden, normed_one, inverse_one = norm_forward(
        row_tokens.astype(jnp.float32) + branch + small_vectors[0], small_vectors[2], small_vectors[3]
    )
    hidden_low = hidden.astype(jnp.bfloat16)
    down_out = 0.0
    dense_saved = []
    for group in range(groups):
        hidden_pre = (
            jnp.dot(hidden_low, dense_full[group, 0], preferred_element_type=jnp.float32) + dense_bias[group]
        )
        activated = gelu_value(hidden_pre).astype(jnp.bfloat16)
        down_partial = lax.dot_general(
            activated, dense_full[group, 1], last_dims, preferred_element_type=jnp.float32
        )
        down_out = down_out + down_partial.astype(jnp.bfloat16).astype(jnp.float32)
        dense_saved.append((hidden_pre, activated))
    final, normed_two, inverse_two = norm_forward(
        hidden + down_out + small_vectors[1], small_vectors[4], small_vectors[5]
    )
    back_two, gain_two, shift_two = norm_backward(upstream, normed_two, inverse_two, small_vectors[4])
    down_grad = back_two.astype(jnp.bfloat16)
    hidden_grad = back_two
    dense_grads, dense_bias_grads = [], []
    for group in range(groups):
        hidden_pre, activated = dense_saved[group]
        grad_down_weight = lax.dot_general(down_grad, activated, first_dims, preferred_element_type=jnp.float32)
        pre_grad = (
            jnp.dot(down_grad, dense_full[group, 1], preferred_element_type=jnp.float32) * gelu_slope(hidden_pre)
        ).astype(jnp.bfloat16)
        grad_up_weight = lax.dot_general(hidden_low, pre_grad, first_dims, preferred_element_type=jnp.float32)
        hidden_grad = hidden_grad + lax.dot_general(
            pre_grad, dense_full[group, 0], last_dims, preferred_element_type=jnp.float32
        )
        dense_grads.append(jnp.stack([grad_up_weight, grad_down_weight]))
        dense_bias_grads.append(jnp.sum(pre_grad.astype(jnp.float32), axis=0))
    back_one, gain_one, shift_one = norm_backward(hidden_grad, normed_one, inverse_one, small_vectors[2])
    small_grad = jnp.stack(
        [jnp.sum(back_one, axis=0), jnp.sum(back_two, axis=0), gain_one, shift_one, gain_two, shift_two]
    )
    branch_grad = back_one.astype(jnp.bfloat16)
    input_rows = back_one
    attention_grads, head_grads = [], []
    for group in range(groups):
        weights = attention_full[group]
        query_heads, key_heads, value_heads, log_total, mixed_heads = saved[group]
        grad_out_weight = lax.dot_general(branch_grad, mixed_heads, first_dims, preferred_element_type=jnp.float32)
        mixed_grad = (
            jnp.dot(branch_grad, weights[3], preferred_element_type=jnp.float32)
            .astype(jnp.bfloat16)
            .reshape(length, local_heads, HEAD_DIM)
        )
        attend = jnp.exp(masked_scores(query_heads, key_heads, allowed) - log_total)
        attend_low = attend.astype(jnp.bfloat16)
        prob_grad = jnp.einsum("qhd,khd->hqk", mixed_grad, value_heads, preferred_element_type=jnp.float32)
        value_grad = jnp.einsum(
            "hqk,qhd->khd", attend_low, mixed_grad, preferred_element_type=jnp.float32
        ).astype(jnp.bfloat16)
        inner_total = jnp.sum(attend * prob_grad, axis=-1, keepdims=True)
        score_grad = (attend * (prob_grad - inner_total)).astype(jnp.bfloat16)
        query_grad = (
            jnp.einsum("hqk,khd->qhd", score_grad, key_heads, preferred_element_type=jnp.float32).astype(jnp.bfloat16)
            * 0.125
        )
        key_grad = jnp.einsum(
            "hqk,qhd->khd", score_grad, query_heads, preferred_element_type=jnp.float32
        ).astype(jnp.bfloat16)
        stacked = [each.reshape(length, local_cols) for each in (query_grad, key_grad, value_grad)]
        grads = [
            lax.dot_general(row_tokens, each, first_dims, preferred_element_type=jnp.float32) for each in stacked
        ]
        for each, weight in zip(stacked, weights[:3]):
            input_rows = input_rows + lax.dot_general(each, weight, last_dims, preferred_element_type=jnp.float32)
        attention_grads.append(jnp.stack(grads + [grad_out_weight]))
        head_grads.append(
            jnp.stack(
                [jnp.sum(stacked[0].astype(jnp.float32), axis=0), jnp.sum(stacked[2].astype(jnp.float32), axis=0)]
            )
        )
    return (
        final.astype(jnp.bfloat16),
        input_rows,
        jnp.stack(attention_grads).astype(jnp.bfloat16),
        jnp.stack(dense_grads).astype(jnp.bfloat16),
        jnp.stack(head_grads),
        jnp.stack(dense_bias_grads),
        small_grad,
    )


def plain_step(tokens, segment_ids, cotangent, attention_low, dense_low, head_bias, dense_bias, small_vectors):
    attention_full, dense_full = plain_gather(attention_low, dense_low)
    head_full = lax.all_gather(head_bias, "mp", axis=0)
    dense_bias_full = lax.all_gather(dense_bias, "mp", axis=0)
    mine = lax.axis_index("mp")
    row_tokens = lax.dynamic_index_in_dim(tokens, mine, 0, keepdims=False)
    segment_row = lax.dynamic_index_in_dim(segment_ids, mine, 0, keepdims=False)
    upstream = lax.dynamic_index_in_dim(cotangent, mine, 0, keepdims=False).astype(jnp.float32)
    final, input_rows, attention_grad, dense_grad, head_grad, dense_bias_grad, small_grad = plain_layer(
        row_tokens, segment_row, upstream, attention_full, dense_full, head_full, dense_bias_full, small_vectors
    )
    width = tokens.shape[2]
    sums = jnp.concatenate([part.reshape(-1, width) for part in (small_grad, dense_bias_grad, head_grad)])
    attention_share, dense_share, sums = plain_scatter(attention_grad, dense_grad, sums)
    out_rows, grad_rows = (lax.all_gather(rows, "mp", axis=0) for rows in (final, input_rows))
    return out_rows, grad_rows, attention_share, dense_share, sums


def make_local(mesh):
    n_dp, n_mp = mesh.shape["dp"], mesh.shape["mp"]
    square = n_dp == 16 and n_mp == 2

    def local(
        tokens,
        segment_ids,
        cotangent,
        attention_master,
        attention_first,
        attention_second,
        dense_master,
        dense_first,
        dense_second,
        head_bias,
        head_bias_first,
        head_bias_second,
        dense_bias,
        dense_bias_first,
        dense_bias_second,
        small_vectors,
        small_first,
        small_second,
    ):
        attention_low, dense_low = attention_master.astype(jnp.bfloat16), dense_master.astype(jnp.bfloat16)
        step = whole_step if square else plain_step
        out_rows, grad_rows, attention_share, dense_share, sums = step(
            tokens, segment_ids, cotangent, attention_low, dense_low, head_bias, dense_bias, small_vectors
        )
        mine = lax.axis_index("mp")
        width, cols, units = tokens.shape[2], head_bias.shape[1], dense_bias.shape[0]
        small_sum = sums[:6]
        dense_bias_sum = lax.dynamic_slice(sums, (6 + 2 * mine, 0), (2, width)).reshape(units)
        head_sum = lax.dynamic_slice(sums, (10 + mine, 0), (1, width)).reshape(2, cols)
        attention_new = adamw(attention_master, attention_share, attention_first, attention_second, 0.03, 0.01)
        dense_new = adamw(dense_master, dense_share, dense_first, dense_second, 0.03, 0.01)
        head_new = adamw(head_bias, head_sum, head_bias_first, head_bias_second, 0.2, 0.0)
        dbias_new = adamw(dense_bias, dense_bias_sum, dense_bias_first, dense_bias_second, 0.2, 0.0)
        small_new = adamw(small_vectors, small_sum, small_first, small_second, 0.2, 0.0)
        return (
            out_rows,
            grad_rows,
            *attention_new,
            attention_new[0].astype(jnp.bfloat16),
            *dense_new,
            dense_new[0].astype(jnp.bfloat16),
            *head_new,
            *dbias_new,
            *small_new,
        )

    return local


def solution(mesh):
    rows, matrix, halves, units = P("dp", None, None), P(None, "dp", "mp"), P(None, "mp"), P("mp")
    return jax.shard_map(
        make_local(mesh),
        mesh=mesh,
        in_specs=(rows, P("dp", None), rows) + (matrix,) * 6 + (halves,) * 3 + (units,) * 3 + (P(),) * 3,
        out_specs=(rows,) * 2 + (matrix,) * 8 + (halves,) * 3 + (units,) * 3 + (P(),) * 3,
        check_vma=False,
    )
```

```python
import functools

import jax
import jax.numpy as jnp
from jax import lax
from jax.experimental import pallas as pl
from jax.experimental.pallas import tpu as pltpu
from jax.sharding import PartitionSpec as P

HEAD_DIM = 64
PAIR = 2 * HEAD_DIM
STEP = 5
MESH_ID = pl.DeviceIdType.MESH

first_dims = (((0,), (0,)), ((), ()))
last_dims = (((1,), (1,)), ((), ()))


def norm_forward(row_values, gain_row, shift_row):
    center = row_values - jnp.mean(row_values, axis=-1, keepdims=True)
    inverse = lax.rsqrt(jnp.mean(center * center, axis=-1, keepdims=True) + 1e-06)
    normed = center * inverse
    return (normed * gain_row + shift_row, normed, inverse)


def norm_backward(upstream, normed, inverse, gain_row):
    scaled = upstream * gain_row
    back_rows = inverse * (
        scaled
        - jnp.mean(scaled, axis=-1, keepdims=True)
        - normed * jnp.mean(scaled * normed, axis=-1, keepdims=True)
    )
    return (back_rows, jnp.sum(upstream * normed, axis=0), jnp.sum(upstream, axis=0))


def gelu_value(hidden_pre):
    return 0.5 * hidden_pre * (1.0 + lax.erf(hidden_pre * 0.7071067811865476))


def gelu_slope(hidden_pre):
    return (
        0.5 * (1.0 + lax.erf(hidden_pre * 0.7071067811865476))
        + hidden_pre * jnp.exp(-0.5 * hidden_pre * hidden_pre) * 0.3989422804014327
    )


def masked_scores(queries, key_rows, allowed):
    scores = jnp.einsum("qhd,khd->hqk", queries, key_rows, preferred_element_type=jnp.float32)
    return jnp.where(allowed, scores, -1000000000.0)


def adamw(parameter, gradient, moment_one, moment_two, learn_rate, weight_decay):
    first_new = 0.5 * moment_one + 0.5 * gradient
    second_new = 0.5 * moment_two + 0.5 * gradient * gradient
    correction = 1.0 - jnp.power(jnp.float32(0.5), jnp.float32(STEP))
    update = first_new / correction / (jnp.sqrt(second_new / correction) + 1e-08)
    return (
        parameter - learn_rate * update - learn_rate * weight_decay * parameter,
        first_new,
        second_new,
    )


def dot(left, right):
    return jnp.dot(left, right, preferred_element_type=jnp.float32)


def dot_last(left, right):
    return lax.dot_general(left, right, last_dims, preferred_element_type=jnp.float32)


def aligned(at, count):
    return pl.ds(pl.multiple_of(at * count, count), count)


def fold(values):
    return jnp.sum(values.reshape(values.shape[0] // 8, 8, values.shape[1]), axis=0)


def loop(count, body):
    def step(at, carry):
        body(at)
        return carry

    lax.fori_loop(0, count, step, 0)


class Place:
    def __init__(self):
        self.dp = lax.axis_index("dp")
        self.mp = lax.axis_index("mp")
        self.x = self.dp % 2
        self.y = (self.dp // 2) % 2
        self.z = self.dp // 4
        self.z_low = self.z % 2
        self.z_high = self.z // 2
        on_x = self.dp + 1 - 2 * self.x
        on_y = self.dp + 2 - 4 * self.y
        self.near_x = (on_x, self.mp)
        self.near_y = (on_y, self.mp)
        self.near_z = (self.dp + 4 - 8 * self.z_low, self.mp)
        self.opposite_z = (self.dp + 12 - 8 * self.z, self.mp)
        self.inner = (self.z_low + self.z_high) == 1
        self.core = (self.dp, 1 - self.mp)
        self.one = (on_x + (on_y - on_x) * self.mp, self.mp)
        self.two = (on_y + (on_x - on_y) * self.mp, self.mp)
        self.one_at = (self.y + (1 - 2 * self.y) * self.mp, self.x + (1 - 2 * self.x) * (1 - self.mp))
        self.two_at = (self.y + (1 - 2 * self.y) * (1 - self.mp), self.x + (1 - 2 * self.x) * self.mp)
        self.own_at = (self.y, self.x)
        self.cross_at = (1 - self.y, 1 - self.x)
        self.near_at = 2 * self.z_high + 1 - self.z_low
        self.these, self.those = pl.ds(2 * self.z_high, 2), pl.ds(2 - 2 * self.z_high, 2)

    def greet(self):
        barrier = pltpu.get_barrier_semaphore()
        partners = (self.near_x, self.near_y, self.near_z, self.opposite_z, self.core)
        for partner in partners:
            pl.semaphore_signal(barrier, inc=1, device_id=partner, device_id_type=MESH_ID)
        pl.semaphore_wait(barrier, len(partners))


class Sender:
    def __init__(self, send_sems, recv_sems, local_sems):
        self.send_sems, self.recv_sems, self.local_sems = send_sems, recv_sems, local_sems
        self.used, self.used_local, self.open = 0, 0, []

    def plan(self, source, target, device, only=None):
        copy = pltpu.make_async_remote_copy(
            src_ref=source,
            dst_ref=target,
            send_sem=self.send_sems.at[self.used],
            recv_sem=self.recv_sems.at[self.used],
            device_id=device,
            device_id_type=MESH_ID,
        )
        self.used += 1
        self.open.append((copy, only))
        return copy

    def start(self, source, target, device):
        copy = self.plan(source, target, device)
        copy.start()
        return copy

    def start_local(self, source, target):
        copy = pltpu.make_async_copy(source, target, self.local_sems.at[self.used_local])
        self.used_local += 1
        copy.start()
        return copy

    def sent(self, copy):
        self.open = [each for each in self.open if each[0] is not copy]
        copy.wait_send()

    def finish(self):
        for copy, only in self.open:
            if only is None:
                copy.wait_send()
            else:
                pl.when(only)(copy.wait_send)


class Program:
    def __init__(self):
        self.actions, self.transfers, self.done = {}, {}, set()

    def action(self, name, act):
        self.actions[name] = act

    def transfer(self, name, stages):
        self.transfers[name] = stages

    def run(self, name):
        if name in self.actions:
            self.actions.pop(name)()
        elif name in self.transfers and name not in self.done:
            try:
                next(self.transfers[name])
            except StopIteration:
                self.done.add(name)

    def need(self, *names):
        for name in names:
            while name not in self.done:
                self.run(name)

    def finish(self):
        for name in list(self.actions):
            self.run(name)
        self.need(*self.transfers)


def spread_square(place, sender, at, cores):
    own, first, second, last = (at(*where) for where in (place.own_at, place.one_at, place.two_at, place.cross_at))
    to_one = sender.start(own, own, place.one)
    to_two = sender.start(own, own, place.two)
    if cores is not None:
        cores.append(sender.start(own, own, place.core))
    yield
    to_one.wait_recv()
    cross = sender.start(first, first, place.two)
    if cores is not None:
        cores.append(sender.start(first, first, place.core))
    yield
    to_two.wait_recv()
    if cores is not None:
        cores.append(sender.start(second, second, place.core))
    yield
    cross.wait_recv()
    if cores is not None:
        cores.append(sender.start(last, last, place.core))


def spread_line(place, sender, at, cores):
    own = at(place.z)
    near = sender.start(own, own, place.near_z)
    yield
    near.wait_recv()
    these, those = at(place.these), at(place.those)
    across = sender.plan(these, these, place.opposite_z, place.inner)
    onward = sender.plan(those, those, place.near_z, place.inner)
    pl.when(place.inner)(across.start)
    if cores is not None:
        cores.append(sender.start(these, these, place.core))
    yield

    @pl.when(place.inner)
    def _():
        across.wait_recv()
        onward.start()

    yield
    pl.when(jnp.logical_not(place.inner))(onward.wait_recv)
    if cores is not None:
        cores.append(sender.start(those, those, place.core))


def gather_piece(place, sender, target, line_first):
    z, (y, x) = place.z, place.own_at
    cores = []
    if line_first:
        yield from spread_line(place, sender, lambda at: target.at[at, y, x], None)
        yield from spread_square(place, sender, lambda *at: target.at[:, at[0], at[1]], cores)
    else:
        yield from spread_square(place, sender, lambda *at: target.at[z, at[0], at[1]], None)
        yield from spread_line(place, sender, lambda at: target.at[at], cores)
    yield
    for copy in cores:
        copy.wait_recv()


GATHER_COPIES = 10


def add_blocks(out, *others):
    lead = out.shape[:-2]
    count = 1
    for size in lead:
        count *= size

    def body(at):
        index = []
        for size in lead[::-1]:
            index.insert(0, at % size)
            at = at // size
        index = tuple(index)
        total = others[0][index].astype(jnp.float32)
        for other in others[1:]:
            total = total + other[index].astype(jnp.float32)
        out[index] = total.astype(out.dtype)

    if lead:
        loop(count, body)
    else:
        total = others[0][...].astype(jnp.float32)
        for other in others[1:]:
            total = total + other[...].astype(jnp.float32)
        out[...] = total.astype(out.dtype)


def reduce_square(place, sender, at, held, out):
    from_cross, from_one, from_two = held
    own, first, second, last = (at(*where) for where in (place.own_at, place.one_at, place.two_at, place.cross_at))
    cross = sender.start(last, from_cross, place.two)
    straight = sender.start(second, from_two, place.two)
    yield
    cross.wait_recv()
    add_blocks(first, first, from_cross)
    turned = sender.start(first, from_one, place.one)
    yield
    straight.wait_recv()
    turned.wait_recv()
    add_blocks(own if out is None else out, own, from_one, from_two)


def reduce_line(place, sender, at, held, out):
    from_end, from_across, from_near = held
    these, those = at(place.these), at(place.those)
    outer = jnp.logical_not(place.inner)
    inward = sender.plan(those, from_end, place.near_z, outer)
    across = sender.plan(those, from_across, place.opposite_z, place.inner)
    pl.when(outer)(inward.start)
    yield

    @pl.when(place.inner)
    def _():
        inward.wait_recv()
        add_blocks(those, those, from_end)
        across.start()

    yield

    @pl.when(place.inner)
    def _():
        across.wait_recv()
        add_blocks(these, these, from_across)

    near = sender.start(at(place.near_at), from_near, place.near_z)
    yield
    near.wait_recv()
    own = at(place.z)
    add_blocks(own if out is None else out, own, from_near)


def scatter_piece(place, sender, gradient, held, out, line_first):
    z, (y, x) = place.z, place.own_at
    if line_first:
        yield from reduce_line(place, sender, lambda at: gradient.at[at], held[3:], None)
        yield from reduce_square(place, sender, lambda *at: gradient.at[z, at[0], at[1]], held[:3], out)
    else:
        yield from reduce_square(place, sender, lambda *at: gradient.at[:, at[0], at[1]], held[:3], None)
        yield from reduce_line(place, sender, lambda at: gradient.at[at, y, x], held[3:], out)


SCATTER_COPIES = 6


def scatter_held(rows, cols, line_first):
    leads = ((),) * 3 + ((2, 2, 2), (2, 2, 2), (2, 2)) if line_first else ((4,),) * 3 + ((2,), (2,), ())
    return [pltpu.VMEM(lead + (rows, cols), jnp.bfloat16) for lead in leads]


def sum_small(place, sender, total, slots):
    for at, partner in enumerate((place.core, place.near_x, place.near_y, place.near_z, place.opposite_z)):
        slots[2 * at] = total[...]
        copy = sender.start(slots.at[2 * at], slots.at[2 * at + 1], partner)
        yield
        copy.wait_recv()
        total[...] = slots[2 * at] + slots[2 * at + 1]


SMALL_HOPS = 5
SMALL_ROWS = 16
DENSE_PARTS = 3
STEP_COLS = 256


SQUARE_FIRST = ("u0", "d0", "D1", "U1")


class Layer:
    NORM_ROWS = 128

    def __init__(self, own, refs):
        self.__dict__.update(refs)
        self.own, self.other = own, 1 - own
        self.length, self.width = self.wide.shape
        self.groups = self.dense_weights.shape[0]
        self.cols = self.attention_weights.shape[-1]
        self.units = self.dense_weights.shape[-1]
        self.pairs = self.cols // PAIR
        views = [self.activated.at[:, :, at * self.cols : (at + 1) * self.cols] for at in range(4)]
        self.query_grad, self.key_grad, self.value_grad, self.mixed_grad = views
        self.projected_other = [self.pre_other.at[:, at * self.cols : (at + 1) * self.cols] for at in range(3)]
        self.final = self.tokens.at[self.other]

    def weight(self, ref, group, matrix, cols=None):
        value = ref[group, matrix] if cols is None else ref[group, matrix, ..., cols]
        return value.reshape(self.width, value.shape[-1])

    def weight_rows(self, ref, group, matrix, rows):
        return ref[group, matrix].reshape(self.width, ref.shape[-1])[rows]

    def put_gradient(self, ref, matrix, cols, value):
        ref[matrix, ..., cols] = value.astype(jnp.bfloat16).reshape(ref.shape[1:-1] + (value.shape[-1],))

    def steps(self, part, body):
        size = self.units // DENSE_PARTS
        step = min(STEP_COLS, size)
        loop(size // step, lambda at: body(pl.ds(pl.multiple_of(part * size + at * step, step), step)))


    def project(self, matrix):
        out = (self.queries, self.keys, self.values)[matrix]
        for group in range(self.groups):
            value = dot(self.tokens[self.own], self.weight(self.attention_weights, group, matrix))
            if matrix == 0:
                value = (value + self.head_bias[group, 0:1]) * 0.125
            elif matrix == 2:
                value = value + self.head_bias[group, 1:2]
            value = value.astype(jnp.bfloat16)
            for pair in range(self.pairs):
                out[group * self.pairs + pair] = value[:, pair * PAIR : (pair + 1) * PAIR]

    def attend(self, group, pair):
        at = group * self.pairs + pair
        cols = aligned(pair, PAIR)
        queries, keys, value_turned = self.queries[at], self.keys[at], self.values[at].T
        first = lax.broadcasted_iota(jnp.int32, queries.shape, 1) < HEAD_DIM
        allowed = self.segment_column[...] == self.segment_row[...]
        mixed = []
        for side in range(2):
            mine = jnp.where(first if side == 0 else ~first, queries, jnp.bfloat16(0))
            scores = jnp.where(allowed, dot_last(keys, mine), -1000000000.0)
            peak = jnp.max(scores, axis=0, keepdims=True)
            shifted = jnp.exp(scores - peak)
            total = jnp.sum(shifted, axis=0, keepdims=True)
            attend_low = (shifted * (1.0 / total)).astype(jnp.bfloat16)
            mixed.append(dot(value_turned[side * HEAD_DIM : (side + 1) * HEAD_DIM], attend_low))
            self.log_totals[group, pl.ds(2 * pair + side, 1)] = peak + jnp.log(total)
        self.mixed[group, :, cols] = jnp.concatenate(mixed, axis=0).T.astype(jnp.bfloat16)

    def add_branch(self, group):
        for start in range(0, self.width, STEP_COLS):
            cols = slice(start, start + STEP_COLS)
            part = dot_last(self.mixed[group], self.weight_rows(self.attention_weights, group, 3, cols))
            part = part.astype(jnp.bfloat16).astype(jnp.float32)
            self.wide[:, cols] = part if group == 0 else self.wide[:, cols] + part

    def norm_one(self):
        out_bias, gain, shift = self.small[0:1], self.small[2:3], self.small[3:4]

        def chunk(block):
            rows = aligned(block, self.NORM_ROWS)
            values = self.tokens[self.own, rows].astype(jnp.float32) + self.wide[rows] + out_bias
            center = values - jnp.mean(values, axis=-1, keepdims=True)
            inverse = lax.rsqrt(jnp.mean(center * center, axis=-1, keepdims=True) + 1e-06)
            normed = center * inverse
            self.normed[rows] = normed
            self.inverse[rows] = inverse
            self.hidden_low[rows] = (normed * gain + shift).astype(jnp.bfloat16)

        loop(self.length // self.NORM_ROWS, chunk)

    def expand(self, part):
        def body(cols):
            for group in range(self.groups):
                pre = dot(self.hidden_low[...], self.weight(self.dense_weights, group, 0, cols))
                pre = pre + self.dense_bias[group, :, cols]
                half = 0.5 * (1.0 + lax.erf(pre * 0.7071067811865476))
                self.activated[group, :, cols] = (pre * half).astype(jnp.bfloat16)
                self.slope[group, :, cols] = half + pre * jnp.exp(-0.5 * pre * pre) * 0.3989422804014327

        self.steps(part, body)

    def add_down(self, group):
        for start in range(0, self.width, STEP_COLS):
            cols = slice(start, start + STEP_COLS)
            part = dot_last(self.activated[group], self.weight_rows(self.dense_weights, group, 1, cols))
            part = part.astype(jnp.bfloat16).astype(jnp.float32)
            self.wide[:, cols] = part if group == 0 else self.wide[:, cols] + part

    def norm_two(self):
        down_bias, gain, shift = self.small[1:2], self.small[4:5], self.small[5:6]
        gain_one, shift_one = self.small[2:3], self.small[3:4]

        def chunk(block, sums):
            rows = aligned(block, self.NORM_ROWS)
            hidden = self.normed[rows] * gain_one + shift_one
            values = hidden + self.wide[rows] + down_bias
            center = values - jnp.mean(values, axis=-1, keepdims=True)
            inverse = lax.rsqrt(jnp.mean(center * center, axis=-1, keepdims=True) + 1e-06)
            normed = center * inverse
            self.final[rows] = (normed * gain + shift).astype(jnp.bfloat16)
            upstream = self.back_low[rows].astype(jnp.float32)
            scaled = upstream * gain
            back = inverse * (
                scaled
                - jnp.mean(scaled, axis=-1, keepdims=True)
                - normed * jnp.mean(scaled * normed, axis=-1, keepdims=True)
            )
            self.wide[rows] = back
            self.back_low[rows] = back.astype(jnp.bfloat16)
            return (sums[0] + fold(back), sums[1] + fold(upstream * normed), sums[2] + fold(upstream))

        self.norm_sums(chunk, (1, 4, 5))

    def norm_sums(self, chunk, places):
        zero = jnp.zeros((8, self.width), jnp.float32)
        sums = lax.fori_loop(0, self.length // self.NORM_ROWS, chunk, (zero, zero, zero))
        for row, total in zip(places, sums):
            self.sums[row : row + 1] = jnp.sum(total, axis=0, keepdims=True)


    def turn(self, source, target):
        step = 128
        for start in range(0, self.length, step):
            target[:, start : start + step] = source[start : start + step].T

    def both(self, turned, own, other):
        return dot(turned[self.own], own) + dot(turned[self.other], other)

    def down_gradient(self, part):
        def body(cols):
            value = self.both(self.back_turned, self.activated[self.own, :, cols], self.activated_other[:, cols])
            self.put_gradient(self.dense_grad, 1, cols, value)

        self.steps(part, body)

    def pre_gradient(self, group, part):
        def body(cols):
            grad = dot(self.back_low[...], self.weight(self.dense_weights, group, 1, cols)) * self.slope[group, :, cols]
            grad = grad.astype(jnp.bfloat16)
            self.activated[group, :, cols] = grad
            self.unit_sums[pl.ds(group, 1), cols] = jnp.sum(fold(grad.astype(jnp.float32)), axis=0, keepdims=True)

        self.steps(part, body)

    def up_gradient(self, part):
        def body(cols):
            value = self.both(self.hidden_turned, self.activated[self.own, :, cols], self.pre_other[:, cols])
            self.put_gradient(self.dense_grad, 0, cols, value)

        self.steps(part, body)

    def add_hidden_gradient(self):
        for start in range(0, self.width, STEP_COLS):
            cols = slice(start, start + STEP_COLS)
            total = self.wide[:, cols]
            for group in range(self.groups):
                total = total + dot_last(self.activated[group], self.weight_rows(self.dense_weights, group, 0, cols))
            self.wide[:, cols] = total

    def norm_one_back(self):
        gain = self.small[2:3]

        def chunk(block, sums):
            rows = aligned(block, self.NORM_ROWS)
            upstream, normed = self.wide[rows], self.normed[rows]
            scaled = upstream * gain
            back = self.inverse[rows] * (
                scaled
                - jnp.mean(scaled, axis=-1, keepdims=True)
                - normed * jnp.mean(scaled * normed, axis=-1, keepdims=True)
            )
            self.wide[rows] = back
            self.back_low[rows] = back.astype(jnp.bfloat16)
            return (sums[0] + fold(back), sums[1] + fold(upstream * normed), sums[2] + fold(upstream))

        self.norm_sums(chunk, (0, 2, 3))

    def out_gradient(self):
        value = self.both(self.branch_turned, self.mixed[self.own], self.mixed_other[...])
        self.put_gradient(self.attention_grad, 3, slice(0, self.cols), value)

    def mix_gradient(self, group):
        grad = dot(self.back_low[...], self.weight(self.attention_weights, group, 3)).astype(jnp.bfloat16)
        self.mixed_grad[group] = grad

    def attend_back(self, group, pair):
        at = group * self.pairs + pair
        cols = aligned(pair, PAIR)
        queries, keys, values = self.queries[at], self.keys[at], self.values[at]
        mixed_grad, key_turned = self.mixed_grad[group, :, cols], keys.T
        first = lax.broadcasted_iota(jnp.int32, queries.shape, 1) < HEAD_DIM
        allowed = self.segment_column[...] == self.segment_row[...]
        query_grads, key_grads, value_grads = [], [], []
        for side in range(2):
            here = first if side == 0 else ~first
            scores = dot_last(keys, jnp.where(here, queries, jnp.bfloat16(0)))
            prob_grad = dot_last(values, jnp.where(here, mixed_grad, jnp.bfloat16(0)))
            total = self.log_totals[group, pl.ds(2 * pair + side, 1)]
            attend = jnp.exp(jnp.where(allowed, scores, -1000000000.0) - total)
            inner = jnp.sum(attend * prob_grad, axis=0, keepdims=True)
            score_grad = (attend * (prob_grad - inner)).astype(jnp.bfloat16)
            value_grads.append(dot(attend.astype(jnp.bfloat16), mixed_grad))
            key_grads.append(dot(score_grad, queries))
            query_grads.append(dot(key_turned[side * HEAD_DIM : (side + 1) * HEAD_DIM], score_grad))
        self.value_grad[group, :, cols] = jnp.where(first, *value_grads).astype(jnp.bfloat16)
        self.key_grad[group, :, cols] = jnp.where(first, *key_grads).astype(jnp.bfloat16)
        grad = jnp.concatenate(query_grads, axis=0).T.astype(jnp.bfloat16)
        self.query_grad[group, :, cols] = grad * jnp.bfloat16(0.125)

    def project_gradient(self, matrix):
        ref = (self.query_grad, self.key_grad, self.value_grad)[matrix]
        value = self.both(self.token_turned, ref[self.own], self.projected_other[matrix][...])
        self.put_gradient(self.attention_grad, matrix, slice(0, self.cols), value)

    def head_sums(self):
        for group in range(self.groups):
            for at, ref in enumerate((self.query_grad, self.value_grad)):
                total = jnp.sum(fold(ref[group].astype(jnp.float32)), axis=0, keepdims=True)
                self.sums[10 + group : 11 + group, at * self.cols : (at + 1) * self.cols] = total

    def unit_totals(self):
        for group in range(self.groups):
            for half in range(2):
                row, start = 6 + 2 * group + half, half * self.width
                self.sums[row : row + 1] = self.unit_sums[group : group + 1, start : start + self.width]

    def input_gradient(self):
        for start in range(0, self.width, STEP_COLS):
            cols = slice(start, start + STEP_COLS)
            total = self.wide[:, cols]
            for group in range(self.groups):
                for matrix, ref in enumerate((self.query_grad, self.key_grad, self.value_grad)):
                    weight = self.weight_rows(self.attention_weights, group, matrix, cols)
                    total = total + dot_last(ref[group], weight)
            self.wide[:, cols] = total


PLAN = (
    "a1", "start", "a0", "u0", "a1", "a2", "a3", "d0", "u0", "d1", "a0", "a1", "u2", "a2", "d0", "a1", "u1", "a0",
    "d0", "d1", "d2", "a3", "u2", "a2", "u0", "a0", "u0", "a1", "a3", "turn", "u1", "u2", "a2", "u0", "a0", "a3",
    "a0", "u1", "a2", "a1", "a0", "d2", "a1", "d0", "a0", "u2", "a1", "d1", "a2", "a2", "d0", "a3", "u1", "u0", "a2",
    "q0", "q1", "q2", "d2", "a3", "u2", "t0", "d1", "a3", "u1", "t1", "u2", "d0", "d2", "u0", "u2", "u1", "a3",
    "branch", "d1", "u1", "u0", "d1", "n1", "u2", "u1", "d2", "d0", "e0", "e1", "d2", "d1", "d2", "d0", "e2", "d1",
    "d2", "down", "n2", "p0", "p1", "p2", "g0", "D0", "g1", "g2", "D1", "r0", "r1", "D2", "r2", "h0", "h1", "D0",
    "h2", "U1", "D2", "U0", "hidden", "n3", "D1", "mix", "out", "U2", "x", "D0", "U1", "U0", "A3", "D1", "D0", "U2",
    "y", "z0", "A3", "U0", "A0", "z1", "U0", "z2", "D2", "D1", "U1", "small", "A0", "A3", "A2", "D2", "A1", "s", "U0",
    "U2", "A3", "s", "A0", "input", "A2", "A3", "D2", "U2", "A1", "U0", "U2", "D0", "A2", "D1", "s", "A0", "A1", "A2",
    "U1", "U2", "s", "A1", "D0", "D1", "U1", "A2", "A0", "s", "D2", "A1", "U1", "A0", "A2", "s", "A3", "A1",
)


def step_kernel(names, *refs):
    refs = dict(zip(names, refs))
    place = Place()
    layer = Layer(place.mp, refs)
    own, other = layer.own, layer.other
    sender = Sender(refs["send_sems"], refs["recv_sems"], refs["local_sems"])
    program = Program()
    size = layer.units // DENSE_PARTS
    rows = refs["attention_master"].shape[1]
    parts = range(DENSE_PARTS)
    links, swaps = {}, {}

    def part_cols(part):
        return slice(part * size, (part + 1) * size)

    def to_core(source, target):
        return sender.start(source, target, place.core)

    def swap(name, ref):
        swaps[name] = to_core(ref.at[own], ref.at[own])

    dense_wide = layer.slope.at[:, 0:rows]
    attention_wide = [layer.slope.at[0, 2 * rows : 3 * rows, at * layer.cols : (at + 1) * layer.cols] for at in range(4)]
    masters = [sender.start_local(refs["attention_master"].at[at], ref) for at, ref in enumerate(attention_wide)]
    masters.append(sender.start_local(refs["dense_master"], dense_wide))
    links["tokens"] = sender.start_local(refs["all_tokens"], layer.tokens)
    links["cotangent"] = sender.start_local(refs["cotangent"].at[own], layer.back_low)
    here = (place.z, place.y, place.x)
    for matrix in range(4):
        masters[matrix].wait()
        layer.attention_weights[(own, matrix) + here] = attention_wide[matrix][...].astype(jnp.bfloat16)
    place.greet()
    for matrix in range(4):
        target = layer.attention_weights.at[own, matrix]
        program.transfer("a%d" % matrix, gather_piece(place, sender, target, True))
    for matrix, letter in enumerate("ud"):
        for part in parts:
            target = layer.dense_weights.at[own, matrix, :, :, :, :, part_cols(part)]
            name = letter + str(part)
            program.transfer(name, gather_piece(place, sender, target, name not in SQUARE_FIRST))

    def start():
        masters[4].wait()
        for matrix in range(2):
            layer.dense_weights[(own, matrix) + here] = dense_wide[matrix].astype(jnp.bfloat16)
        layer.head_bias[own] = refs["head_shard"][...]
        layer.dense_bias[own] = refs["dense_bias_shard"][...].reshape(1, layer.units)
        swap("head_bias", layer.head_bias)
        swap("dense_bias", layer.dense_bias)
        layer.sums[...] = jnp.zeros_like(layer.sums)
        segments = refs["segment_ids"][pl.ds(own, 1)].astype(jnp.float32)
        layer.segment_row[...] = segments
        layer.segment_column[...] = jnp.broadcast_to(segments, (8, layer.length)).T[:, 0:1]

    def turn_tokens():
        links["tokens"].wait()
        for core in range(2):
            layer.turn(layer.tokens.at[core], layer.token_turned.at[core])
        for name in ("head_bias", "dense_bias"):
            swaps[name].wait_recv()

    def project(matrix):
        program.need("a%d" % matrix)
        layer.project(matrix)

    def attend(group):
        loop(layer.pairs, lambda pair: layer.attend(group, pair))

    def branch():
        links["mixed"] = to_core(layer.mixed.at[other], layer.mixed_other)
        program.need("a3")
        for group in range(layer.groups):
            layer.add_branch(group)

    def norm_one():
        layer.norm_one()
        layer.turn(layer.hidden_low, layer.hidden_turned.at[own])
        swap("hidden", layer.hidden_turned)

    def expand(part):
        program.need("u%d" % part)
        layer.expand(part)
        if part == DENSE_PARTS - 1:
            links["activated"] = to_core(layer.activated.at[other], layer.activated_other)

    def down():
        program.need(*("d%d" % part for part in parts))
        for group in range(layer.groups):
            layer.add_down(group)

    def norm_two():
        links["cotangent"].wait()
        layer.norm_two()
        layer.turn(layer.back_low, layer.back_turned.at[own])
        swap("back", layer.back_turned)
        links["out"] = sender.start_local(layer.final, refs["out_rows"].at[own])
        swaps["out"] = to_core(layer.final, refs["out_rows"].at[own])

    def pre_other(part):
        if part == 0:
            sender.sent(links["activated"])
        layer.pre_gradient(other, part)
        if part == DENSE_PARTS - 1:
            links["pre"] = to_core(layer.activated.at[other], layer.pre_other)

    def pre_own(part):
        layer.pre_gradient(own, part)

    held = dict(zip(HELD, refs["held"]))

    def scatter(name, gradient, out):
        program.transfer(name, scatter_piece(place, sender, gradient, held[name], out, name in SQUARE_FIRST))

    def scatter_dense(name, matrix, part):
        gradient = layer.dense_grad.at[matrix, :, :, :, :, part_cols(part)]
        scatter(name, gradient, refs["dense_share"].at[matrix, :, part_cols(part)])

    def scatter_attention(matrix):
        out = refs["attention_share"].at[matrix]
        scatter("A%d" % matrix, layer.attention_grad.at[matrix], out)

    def down_gradient(part):
        if part == 0:
            links["activated"].wait_recv()
            swaps["back"].wait_recv()
        layer.down_gradient(part)
        scatter_dense("D%d" % part, 1, part)

    def up_gradient(part):
        if part == 0:
            links["pre"].wait_recv()
            swaps["hidden"].wait_recv()
        layer.up_gradient(part)
        scatter_dense("U%d" % part, 0, part)

    def norm_one_back():
        layer.norm_one_back()
        layer.turn(layer.back_low, layer.branch_turned.at[own])
        swap("branch", layer.branch_turned)

    def mix():
        sender.sent(links["pre"])
        for group in range(layer.groups):
            layer.mix_gradient(group)

    def out_gradient():
        links["mixed"].wait_recv()
        swaps["branch"].wait_recv()
        layer.out_gradient()
        scatter_attention(3)

    projected = []

    def attend_back(group):
        loop(layer.pairs, lambda pair: layer.attend_back(group, pair))
        if group is other:
            for matrix, ref in enumerate((layer.query_grad, layer.key_grad, layer.value_grad)):
                projected.append(to_core(ref.at[other], layer.projected_other[matrix]))

    def project_gradient(matrix):
        projected[matrix].wait_recv()
        layer.project_gradient(matrix)
        scatter_attention(matrix)

    def small_sums():
        layer.unit_totals()
        layer.head_sums()
        program.transfer("s", sum_small(place, sender, layer.sums, refs["slots"]))

    def input_gradient():
        layer.input_gradient()
        links["grad"] = sender.start_local(layer.wide, refs["grad_rows"].at[own])
        swaps["grad"] = to_core(layer.wide, refs["grad_rows"].at[own])

    def several(letter, act, count):
        for at in range(count):
            program.action(letter + str(at), functools.partial(act, at))

    program.action("start", start)
    program.action("turn", turn_tokens)
    several("q", project, 3)
    several("t", attend, layer.groups)
    program.action("branch", branch)
    program.action("n1", norm_one)
    several("e", expand, DENSE_PARTS)
    program.action("down", down)
    program.action("n2", norm_two)
    several("p", pre_other, DENSE_PARTS)
    several("g", down_gradient, DENSE_PARTS)
    several("r", pre_own, DENSE_PARTS)
    several("h", up_gradient, DENSE_PARTS)
    program.action("hidden", layer.add_hidden_gradient)
    program.action("n3", norm_one_back)
    program.action("mix", mix)
    program.action("out", out_gradient)
    program.action("x", functools.partial(attend_back, other))
    program.action("y", functools.partial(attend_back, own))
    several("z", project_gradient, 3)
    program.action("small", small_sums)
    program.action("input", input_gradient)
    for name in PLAN:
        program.run(name)
    program.finish()
    for name in ("out", "grad"):
        swaps[name].wait_recv()
        links[name].wait()
    sender.finish()


HELD = tuple("%s%d" % (letter, part) for letter in "DU" for part in range(DENSE_PARTS)) + ("A0", "A1", "A2", "A3")


def whole_step(tokens, segment_ids, cotangent, attention_master, dense_master, head_bias, dense_bias, small):
    _, length, width = tokens.shape
    groups = 2
    rows, cols = attention_master.shape[1:]
    units = dense_master.shape[2]
    pairs = groups * cols // PAIR
    low, wide = jnp.bfloat16, jnp.float32
    vmem, anywhere = pl.BlockSpec(memory_space=pltpu.VMEM), pl.BlockSpec(memory_space=pl.ANY)
    inputs = {
        "all_tokens": (tokens, anywhere),
        "segment_ids": (segment_ids, vmem),
        "cotangent": (cotangent, anywhere),
        "attention_master": (attention_master, anywhere),
        "dense_master": (dense_master, anywhere),
        "head_shard": (head_bias, vmem),
        "dense_bias_shard": (dense_bias, vmem),
        "small": (small, vmem),
    }
    outputs = {
        "out_rows": ((tokens.shape, low), anywhere),
        "grad_rows": ((tokens.shape, wide), anywhere),
        "attention_share": ((attention_master.shape, wide), vmem),
        "dense_share": ((dense_master.shape, wide), vmem),
        "sums": (((SMALL_ROWS, width), wide), vmem),
    }
    buffers = {
        "attention_weights": ((groups, 4, 4, 2, 2, rows, cols), low),
        "dense_weights": ((groups, 2, 4, 2, 2, rows, units), low),
        "head_bias": ((groups, 2, cols), wide),
        "dense_bias": ((groups, 1, units), wide),
        "attention_grad": ((4, 4, 2, 2, rows, cols), low),
        "dense_grad": ((2, 4, 2, 2, rows, units), low),
        "tokens": (tokens.shape, low),
        "token_turned": ((groups, width, length), low),
        "hidden_turned": ((groups, width, length), low),
        "back_turned": ((groups, width, length), low),
        "branch_turned": ((groups, width, length), low),
        "activated_other": ((length, units), low),
        "pre_other": ((length, units), low),
        "mixed_other": ((length, cols), low),
        "queries": ((pairs, length, PAIR), low),
        "keys": ((pairs, length, PAIR), low),
        "values": ((pairs, length, PAIR), low),
        "mixed": ((groups, length, cols), low),
        "log_totals": ((groups, pl.cdiv(cols // HEAD_DIM, 8) * 8, length), wide),
        "normed": ((length, width), wide),
        "inverse": ((length, 1), wide),
        "hidden_low": ((length, width), low),
        "activated": ((groups, length, units), low),
        "slope": ((groups, length, units), wide),
        "back_low": ((length, width), low),
        "wide": ((length, width), wide),
        "unit_sums": ((groups, units), wide),
        "segment_row": ((1, length), wide),
        "segment_column": ((length, 1), wide),
        "slots": ((2 * SMALL_HOPS, SMALL_ROWS, width), wide),
    }
    scratch = {name: pltpu.VMEM(*what) for name, what in buffers.items()}
    pieces = 4 + 2 * DENSE_PARTS
    copies = pieces * (GATHER_COPIES + SCATTER_COPIES) + SMALL_HOPS + 16
    scratch["send_sems"] = pltpu.SemaphoreType.DMA((copies,))
    scratch["recv_sems"] = pltpu.SemaphoreType.DMA((copies,))
    scratch["local_sems"] = pltpu.SemaphoreType.DMA((9,))
    held = [scatter_held(rows, cols if name[0] == "A" else units // DENSE_PARTS, name in SQUARE_FIRST) for name in HELD]
    scratch["held"] = held
    return pl.pallas_call(
        functools.partial(step_kernel, tuple(inputs) + tuple(outputs) + tuple(scratch)),
        name="whole_step",
        out_shape=tuple(jax.ShapeDtypeStruct(*what) for what, _ in outputs.values()),
        in_specs=[spec for _, spec in inputs.values()],
        out_specs=tuple(spec for _, spec in outputs.values()),
        scratch_shapes=list(scratch.values()),
        compiler_params=pltpu.CompilerParams(
            collective_id=0, has_side_effects=True, vmem_limit_bytes=63 * 2**20
        ),
    )(*(value for value, _ in inputs.values()))


def finish_kernel(inputs, outputs, *refs):
    count = len(inputs) + len(outputs)
    outside = dict(zip(inputs + outputs, refs))
    inside = dict(zip(inputs + outputs, refs[count:]))
    sems = refs[-1]
    for name in ("out_rows", "grad_rows"):
        inside[name + "_new"] = inside[name]
    loads, stores = {}, []
    for at, name in enumerate(inputs):
        loads[name] = pltpu.make_async_copy(outside[name], inside[name], sems.at[at])
        loads[name].start()

    def store(name):
        copy = pltpu.make_async_copy(inside[name], outside[name], sems.at[len(inputs) + outputs.index(name)])
        copy.start()
        stores.append(copy)

    def update(name, gradients, learn_rate, weight_decay, shape=None):
        for part in ("", "_first", "_second"):
            loads[name + part].wait()
        for index, gradient in gradients:
            parts = [inside[name + part][index] for part in ("", "_first", "_second")]
            if shape is not None:
                parts = [part.reshape(shape) for part in parts]
            results = adamw(parts[0], gradient, parts[1], parts[2], learn_rate, weight_decay)
            for part, value in zip(("_new", "_first_new", "_second_new"), results):
                inside[name + part][index] = value.reshape(inside[name][index].shape)
            if name + "_copy" in inside:
                inside[name + "_copy"][index] = results[0].astype(jnp.bfloat16)
        for part in ("_new", "_first_new", "_second_new", "_copy"):
            if name + part in inside:
                store(name + part)

    for name in ("out_rows", "grad_rows"):
        loads[name].wait()
        store(name + "_new")
    for name in ("attention", "dense"):
        loads[name + "_share"].wait()
        share = inside[name + "_share"]
        update(name, ((matrix, share[matrix]) for matrix in range(share.shape[0])), 0.03, 0.01)
    own = lax.axis_index("mp")
    loads["sums"].wait()
    sums = inside["sums"]
    cols, units = inside["head"].shape[1], inside["bias"].shape[0]
    update("small", ((slice(0, 6), sums[0:6]),), 0.2, 0.0)
    heads = sums[pl.ds(10 + own, 1)]
    update("head", ((slice(row, row + 1), heads[:, row * cols : (row + 1) * cols]) for row in range(2)), 0.2, 0.0)
    totals = [sums[pl.ds(6 + 2 * own + row, 1)] for row in range(2)]
    update("bias", ((slice(None), jnp.concatenate(totals, axis=1)),), 0.2, 0.0, (1, units))
    for copy in stores:
        copy.wait()


def finish_step(step_results, attention, dense, head, bias, small):
    inputs = dict(zip(("out_rows", "grad_rows", "attention_share", "dense_share", "sums"), step_results))
    outputs = {name + "_new": inputs[name] for name in ("out_rows", "grad_rows")}
    for name, state in (("attention", attention), ("dense", dense), ("head", head), ("bias", bias), ("small", small)):
        for part, value in zip(("", "_first", "_second"), state):
            inputs[name + part] = value
            outputs[name + part + "_new"] = value
        if name in ("attention", "dense"):
            outputs[name + "_copy"] = jax.ShapeDtypeStruct(state[0].shape, jnp.bfloat16)
    anywhere = pl.BlockSpec(memory_space=pl.ANY)
    scratch = [pltpu.VMEM(value.shape, value.dtype) for value in inputs.values()]
    for name, value in outputs.items():
        scratch.append(pltpu.VMEM((8, 128) if "rows" in name else value.shape, value.dtype))
    return pl.pallas_call(
        functools.partial(finish_kernel, tuple(inputs), tuple(outputs)),
        name="finish_step",
        out_shape=tuple(jax.ShapeDtypeStruct(value.shape, value.dtype) for value in outputs.values()),
        in_specs=[anywhere] * len(inputs),
        out_specs=(anywhere,) * len(outputs),
        scratch_shapes=scratch + [pltpu.SemaphoreType.DMA((len(inputs) + len(outputs),))],
        compiler_params=pltpu.CompilerParams(vmem_limit_bytes=62 * 2**20),
    )(*inputs.values())


def plain_gather(attention_low, dense_low):
    def both(shard):
        return lax.all_gather(lax.all_gather(shard, "dp", axis=1, tiled=True), "mp", axis=0)

    return both(attention_low), both(dense_low)


def plain_scatter(attention_gradient, dense_gradient, small):
    def share(gradient):
        half = lax.psum_scatter(gradient.astype(jnp.float32), "mp", scatter_dimension=0)
        return lax.psum_scatter(half, "dp", scatter_dimension=1, tiled=True)

    return share(attention_gradient), share(dense_gradient), lax.psum(small, ("dp", "mp"))


def plain_layer(row_tokens, segment_row, upstream, attention_full, dense_full, head_bias, dense_bias, small_vectors):
    groups = attention_full.shape[0]
    length = row_tokens.shape[0]
    local_cols = attention_full.shape[3]
    local_heads = local_cols // HEAD_DIM
    allowed = (segment_row[:, None] == segment_row[None, :])[None]
    saved = []
    branch = 0.0
    for group in range(groups):
        weights = attention_full[group]
        queries = (
            (jnp.dot(row_tokens, weights[0], preferred_element_type=jnp.float32) + head_bias[group, 0]) * 0.125
        ).astype(jnp.bfloat16)
        key_rows = jnp.dot(row_tokens, weights[1], preferred_element_type=jnp.float32).astype(jnp.bfloat16)
        value_rows = (
            jnp.dot(row_tokens, weights[2], preferred_element_type=jnp.float32) + head_bias[group, 1]
        ).astype(jnp.bfloat16)
        query_heads = queries.reshape(length, local_heads, HEAD_DIM)
        key_heads = key_rows.reshape(length, local_heads, HEAD_DIM)
        value_heads = value_rows.reshape(length, local_heads, HEAD_DIM)
        scores = masked_scores(query_heads, key_heads, allowed)
        row_peak = jnp.max(scores, axis=-1, keepdims=True)
        shifted_exp = jnp.exp(scores - row_peak)
        exp_total = jnp.sum(shifted_exp, axis=-1, keepdims=True)
        attend_low = (shifted_exp / exp_total).astype(jnp.bfloat16)
        log_total = row_peak + jnp.log(exp_total)
        mixed_heads = (
            jnp.einsum("hqk,khd->qhd", attend_low, value_heads, preferred_element_type=jnp.float32)
            .reshape(length, local_cols)
            .astype(jnp.bfloat16)
        )
        partial_value = lax.dot_general(mixed_heads, weights[3], last_dims, preferred_element_type=jnp.float32)
        branch = branch + partial_value.astype(jnp.bfloat16).astype(jnp.float32)
        saved.append((query_heads, key_heads, value_heads, log_total, mixed_heads))
    hidden, normed_one, inverse_one = norm_forward(
        row_tokens.astype(jnp.float32) + branch + small_vectors[0], small_vectors[2], small_vectors[3]
    )
    hidden_low = hidden.astype(jnp.bfloat16)
    down_out = 0.0
    dense_saved = []
    for group in range(groups):
        hidden_pre = (
            jnp.dot(hidden_low, dense_full[group, 0], preferred_element_type=jnp.float32) + dense_bias[group]
        )
        activated = gelu_value(hidden_pre).astype(jnp.bfloat16)
        down_partial = lax.dot_general(
            activated, dense_full[group, 1], last_dims, preferred_element_type=jnp.float32
        )
        down_out = down_out + down_partial.astype(jnp.bfloat16).astype(jnp.float32)
        dense_saved.append((hidden_pre, activated))
    final, normed_two, inverse_two = norm_forward(
        hidden + down_out + small_vectors[1], small_vectors[4], small_vectors[5]
    )
    back_two, gain_two, shift_two = norm_backward(upstream, normed_two, inverse_two, small_vectors[4])
    down_grad = back_two.astype(jnp.bfloat16)
    hidden_grad = back_two
    dense_grads, dense_bias_grads = [], []
    for group in range(groups):
        hidden_pre, activated = dense_saved[group]
        grad_down_weight = lax.dot_general(down_grad, activated, first_dims, preferred_element_type=jnp.float32)
        pre_grad = (
            jnp.dot(down_grad, dense_full[group, 1], preferred_element_type=jnp.float32) * gelu_slope(hidden_pre)
        ).astype(jnp.bfloat16)
        grad_up_weight = lax.dot_general(hidden_low, pre_grad, first_dims, preferred_element_type=jnp.float32)
        hidden_grad = hidden_grad + lax.dot_general(
            pre_grad, dense_full[group, 0], last_dims, preferred_element_type=jnp.float32
        )
        dense_grads.append(jnp.stack([grad_up_weight, grad_down_weight]))
        dense_bias_grads.append(jnp.sum(pre_grad.astype(jnp.float32), axis=0))
    back_one, gain_one, shift_one = norm_backward(hidden_grad, normed_one, inverse_one, small_vectors[2])
    small_grad = jnp.stack(
        [jnp.sum(back_one, axis=0), jnp.sum(back_two, axis=0), gain_one, shift_one, gain_two, shift_two]
    )
    branch_grad = back_one.astype(jnp.bfloat16)
    input_rows = back_one
    attention_grads, head_grads = [], []
    for group in range(groups):
        weights = attention_full[group]
        query_heads, key_heads, value_heads, log_total, mixed_heads = saved[group]
        grad_out_weight = lax.dot_general(branch_grad, mixed_heads, first_dims, preferred_element_type=jnp.float32)
        mixed_grad = (
            jnp.dot(branch_grad, weights[3], preferred_element_type=jnp.float32)
            .astype(jnp.bfloat16)
            .reshape(length, local_heads, HEAD_DIM)
        )
        attend = jnp.exp(masked_scores(query_heads, key_heads, allowed) - log_total)
        attend_low = attend.astype(jnp.bfloat16)
        prob_grad = jnp.einsum("qhd,khd->hqk", mixed_grad, value_heads, preferred_element_type=jnp.float32)
        value_grad = jnp.einsum(
            "hqk,qhd->khd", attend_low, mixed_grad, preferred_element_type=jnp.float32
        ).astype(jnp.bfloat16)
        inner_total = jnp.sum(attend * prob_grad, axis=-1, keepdims=True)
        score_grad = (attend * (prob_grad - inner_total)).astype(jnp.bfloat16)
        query_grad = (
            jnp.einsum("hqk,khd->qhd", score_grad, key_heads, preferred_element_type=jnp.float32).astype(jnp.bfloat16)
            * 0.125
        )
        key_grad = jnp.einsum(
            "hqk,qhd->khd", score_grad, query_heads, preferred_element_type=jnp.float32
        ).astype(jnp.bfloat16)
        stacked = [each.reshape(length, local_cols) for each in (query_grad, key_grad, value_grad)]
        grads = [
            lax.dot_general(row_tokens, each, first_dims, preferred_element_type=jnp.float32) for each in stacked
        ]
        for each, weight in zip(stacked, weights[:3]):
            input_rows = input_rows + lax.dot_general(each, weight, last_dims, preferred_element_type=jnp.float32)
        attention_grads.append(jnp.stack(grads + [grad_out_weight]))
        head_grads.append(
            jnp.stack(
                [jnp.sum(stacked[0].astype(jnp.float32), axis=0), jnp.sum(stacked[2].astype(jnp.float32), axis=0)]
            )
        )
    return (
        final.astype(jnp.bfloat16),
        input_rows,
        jnp.stack(attention_grads).astype(jnp.bfloat16),
        jnp.stack(dense_grads).astype(jnp.bfloat16),
        jnp.stack(head_grads),
        jnp.stack(dense_bias_grads),
        small_grad,
    )


def plain_step(tokens, segment_ids, cotangent, attention_master, dense_master, head_bias, dense_bias, small_vectors):
    attention_full, dense_full = plain_gather(attention_master.astype(jnp.bfloat16), dense_master.astype(jnp.bfloat16))
    head_full = lax.all_gather(head_bias, "mp", axis=0)
    dense_bias_full = lax.all_gather(dense_bias, "mp", axis=0)
    mine = lax.axis_index("mp")
    row_tokens = lax.dynamic_index_in_dim(tokens, mine, 0, keepdims=False)
    segment_row = lax.dynamic_index_in_dim(segment_ids, mine, 0, keepdims=False)
    upstream = lax.dynamic_index_in_dim(cotangent, mine, 0, keepdims=False).astype(jnp.float32)
    final, input_rows, attention_grad, dense_grad, head_grad, dense_bias_grad, small_grad = plain_layer(
        row_tokens, segment_row, upstream, attention_full, dense_full, head_full, dense_bias_full, small_vectors
    )
    width = tokens.shape[2]
    sums = jnp.concatenate([part.reshape(-1, width) for part in (small_grad, dense_bias_grad, head_grad)])
    attention_share, dense_share, sums = plain_scatter(attention_grad, dense_grad, sums)
    out_rows, grad_rows = (lax.all_gather(rows, "mp", axis=0) for rows in (final, input_rows))
    return out_rows, grad_rows, attention_share, dense_share, sums


def make_local(mesh):
    n_dp, n_mp = mesh.shape["dp"], mesh.shape["mp"]
    square = n_dp == 16 and n_mp == 2

    def local(
        tokens,
        segment_ids,
        cotangent,
        attention_master,
        attention_first,
        attention_second,
        dense_master,
        dense_first,
        dense_second,
        head_bias,
        head_bias_first,
        head_bias_second,
        dense_bias,
        dense_bias_first,
        dense_bias_second,
        small_vectors,
        small_first,
        small_second,
    ):
        states = (
            (attention_master, attention_first, attention_second),
            (dense_master, dense_first, dense_second),
            (head_bias, head_bias_first, head_bias_second),
            (dense_bias, dense_bias_first, dense_bias_second),
            (small_vectors, small_first, small_second),
        )
        step = whole_step if square else plain_step
        results = step(
            tokens, segment_ids, cotangent, attention_master, dense_master, head_bias, dense_bias, small_vectors
        )
        if square:
            return finish_step(results, *states)
        out_rows, grad_rows, attention_share, dense_share, sums = results
        mine = lax.axis_index("mp")
        width, cols, units = tokens.shape[2], head_bias.shape[1], dense_bias.shape[0]
        small_sum = sums[:6]
        dense_bias_sum = lax.dynamic_slice(sums, (6 + 2 * mine, 0), (2, width)).reshape(units)
        head_sum = lax.dynamic_slice(sums, (10 + mine, 0), (1, width)).reshape(2, cols)
        attention_new = adamw(attention_master, attention_share, attention_first, attention_second, 0.03, 0.01)
        dense_new = adamw(dense_master, dense_share, dense_first, dense_second, 0.03, 0.01)
        head_new = adamw(head_bias, head_sum, head_bias_first, head_bias_second, 0.2, 0.0)
        dbias_new = adamw(dense_bias, dense_bias_sum, dense_bias_first, dense_bias_second, 0.2, 0.0)
        small_new = adamw(small_vectors, small_sum, small_first, small_second, 0.2, 0.0)
        return (
            out_rows,
            grad_rows,
            *attention_new,
            attention_new[0].astype(jnp.bfloat16),
            *dense_new,
            dense_new[0].astype(jnp.bfloat16),
            *head_new,
            *dbias_new,
            *small_new,
        )

    return local


def solution(mesh):
    rows, matrix, halves, units = P("dp", None, None), P(None, "dp", "mp"), P(None, "mp"), P("mp")
    return jax.shard_map(
        make_local(mesh),
        mesh=mesh,
        in_specs=(rows, P("dp", None), rows) + (matrix,) * 6 + (halves,) * 3 + (units,) * 3 + (P(),) * 3,
        out_specs=(rows,) * 2 + (matrix,) * 8 + (halves,) * 3 + (units,) * 3 + (P(),) * 3,
        check_vma=False,
    )
```

```python
import functools
import types

import jax
import jax.numpy as jnp
from jax import lax
from jax.experimental import pallas as pl
from jax.experimental.pallas import tpu as pltpu
from jax.sharding import PartitionSpec as P

HEAD_DIM = 64
PAIR = 2 * HEAD_DIM
STEP = 5
MESH_ID = pl.DeviceIdType.MESH

first_dims = (((0,), (0,)), ((), ()))
last_dims = (((1,), (1,)), ((), ()))


def norm_forward(row_values, gain_row, shift_row):
    center = row_values - jnp.mean(row_values, axis=-1, keepdims=True)
    inverse = lax.rsqrt(jnp.mean(center * center, axis=-1, keepdims=True) + 1e-06)
    normed = center * inverse
    return (normed * gain_row + shift_row, normed, inverse)


def norm_backward(upstream, normed, inverse, gain_row):
    scaled = upstream * gain_row
    back_rows = inverse * (
        scaled
        - jnp.mean(scaled, axis=-1, keepdims=True)
        - normed * jnp.mean(scaled * normed, axis=-1, keepdims=True)
    )
    return (back_rows, jnp.sum(upstream * normed, axis=0), jnp.sum(upstream, axis=0))


def gelu_value(hidden_pre):
    return 0.5 * hidden_pre * (1.0 + lax.erf(hidden_pre * 0.7071067811865476))


def gelu_slope(hidden_pre):
    return (
        0.5 * (1.0 + lax.erf(hidden_pre * 0.7071067811865476))
        + hidden_pre * jnp.exp(-0.5 * hidden_pre * hidden_pre) * 0.3989422804014327
    )


def masked_scores(queries, key_rows, allowed):
    scores = jnp.einsum("qhd,khd->hqk", queries, key_rows, preferred_element_type=jnp.float32)
    return jnp.where(allowed, scores, -1000000000.0)


def adamw(parameter, gradient, moment_one, moment_two, learn_rate, weight_decay):
    first_new = 0.5 * moment_one + 0.5 * gradient
    second_new = 0.5 * moment_two + 0.5 * gradient * gradient
    correction = 1.0 - jnp.power(jnp.float32(0.5), jnp.float32(STEP))
    update = first_new / correction / (jnp.sqrt(second_new / correction) + 1e-08)
    return (
        parameter - learn_rate * update - learn_rate * weight_decay * parameter,
        first_new,
        second_new,
    )


def dot(left, right):
    return jnp.dot(left, right, preferred_element_type=jnp.float32)


def dot_last(left, right):
    return lax.dot_general(left, right, last_dims, preferred_element_type=jnp.float32)


def aligned(at, count):
    return pl.ds(pl.multiple_of(at * count, count), count)


def fold(values):
    return jnp.sum(values.reshape(values.shape[0] // 8, 8, values.shape[1]), axis=0)


def loop(count, body):
    def step(at, carry):
        body(at)
        return carry

    lax.fori_loop(0, count, step, 0)


class Place:
    def __init__(self):
        self.dp = lax.axis_index("dp")
        self.mp = lax.axis_index("mp")
        self.x = self.dp % 2
        self.y = (self.dp // 2) % 2
        self.z = self.dp // 4
        self.z_low = self.z % 2
        self.z_high = self.z // 2
        on_x = self.dp + 1 - 2 * self.x
        on_y = self.dp + 2 - 4 * self.y
        self.near_x = (on_x, self.mp)
        self.near_y = (on_y, self.mp)
        self.near_z = (self.dp + 4 - 8 * self.z_low, self.mp)
        self.opposite_z = (self.dp + 12 - 8 * self.z, self.mp)
        self.inner = (self.z_low + self.z_high) == 1
        self.core = (self.dp, 1 - self.mp)
        self.one = (on_x + (on_y - on_x) * self.mp, self.mp)
        self.two = (on_y + (on_x - on_y) * self.mp, self.mp)
        self.one_at = (self.y + (1 - 2 * self.y) * self.mp, self.x + (1 - 2 * self.x) * (1 - self.mp))
        self.two_at = (self.y + (1 - 2 * self.y) * (1 - self.mp), self.x + (1 - 2 * self.x) * self.mp)
        self.own_at = (self.y, self.x)
        self.cross_at = (1 - self.y, 1 - self.x)
        self.near_at = 2 * self.z_high + 1 - self.z_low
        self.these, self.those = pl.ds(2 * self.z_high, 2), pl.ds(2 - 2 * self.z_high, 2)

    def greet(self):
        barrier = pltpu.get_barrier_semaphore()
        partners = (self.near_x, self.near_y, self.near_z, self.opposite_z, self.core)
        for partner in partners:
            pl.semaphore_signal(barrier, inc=1, device_id=partner, device_id_type=MESH_ID)
        pl.semaphore_wait(barrier, len(partners))


class Sender:
    def __init__(self, send_sems, recv_sems, local_sems):
        self.send_sems, self.recv_sems, self.local_sems = send_sems, recv_sems, local_sems
        self.used, self.used_local, self.open = 0, 0, []

    def plan(self, source, target, device, only=None):
        copy = pltpu.make_async_remote_copy(
            src_ref=source,
            dst_ref=target,
            send_sem=self.send_sems.at[self.used],
            recv_sem=self.recv_sems.at[self.used],
            device_id=device,
            device_id_type=MESH_ID,
        )
        self.used += 1
        self.open.append((copy, only))
        return copy

    def start(self, source, target, device):
        copy = self.plan(source, target, device)
        copy.start()
        return copy

    def start_local(self, source, target):
        copy = pltpu.make_async_copy(source, target, self.local_sems.at[self.used_local])
        self.used_local += 1
        copy.start()
        return copy

    def sent(self, copy):
        self.open = [each for each in self.open if each[0] is not copy]
        copy.wait_send()

    def finish(self):
        for copy, only in self.open:
            if only is None:
                copy.wait_send()
            else:
                pl.when(only)(copy.wait_send)


class Program:
    def __init__(self):
        self.actions, self.transfers, self.done = {}, {}, set()

    def action(self, name, act):
        self.actions[name] = act

    def transfer(self, name, stages):
        self.transfers[name] = stages

    def run(self, name):
        if name in self.actions:
            self.actions.pop(name)()
        elif name in self.transfers and name not in self.done:
            try:
                next(self.transfers[name])
            except StopIteration:
                self.done.add(name)

    def need(self, *names):
        for name in names:
            while name not in self.done:
                self.run(name)

    def finish(self):
        for name in list(self.actions):
            self.run(name)
        self.need(*self.transfers)


def spread_square(place, sender, at, cores):
    own, first, second, last = (at(*where) for where in (place.own_at, place.one_at, place.two_at, place.cross_at))
    to_one = sender.start(own, own, place.one)
    to_two = sender.start(own, own, place.two)
    if cores is not None:
        cores.append(sender.start(own, own, place.core))
    yield
    to_one.wait_recv()
    cross = sender.start(first, first, place.two)
    if cores is not None:
        cores.append(sender.start(first, first, place.core))
    yield
    to_two.wait_recv()
    if cores is not None:
        cores.append(sender.start(second, second, place.core))
    yield
    cross.wait_recv()
    if cores is not None:
        cores.append(sender.start(last, last, place.core))


def spread_line(place, sender, at, cores):
    own = at(place.z)
    near = sender.start(own, own, place.near_z)
    yield
    near.wait_recv()
    these, those = at(place.these), at(place.those)
    across = sender.plan(these, these, place.opposite_z, place.inner)
    onward = sender.plan(those, those, place.near_z, place.inner)
    pl.when(place.inner)(across.start)
    if cores is not None:
        cores.append(sender.start(these, these, place.core))
    yield

    @pl.when(place.inner)
    def _():
        across.wait_recv()
        onward.start()

    yield
    pl.when(jnp.logical_not(place.inner))(onward.wait_recv)
    if cores is not None:
        cores.append(sender.start(those, those, place.core))


def gather_piece(place, sender, target, line_first):
    z, (y, x) = place.z, place.own_at
    cores = []
    if line_first:
        yield from spread_line(place, sender, lambda at: target.at[at, y, x], None)
        yield from spread_square(place, sender, lambda *at: target.at[:, at[0], at[1]], cores)
    else:
        yield from spread_square(place, sender, lambda *at: target.at[z, at[0], at[1]], None)
        yield from spread_line(place, sender, lambda at: target.at[at], cores)
    yield
    for copy in cores:
        copy.wait_recv()


GATHER_COPIES = 10


def add_blocks(out, *others):
    lead = out.shape[:-2]
    count = 1
    for size in lead:
        count *= size

    def body(at):
        index = []
        for size in lead[::-1]:
            index.insert(0, at % size)
            at = at // size
        index = tuple(index)
        total = others[0][index].astype(jnp.float32)
        for other in others[1:]:
            total = total + other[index].astype(jnp.float32)
        out[index] = total.astype(out.dtype)

    if lead:
        loop(count, body)
    else:
        total = others[0][...].astype(jnp.float32)
        for other in others[1:]:
            total = total + other[...].astype(jnp.float32)
        out[...] = total.astype(out.dtype)


def reduce_square(place, sender, at, held, out):
    from_cross, from_one, from_two = held
    own, first, second, last = (at(*where) for where in (place.own_at, place.one_at, place.two_at, place.cross_at))
    cross = sender.start(last, from_cross, place.two)
    straight = sender.start(second, from_two, place.two)
    yield
    cross.wait_recv()
    add_blocks(first, first, from_cross)
    turned = sender.start(first, from_one, place.one)
    yield
    straight.wait_recv()
    turned.wait_recv()
    add_blocks(own if out is None else out, own, from_one, from_two)


def reduce_line(place, sender, at, held, out):
    from_end, from_across, from_near = held
    these, those = at(place.these), at(place.those)
    outer = jnp.logical_not(place.inner)
    inward = sender.plan(those, from_end, place.near_z, outer)
    across = sender.plan(those, from_across, place.opposite_z, place.inner)
    pl.when(outer)(inward.start)
    yield

    @pl.when(place.inner)
    def _():
        inward.wait_recv()
        add_blocks(those, those, from_end)
        across.start()

    yield

    @pl.when(place.inner)
    def _():
        across.wait_recv()
        add_blocks(these, these, from_across)

    near = sender.start(at(place.near_at), from_near, place.near_z)
    yield
    near.wait_recv()
    own = at(place.z)
    add_blocks(own if out is None else out, own, from_near)


def scatter_piece(place, sender, gradient, held, out, line_first):
    z, (y, x) = place.z, place.own_at
    if line_first:
        yield from reduce_line(place, sender, lambda at: gradient.at[at], held[3:], None)
        yield from reduce_square(place, sender, lambda *at: gradient.at[z, at[0], at[1]], held[:3], out)
    else:
        yield from reduce_square(place, sender, lambda *at: gradient.at[:, at[0], at[1]], held[:3], None)
        yield from reduce_line(place, sender, lambda at: gradient.at[at, y, x], held[3:], out)


SCATTER_COPIES = 6


def scatter_held(rows, cols, line_first):
    leads = ((),) * 3 + ((2, 2, 2), (2, 2, 2), (2, 2)) if line_first else ((4,),) * 3 + ((2,), (2,), ())
    return [pltpu.VMEM(lead + (rows, cols), jnp.bfloat16) for lead in leads]


def sum_small(place, sender, total, slots):
    for at, partner in enumerate((place.core, place.near_x, place.near_y, place.near_z, place.opposite_z)):
        slots[2 * at] = total[...]
        copy = sender.start(slots.at[2 * at], slots.at[2 * at + 1], partner)
        yield
        copy.wait_recv()
        total[...] = slots[2 * at] + slots[2 * at + 1]


SMALL_HOPS = 5
SMALL_ROWS = 16
DENSE_PARTS = 3
STEP_COLS = 256


SQUARE_FIRST = ("u0", "d0", "D1", "U1")


class Layer:
    NORM_ROWS = 128

    def __init__(self, own, refs):
        self.__dict__.update(refs)
        self.own, self.other = own, 1 - own
        self.length, self.width = self.wide.shape
        self.groups = self.dense_weights.shape[0]
        self.cols = self.attention_weights.shape[-1]
        self.units = self.dense_weights.shape[-1]
        self.pairs = self.cols // PAIR
        views = [self.activated.at[:, :, at * self.cols : (at + 1) * self.cols] for at in range(4)]
        self.query_grad, self.key_grad, self.value_grad, self.mixed_grad = views
        self.projected_other = [self.pre_other.at[:, at * self.cols : (at + 1) * self.cols] for at in range(3)]
        self.final = self.tokens.at[self.other]

    def weight(self, ref, group, matrix, cols=None):
        value = ref[group, matrix] if cols is None else ref[group, matrix, ..., cols]
        return value.reshape(self.width, value.shape[-1])

    def weight_rows(self, ref, group, matrix, rows):
        return ref[group, matrix].reshape(self.width, ref.shape[-1])[rows]

    def put_gradient(self, ref, matrix, cols, value):
        ref[matrix, ..., cols] = value.astype(jnp.bfloat16).reshape(ref.shape[1:-1] + (value.shape[-1],))

    def steps(self, part, body):
        size = self.units // DENSE_PARTS
        step = min(STEP_COLS, size)
        loop(size // step, lambda at: body(pl.ds(pl.multiple_of(part * size + at * step, step), step)))


    def project(self, matrix):
        out = (self.queries, self.keys, self.values)[matrix]
        for group in range(self.groups):
            value = dot(self.tokens[self.own], self.weight(self.attention_weights, group, matrix))
            if matrix == 0:
                value = (value + self.head_bias[group, 0:1]) * 0.125
            elif matrix == 2:
                value = value + self.head_bias[group, 1:2]
            value = value.astype(jnp.bfloat16)
            for pair in range(self.pairs):
                out[group * self.pairs + pair] = value[:, pair * PAIR : (pair + 1) * PAIR]

    def attend(self, group, pair):
        at = group * self.pairs + pair
        cols = aligned(pair, PAIR)
        queries, keys, value_turned = self.queries[at], self.keys[at], self.values[at].T
        first = lax.broadcasted_iota(jnp.int32, queries.shape, 1) < HEAD_DIM
        allowed = self.segment_column[...] == self.segment_row[...]
        mixed = []
        for side in range(2):
            mine = jnp.where(first if side == 0 else ~first, queries, jnp.bfloat16(0))
            scores = jnp.where(allowed, dot_last(keys, mine), -1000000000.0)
            peak = jnp.max(scores, axis=0, keepdims=True)
            shifted = jnp.exp(scores - peak)
            total = jnp.sum(shifted, axis=0, keepdims=True)
            attend_low = (shifted * (1.0 / total)).astype(jnp.bfloat16)
            mixed.append(dot(value_turned[side * HEAD_DIM : (side + 1) * HEAD_DIM], attend_low))
            self.log_totals[group, pl.ds(2 * pair + side, 1)] = peak + jnp.log(total)
        self.mixed[group, :, cols] = jnp.concatenate(mixed, axis=0).T.astype(jnp.bfloat16)

    def add_branch(self, group):
        for start in range(0, self.width, STEP_COLS):
            cols = slice(start, start + STEP_COLS)
            part = dot_last(self.mixed[group], self.weight_rows(self.attention_weights, group, 3, cols))
            part = part.astype(jnp.bfloat16).astype(jnp.float32)
            self.wide[:, cols] = part if group == 0 else self.wide[:, cols] + part

    def norm_one(self):
        out_bias, gain, shift = self.small[0:1], self.small[2:3], self.small[3:4]

        def chunk(block):
            rows = aligned(block, self.NORM_ROWS)
            values = self.tokens[self.own, rows].astype(jnp.float32) + self.wide[rows] + out_bias
            center = values - jnp.mean(values, axis=-1, keepdims=True)
            inverse = lax.rsqrt(jnp.mean(center * center, axis=-1, keepdims=True) + 1e-06)
            normed = center * inverse
            self.normed[rows] = normed
            self.inverse[rows] = inverse
            self.hidden_low[rows] = (normed * gain + shift).astype(jnp.bfloat16)

        loop(self.length // self.NORM_ROWS, chunk)

    def expand(self, part):
        def body(cols):
            for group in range(self.groups):
                pre = dot(self.hidden_low[...], self.weight(self.dense_weights, group, 0, cols))
                pre = pre + self.dense_bias[group, :, cols]
                half = 0.5 * (1.0 + lax.erf(pre * 0.7071067811865476))
                self.activated[group, :, cols] = (pre * half).astype(jnp.bfloat16)
                self.slope[group, :, cols] = half + pre * jnp.exp(-0.5 * pre * pre) * 0.3989422804014327

        self.steps(part, body)

    def add_down(self, group):
        for start in range(0, self.width, STEP_COLS):
            cols = slice(start, start + STEP_COLS)
            part = dot_last(self.activated[group], self.weight_rows(self.dense_weights, group, 1, cols))
            part = part.astype(jnp.bfloat16).astype(jnp.float32)
            self.wide[:, cols] = part if group == 0 else self.wide[:, cols] + part

    def norm_two(self):
        down_bias, gain, shift = self.small[1:2], self.small[4:5], self.small[5:6]
        gain_one, shift_one = self.small[2:3], self.small[3:4]

        def chunk(block, sums):
            rows = aligned(block, self.NORM_ROWS)
            hidden = self.normed[rows] * gain_one + shift_one
            values = hidden + self.wide[rows] + down_bias
            center = values - jnp.mean(values, axis=-1, keepdims=True)
            inverse = lax.rsqrt(jnp.mean(center * center, axis=-1, keepdims=True) + 1e-06)
            normed = center * inverse
            self.final[rows] = (normed * gain + shift).astype(jnp.bfloat16)
            upstream = self.back_low[rows].astype(jnp.float32)
            scaled = upstream * gain
            back = inverse * (
                scaled
                - jnp.mean(scaled, axis=-1, keepdims=True)
                - normed * jnp.mean(scaled * normed, axis=-1, keepdims=True)
            )
            self.wide[rows] = back
            self.back_low[rows] = back.astype(jnp.bfloat16)
            return (sums[0] + fold(back), sums[1] + fold(upstream * normed), sums[2] + fold(upstream))

        self.norm_sums(chunk, (1, 4, 5))

    def norm_sums(self, chunk, places):
        zero = jnp.zeros((8, self.width), jnp.float32)
        sums = lax.fori_loop(0, self.length // self.NORM_ROWS, chunk, (zero, zero, zero))
        for row, total in zip(places, sums):
            self.sums[row : row + 1] = jnp.sum(total, axis=0, keepdims=True)


    def turn(self, source, target):
        step = 128
        for start in range(0, self.length, step):
            target[:, start : start + step] = source[start : start + step].T

    def both(self, turned, own, other):
        return dot(turned[self.own], own) + dot(turned[self.other], other)

    def down_gradient(self, part):
        def body(cols):
            value = self.both(self.back_turned, self.activated[self.own, :, cols], self.activated_other[:, cols])
            self.put_gradient(self.dense_grad, 1, cols, value)

        self.steps(part, body)

    def pre_gradient(self, group, part):
        def body(cols):
            grad = dot(self.back_low[...], self.weight(self.dense_weights, group, 1, cols)) * self.slope[group, :, cols]
            grad = grad.astype(jnp.bfloat16)
            self.activated[group, :, cols] = grad
            self.unit_sums[pl.ds(group, 1), cols] = jnp.sum(fold(grad.astype(jnp.float32)), axis=0, keepdims=True)

        self.steps(part, body)

    def up_gradient(self, part):
        def body(cols):
            value = self.both(self.hidden_turned, self.activated[self.own, :, cols], self.pre_other[:, cols])
            self.put_gradient(self.dense_grad, 0, cols, value)

        self.steps(part, body)

    def add_hidden_gradient(self):
        for start in range(0, self.width, STEP_COLS):
            cols = slice(start, start + STEP_COLS)
            total = self.wide[:, cols]
            for group in range(self.groups):
                total = total + dot_last(self.activated[group], self.weight_rows(self.dense_weights, group, 0, cols))
            self.wide[:, cols] = total

    def norm_one_back(self):
        gain = self.small[2:3]

        def chunk(block, sums):
            rows = aligned(block, self.NORM_ROWS)
            upstream, normed = self.wide[rows], self.normed[rows]
            scaled = upstream * gain
            back = self.inverse[rows] * (
                scaled
                - jnp.mean(scaled, axis=-1, keepdims=True)
                - normed * jnp.mean(scaled * normed, axis=-1, keepdims=True)
            )
            self.wide[rows] = back
            self.back_low[rows] = back.astype(jnp.bfloat16)
            return (sums[0] + fold(back), sums[1] + fold(upstream * normed), sums[2] + fold(upstream))

        self.norm_sums(chunk, (0, 2, 3))

    def out_gradient(self):
        value = self.both(self.branch_turned, self.mixed[self.own], self.mixed_other[...])
        self.put_gradient(self.attention_grad, 3, slice(0, self.cols), value)

    def mix_gradient(self, group):
        grad = dot(self.back_low[...], self.weight(self.attention_weights, group, 3)).astype(jnp.bfloat16)
        self.mixed_grad[group] = grad

    def attend_back(self, group, pair):
        at = group * self.pairs + pair
        cols = aligned(pair, PAIR)
        queries, keys, values = self.queries[at], self.keys[at], self.values[at]
        mixed_grad, key_turned = self.mixed_grad[group, :, cols], keys.T
        first = lax.broadcasted_iota(jnp.int32, queries.shape, 1) < HEAD_DIM
        allowed = self.segment_column[...] == self.segment_row[...]
        query_grads, key_grads, value_grads = [], [], []
        for side in range(2):
            here = first if side == 0 else ~first
            scores = dot_last(keys, jnp.where(here, queries, jnp.bfloat16(0)))
            prob_grad = dot_last(values, jnp.where(here, mixed_grad, jnp.bfloat16(0)))
            total = self.log_totals[group, pl.ds(2 * pair + side, 1)]
            attend = jnp.exp(jnp.where(allowed, scores, -1000000000.0) - total)
            inner = jnp.sum(attend * prob_grad, axis=0, keepdims=True)
            score_grad = (attend * (prob_grad - inner)).astype(jnp.bfloat16)
            value_grads.append(dot(attend.astype(jnp.bfloat16), mixed_grad))
            key_grads.append(dot(score_grad, queries))
            query_grads.append(dot(key_turned[side * HEAD_DIM : (side + 1) * HEAD_DIM], score_grad))
        self.value_grad[group, :, cols] = jnp.where(first, *value_grads).astype(jnp.bfloat16)
        self.key_grad[group, :, cols] = jnp.where(first, *key_grads).astype(jnp.bfloat16)
        grad = jnp.concatenate(query_grads, axis=0).T.astype(jnp.bfloat16)
        self.query_grad[group, :, cols] = grad * jnp.bfloat16(0.125)

    def project_gradient(self, matrix):
        ref = (self.query_grad, self.key_grad, self.value_grad)[matrix]
        value = self.both(self.token_turned, ref[self.own], self.projected_other[matrix][...])
        self.put_gradient(self.attention_grad, matrix, slice(0, self.cols), value)

    def head_sums(self):
        for group in range(self.groups):
            for at, ref in enumerate((self.query_grad, self.value_grad)):
                total = jnp.sum(fold(ref[group].astype(jnp.float32)), axis=0, keepdims=True)
                self.sums[10 + group : 11 + group, at * self.cols : (at + 1) * self.cols] = total

    def unit_totals(self):
        for group in range(self.groups):
            for half in range(2):
                row, start = 6 + 2 * group + half, half * self.width
                self.sums[row : row + 1] = self.unit_sums[group : group + 1, start : start + self.width]

    def input_gradient(self):
        for start in range(0, self.width, STEP_COLS):
            cols = slice(start, start + STEP_COLS)
            total = self.wide[:, cols]
            for group in range(self.groups):
                for matrix, ref in enumerate((self.query_grad, self.key_grad, self.value_grad)):
                    weight = self.weight_rows(self.attention_weights, group, matrix, cols)
                    total = total + dot_last(ref[group], weight)
            self.wide[:, cols] = total


STEPS = (
    "a1", "start", "a0", "u0", "a2", "a3", "d0", "d1", "u2", "u1", "d2", "turn", "q0", "q1", "q2", "t0", "t1",
    "branch", "n1", "e0", "e1", "e2", "down", "n2", "p0", "p1", "p2", "g0", "D0", "g1", "g2", "D1", "r0", "r1", "D2",
    "r2", "h0", "h1", "h2", "U1", "U0", "hidden", "n3", "mix", "out", "U2", "x", "A3", "y", "z0", "A0", "z1", "z2",
    "small", "A2", "A1", "s", "input",
)
PLAN = (
    0, 1, 2, 3, 0, 4, 5, 6, 3, 7, 2, 0, 8, 4, 6, 0, 9, 2, 6, 7, 10, 5, 8, 4, 3, 2, 3, 0, 5, 11, 9, 8, 4, 3, 2, 5, 2,
    9, 4, 0, 2, 10, 0, 6, 2, 8, 0, 7, 4, 4, 6, 5, 9, 3, 4, 12, 13, 14, 10, 5, 8, 15, 7, 5, 9, 16, 8, 6, 10, 3, 8, 9,
    5, 17, 7, 9, 3, 7, 18, 8, 9, 10, 6, 19, 20, 10, 7, 10, 6, 21, 7, 10, 22, 23, 24, 25, 26, 27, 28, 29, 30, 31, 32,
    33, 34, 35, 36, 37, 28, 38, 39, 34, 40, 41, 42, 31, 43, 44, 45, 46, 28, 39, 40, 47, 31, 28, 45, 48, 49, 47, 40,
    50, 51, 40, 52, 34, 31, 39, 53, 50, 47, 54, 34, 55, 56, 40, 45, 47, 56, 50, 57, 54, 47, 34, 45, 55, 40, 45, 28,
    54, 31, 56, 50, 55, 54, 39, 45, 56, 55, 28, 31, 39, 54, 50, 56, 34, 55, 39, 50, 54, 56, 47, 55,
)


def step_kernel(names, *refs):
    refs = types.SimpleNamespace(**dict(zip(names, refs)))
    place = Place()
    layer = Layer(place.mp, vars(refs))
    own, other = layer.own, layer.other
    sender = Sender(refs.send_sems, refs.recv_sems, refs.local_sems)
    program = Program()
    size = layer.units // DENSE_PARTS
    rows = refs.attention_master.shape[1]
    parts = range(DENSE_PARTS)
    links, swaps = {}, {}

    def part_cols(part):
        return slice(part * size, (part + 1) * size)

    def to_core(source, target):
        return sender.start(source, target, place.core)

    def swap(name, ref):
        swaps[name] = to_core(ref.at[own], ref.at[own])

    dense_wide = layer.slope.at[:, 0:rows]
    attention_wide = [layer.slope.at[0, 2 * rows : 3 * rows, at * layer.cols : (at + 1) * layer.cols] for at in range(4)]
    masters = [sender.start_local(refs.attention_master.at[at], ref) for at, ref in enumerate(attention_wide)]
    masters.append(sender.start_local(refs.dense_master, dense_wide))
    links["tokens"] = sender.start_local(refs.all_tokens, layer.tokens)
    links["cotangent"] = sender.start_local(refs.cotangent.at[own], layer.back_low)
    here = (place.z, place.y, place.x)
    for matrix in range(4):
        masters[matrix].wait()
        layer.attention_weights[(own, matrix) + here] = attention_wide[matrix][...].astype(jnp.bfloat16)
    place.greet()
    for matrix in range(4):
        target = layer.attention_weights.at[own, matrix]
        program.transfer("a%d" % matrix, gather_piece(place, sender, target, True))
    for matrix, letter in enumerate("ud"):
        for part in parts:
            target = layer.dense_weights.at[own, matrix, :, :, :, :, part_cols(part)]
            name = letter + str(part)
            program.transfer(name, gather_piece(place, sender, target, name not in SQUARE_FIRST))

    def start():
        masters[4].wait()
        for matrix in range(2):
            layer.dense_weights[(own, matrix) + here] = dense_wide[matrix].astype(jnp.bfloat16)
        layer.head_bias[own] = refs.head_shard[...]
        layer.dense_bias[own] = refs.dense_bias_shard[...].reshape(1, layer.units)
        swap("head_bias", layer.head_bias)
        swap("dense_bias", layer.dense_bias)
        layer.sums[...] = jnp.zeros_like(layer.sums)
        segments = refs.segment_ids[pl.ds(own, 1)].astype(jnp.float32)
        layer.segment_row[...] = segments
        layer.segment_column[...] = jnp.broadcast_to(segments, (8, layer.length)).T[:, 0:1]

    def turn_tokens():
        links["tokens"].wait()
        for core in range(2):
            layer.turn(layer.tokens.at[core], layer.token_turned.at[core])
        for name in ("head_bias", "dense_bias"):
            swaps[name].wait_recv()

    def project(matrix):
        program.need("a%d" % matrix)
        layer.project(matrix)

    def attend(group):
        loop(layer.pairs, lambda pair: layer.attend(group, pair))

    def branch():
        links["mixed"] = to_core(layer.mixed.at[other], layer.mixed_other)
        program.need("a3")
        for group in range(layer.groups):
            layer.add_branch(group)

    def norm_one():
        layer.norm_one()
        layer.turn(layer.hidden_low, layer.hidden_turned.at[own])
        swap("hidden", layer.hidden_turned)

    def expand(part):
        program.need("u%d" % part)
        layer.expand(part)
        if part == DENSE_PARTS - 1:
            links["activated"] = to_core(layer.activated.at[other], layer.activated_other)

    def down():
        program.need(*("d%d" % part for part in parts))
        for group in range(layer.groups):
            layer.add_down(group)

    def norm_two():
        links["cotangent"].wait()
        layer.norm_two()
        layer.turn(layer.back_low, layer.back_turned.at[own])
        swap("back", layer.back_turned)
        links["out"] = sender.start_local(layer.final, refs.out_rows.at[own])
        swaps["out"] = to_core(layer.final, refs.out_rows.at[own])

    def pre_other(part):
        if part == 0:
            sender.sent(links["activated"])
        layer.pre_gradient(other, part)
        if part == DENSE_PARTS - 1:
            links["pre"] = to_core(layer.activated.at[other], layer.pre_other)

    def pre_own(part):
        layer.pre_gradient(own, part)

    held = dict(zip(HELD, refs.held))

    def scatter(name, gradient, out):
        program.transfer(name, scatter_piece(place, sender, gradient, held[name], out, name in SQUARE_FIRST))

    def scatter_dense(name, matrix, part):
        gradient = layer.dense_grad.at[matrix, :, :, :, :, part_cols(part)]
        scatter(name, gradient, refs.dense_share.at[matrix, :, part_cols(part)])

    def scatter_attention(matrix):
        out = refs.attention_share.at[matrix]
        scatter("A%d" % matrix, layer.attention_grad.at[matrix], out)

    def down_gradient(part):
        if part == 0:
            links["activated"].wait_recv()
            swaps["back"].wait_recv()
        layer.down_gradient(part)
        scatter_dense("D%d" % part, 1, part)

    def up_gradient(part):
        if part == 0:
            links["pre"].wait_recv()
            swaps["hidden"].wait_recv()
        layer.up_gradient(part)
        scatter_dense("U%d" % part, 0, part)

    def norm_one_back():
        layer.norm_one_back()
        layer.turn(layer.back_low, layer.branch_turned.at[own])
        swap("branch", layer.branch_turned)

    def mix():
        sender.sent(links["pre"])
        for group in range(layer.groups):
            layer.mix_gradient(group)

    def out_gradient():
        links["mixed"].wait_recv()
        swaps["branch"].wait_recv()
        layer.out_gradient()
        scatter_attention(3)

    projected = []

    def attend_back(group):
        loop(layer.pairs, lambda pair: layer.attend_back(group, pair))
        if group is other:
            for matrix, ref in enumerate((layer.query_grad, layer.key_grad, layer.value_grad)):
                projected.append(to_core(ref.at[other], layer.projected_other[matrix]))

    def project_gradient(matrix):
        projected[matrix].wait_recv()
        layer.project_gradient(matrix)
        scatter_attention(matrix)

    def small_sums():
        layer.unit_totals()
        layer.head_sums()
        program.transfer("s", sum_small(place, sender, layer.sums, refs.slots))

    def input_gradient():
        layer.input_gradient()
        links["grad"] = sender.start_local(layer.wide, refs.grad_rows.at[own])
        swaps["grad"] = to_core(layer.wide, refs.grad_rows.at[own])

    def several(letter, act, count):
        for at in range(count):
            program.action(letter + str(at), functools.partial(act, at))

    program.action("start", start)
    program.action("turn", turn_tokens)
    several("q", project, 3)
    several("t", attend, layer.groups)
    program.action("branch", branch)
    program.action("n1", norm_one)
    several("e", expand, DENSE_PARTS)
    program.action("down", down)
    program.action("n2", norm_two)
    several("p", pre_other, DENSE_PARTS)
    several("g", down_gradient, DENSE_PARTS)
    several("r", pre_own, DENSE_PARTS)
    several("h", up_gradient, DENSE_PARTS)
    program.action("hidden", layer.add_hidden_gradient)
    program.action("n3", norm_one_back)
    program.action("mix", mix)
    program.action("out", out_gradient)
    program.action("x", functools.partial(attend_back, other))
    program.action("y", functools.partial(attend_back, own))
    several("z", project_gradient, 3)
    program.action("small", small_sums)
    program.action("input", input_gradient)
    for at in PLAN:
        program.run(STEPS[at])
    program.finish()
    for name in ("out", "grad"):
        swaps[name].wait_recv()
        links[name].wait()
    sender.finish()


HELD = tuple("%s%d" % (letter, part) for letter in "DU" for part in range(DENSE_PARTS)) + ("A0", "A1", "A2", "A3")


def whole_step(tokens, segment_ids, cotangent, attention_master, dense_master, head_bias, dense_bias, small):
    _, length, width = tokens.shape
    groups = 2
    rows, cols = attention_master.shape[1:]
    units = dense_master.shape[2]
    pairs = groups * cols // PAIR
    low, wide = jnp.bfloat16, jnp.float32
    vmem, anywhere = pl.BlockSpec(memory_space=pltpu.VMEM), pl.BlockSpec(memory_space=pl.ANY)
    inputs = dict(
        all_tokens=(tokens, anywhere),
        segment_ids=(segment_ids, vmem),
        cotangent=(cotangent, anywhere),
        attention_master=(attention_master, anywhere),
        dense_master=(dense_master, anywhere),
        head_shard=(head_bias, vmem),
        dense_bias_shard=(dense_bias, vmem),
        small=(small, vmem),
    )
    outputs = dict(
        out_rows=((tokens.shape, low), anywhere),
        grad_rows=((tokens.shape, wide), anywhere),
        attention_share=((attention_master.shape, wide), vmem),
        dense_share=((dense_master.shape, wide), vmem),
        sums=(((SMALL_ROWS, width), wide), vmem),
    )
    buffers = dict(
        attention_weights=((groups, 4, 4, 2, 2, rows, cols), low),
        dense_weights=((groups, 2, 4, 2, 2, rows, units), low),
        head_bias=((groups, 2, cols), wide),
        dense_bias=((groups, 1, units), wide),
        attention_grad=((4, 4, 2, 2, rows, cols), low),
        dense_grad=((2, 4, 2, 2, rows, units), low),
        tokens=(tokens.shape, low),
        token_turned=((groups, width, length), low),
        hidden_turned=((groups, width, length), low),
        back_turned=((groups, width, length), low),
        branch_turned=((groups, width, length), low),
        activated_other=((length, units), low),
        pre_other=((length, units), low),
        mixed_other=((length, cols), low),
        queries=((pairs, length, PAIR), low),
        keys=((pairs, length, PAIR), low),
        values=((pairs, length, PAIR), low),
        mixed=((groups, length, cols), low),
        log_totals=((groups, pl.cdiv(cols // HEAD_DIM, 8) * 8, length), wide),
        normed=((length, width), wide),
        inverse=((length, 1), wide),
        hidden_low=((length, width), low),
        activated=((groups, length, units), low),
        slope=((groups, length, units), wide),
        back_low=((length, width), low),
        wide=((length, width), wide),
        unit_sums=((groups, units), wide),
        segment_row=((1, length), wide),
        segment_column=((length, 1), wide),
        slots=((2 * SMALL_HOPS, SMALL_ROWS, width), wide),
    )
    scratch = {name: pltpu.VMEM(*what) for name, what in buffers.items()}
    pieces = 4 + 2 * DENSE_PARTS
    copies = pieces * (GATHER_COPIES + SCATTER_COPIES) + SMALL_HOPS + 16
    scratch["send_sems"] = pltpu.SemaphoreType.DMA((copies,))
    scratch["recv_sems"] = pltpu.SemaphoreType.DMA((copies,))
    scratch["local_sems"] = pltpu.SemaphoreType.DMA((9,))
    held = [scatter_held(rows, cols if name[0] == "A" else units // DENSE_PARTS, name in SQUARE_FIRST) for name in HELD]
    scratch["held"] = held
    return pl.pallas_call(
        functools.partial(step_kernel, tuple(inputs) + tuple(outputs) + tuple(scratch)),
        name="whole_step",
        out_shape=tuple(jax.ShapeDtypeStruct(*what) for what, _ in outputs.values()),
        in_specs=[spec for _, spec in inputs.values()],
        out_specs=tuple(spec for _, spec in outputs.values()),
        scratch_shapes=list(scratch.values()),
        compiler_params=pltpu.CompilerParams(
            collective_id=0, has_side_effects=True, vmem_limit_bytes=63 * 2**20
        ),
    )(*(value for value, _ in inputs.values()))


def finish_kernel(inputs, outputs, *refs):
    count = len(inputs) + len(outputs)
    outside = dict(zip(inputs + outputs, refs))
    inside = dict(zip(inputs + outputs, refs[count:]))
    sems = refs[-1]
    for name in ("out_rows", "grad_rows"):
        inside[name + "_new"] = inside[name]
    loads, stores = {}, []
    for at, name in enumerate(inputs):
        loads[name] = pltpu.make_async_copy(outside[name], inside[name], sems.at[at])
        loads[name].start()

    def store(name):
        copy = pltpu.make_async_copy(inside[name], outside[name], sems.at[len(inputs) + outputs.index(name)])
        copy.start()
        stores.append(copy)

    def update(name, gradients, learn_rate, weight_decay, shape=None):
        for part in ("", "_first", "_second"):
            loads[name + part].wait()
        for index, gradient in gradients:
            parts = [inside[name + part][index] for part in ("", "_first", "_second")]
            if shape is not None:
                parts = [part.reshape(shape) for part in parts]
            results = adamw(parts[0], gradient, parts[1], parts[2], learn_rate, weight_decay)
            for part, value in zip(("_new", "_first_new", "_second_new"), results):
                inside[name + part][index] = value.reshape(inside[name][index].shape)
            if name + "_copy" in inside:
                inside[name + "_copy"][index] = results[0].astype(jnp.bfloat16)
        for part in ("_new", "_first_new", "_second_new", "_copy"):
            if name + part in inside:
                store(name + part)

    for name in ("out_rows", "grad_rows"):
        loads[name].wait()
        store(name + "_new")
    for name in ("attention", "dense"):
        loads[name + "_share"].wait()
        share = inside[name + "_share"]
        update(name, ((matrix, share[matrix]) for matrix in range(share.shape[0])), 0.03, 0.01)
    own = lax.axis_index("mp")
    loads["sums"].wait()
    sums = inside["sums"]
    cols, units = inside["head"].shape[1], inside["bias"].shape[0]
    update("small", ((slice(0, 6), sums[0:6]),), 0.2, 0.0)
    heads = sums[pl.ds(10 + own, 1)]
    update("head", ((slice(row, row + 1), heads[:, row * cols : (row + 1) * cols]) for row in range(2)), 0.2, 0.0)
    totals = [sums[pl.ds(6 + 2 * own + row, 1)] for row in range(2)]
    update("bias", ((slice(None), jnp.concatenate(totals, axis=1)),), 0.2, 0.0, (1, units))
    for copy in stores:
        copy.wait()


def finish_step(step_results, attention, dense, head, bias, small):
    inputs = dict(zip(("out_rows", "grad_rows", "attention_share", "dense_share", "sums"), step_results))
    outputs = {name + "_new": inputs[name] for name in ("out_rows", "grad_rows")}
    for name, state in (("attention", attention), ("dense", dense), ("head", head), ("bias", bias), ("small", small)):
        for part, value in zip(("", "_first", "_second"), state):
            inputs[name + part] = value
            outputs[name + part + "_new"] = value
        if name in ("attention", "dense"):
            outputs[name + "_copy"] = jax.ShapeDtypeStruct(state[0].shape, jnp.bfloat16)
    anywhere = pl.BlockSpec(memory_space=pl.ANY)
    scratch = [pltpu.VMEM(value.shape, value.dtype) for value in inputs.values()]
    for name, value in outputs.items():
        scratch.append(pltpu.VMEM((8, 128) if "rows" in name else value.shape, value.dtype))
    return pl.pallas_call(
        functools.partial(finish_kernel, tuple(inputs), tuple(outputs)),
        name="finish_step",
        out_shape=tuple(jax.ShapeDtypeStruct(value.shape, value.dtype) for value in outputs.values()),
        in_specs=[anywhere] * len(inputs),
        out_specs=(anywhere,) * len(outputs),
        scratch_shapes=scratch + [pltpu.SemaphoreType.DMA((len(inputs) + len(outputs),))],
        compiler_params=pltpu.CompilerParams(vmem_limit_bytes=62 * 2**20),
    )(*inputs.values())


def plain_gather(attention_low, dense_low):
    def both(shard):
        return lax.all_gather(lax.all_gather(shard, "dp", axis=1, tiled=True), "mp", axis=0)

    return both(attention_low), both(dense_low)


def plain_scatter(attention_gradient, dense_gradient, small):
    def share(gradient):
        half = lax.psum_scatter(gradient.astype(jnp.float32), "mp", scatter_dimension=0)
        return lax.psum_scatter(half, "dp", scatter_dimension=1, tiled=True)

    return share(attention_gradient), share(dense_gradient), lax.psum(small, ("dp", "mp"))


def plain_layer(row_tokens, segment_row, upstream, attention_full, dense_full, head_bias, dense_bias, small_vectors):
    groups = attention_full.shape[0]
    length = row_tokens.shape[0]
    local_cols = attention_full.shape[3]
    local_heads = local_cols // HEAD_DIM
    allowed = (segment_row[:, None] == segment_row[None, :])[None]
    saved = []
    branch = 0.0
    for group in range(groups):
        weights = attention_full[group]
        queries = (
            (jnp.dot(row_tokens, weights[0], preferred_element_type=jnp.float32) + head_bias[group, 0]) * 0.125
        ).astype(jnp.bfloat16)
        key_rows = jnp.dot(row_tokens, weights[1], preferred_element_type=jnp.float32).astype(jnp.bfloat16)
        value_rows = (
            jnp.dot(row_tokens, weights[2], preferred_element_type=jnp.float32) + head_bias[group, 1]
        ).astype(jnp.bfloat16)
        query_heads = queries.reshape(length, local_heads, HEAD_DIM)
        key_heads = key_rows.reshape(length, local_heads, HEAD_DIM)
        value_heads = value_rows.reshape(length, local_heads, HEAD_DIM)
        scores = masked_scores(query_heads, key_heads, allowed)
        row_peak = jnp.max(scores, axis=-1, keepdims=True)
        shifted_exp = jnp.exp(scores - row_peak)
        exp_total = jnp.sum(shifted_exp, axis=-1, keepdims=True)
        attend_low = (shifted_exp / exp_total).astype(jnp.bfloat16)
        log_total = row_peak + jnp.log(exp_total)
        mixed_heads = (
            jnp.einsum("hqk,khd->qhd", attend_low, value_heads, preferred_element_type=jnp.float32)
            .reshape(length, local_cols)
            .astype(jnp.bfloat16)
        )
        partial_value = lax.dot_general(mixed_heads, weights[3], last_dims, preferred_element_type=jnp.float32)
        branch = branch + partial_value.astype(jnp.bfloat16).astype(jnp.float32)
        saved.append((query_heads, key_heads, value_heads, log_total, mixed_heads))
    hidden, normed_one, inverse_one = norm_forward(
        row_tokens.astype(jnp.float32) + branch + small_vectors[0], small_vectors[2], small_vectors[3]
    )
    hidden_low = hidden.astype(jnp.bfloat16)
    down_out = 0.0
    dense_saved = []
    for group in range(groups):
        hidden_pre = (
            jnp.dot(hidden_low, dense_full[group, 0], preferred_element_type=jnp.float32) + dense_bias[group]
        )
        activated = gelu_value(hidden_pre).astype(jnp.bfloat16)
        down_partial = lax.dot_general(
            activated, dense_full[group, 1], last_dims, preferred_element_type=jnp.float32
        )
        down_out = down_out + down_partial.astype(jnp.bfloat16).astype(jnp.float32)
        dense_saved.append((hidden_pre, activated))
    final, normed_two, inverse_two = norm_forward(
        hidden + down_out + small_vectors[1], small_vectors[4], small_vectors[5]
    )
    back_two, gain_two, shift_two = norm_backward(upstream, normed_two, inverse_two, small_vectors[4])
    down_grad = back_two.astype(jnp.bfloat16)
    hidden_grad = back_two
    dense_grads, dense_bias_grads = [], []
    for group in range(groups):
        hidden_pre, activated = dense_saved[group]
        grad_down_weight = lax.dot_general(down_grad, activated, first_dims, preferred_element_type=jnp.float32)
        pre_grad = (
            jnp.dot(down_grad, dense_full[group, 1], preferred_element_type=jnp.float32) * gelu_slope(hidden_pre)
        ).astype(jnp.bfloat16)
        grad_up_weight = lax.dot_general(hidden_low, pre_grad, first_dims, preferred_element_type=jnp.float32)
        hidden_grad = hidden_grad + lax.dot_general(
            pre_grad, dense_full[group, 0], last_dims, preferred_element_type=jnp.float32
        )
        dense_grads.append(jnp.stack([grad_up_weight, grad_down_weight]))
        dense_bias_grads.append(jnp.sum(pre_grad.astype(jnp.float32), axis=0))
    back_one, gain_one, shift_one = norm_backward(hidden_grad, normed_one, inverse_one, small_vectors[2])
    small_grad = jnp.stack(
        [jnp.sum(back_one, axis=0), jnp.sum(back_two, axis=0), gain_one, shift_one, gain_two, shift_two]
    )
    branch_grad = back_one.astype(jnp.bfloat16)
    input_rows = back_one
    attention_grads, head_grads = [], []
    for group in range(groups):
        weights = attention_full[group]
        query_heads, key_heads, value_heads, log_total, mixed_heads = saved[group]
        grad_out_weight = lax.dot_general(branch_grad, mixed_heads, first_dims, preferred_element_type=jnp.float32)
        mixed_grad = (
            jnp.dot(branch_grad, weights[3], preferred_element_type=jnp.float32)
            .astype(jnp.bfloat16)
            .reshape(length, local_heads, HEAD_DIM)
        )
        attend = jnp.exp(masked_scores(query_heads, key_heads, allowed) - log_total)
        attend_low = attend.astype(jnp.bfloat16)
        prob_grad = jnp.einsum("qhd,khd->hqk", mixed_grad, value_heads, preferred_element_type=jnp.float32)
        value_grad = jnp.einsum(
            "hqk,qhd->khd", attend_low, mixed_grad, preferred_element_type=jnp.float32
        ).astype(jnp.bfloat16)
        inner_total = jnp.sum(attend * prob_grad, axis=-1, keepdims=True)
        score_grad = (attend * (prob_grad - inner_total)).astype(jnp.bfloat16)
        query_grad = (
            jnp.einsum("hqk,khd->qhd", score_grad, key_heads, preferred_element_type=jnp.float32).astype(jnp.bfloat16)
            * 0.125
        )
        key_grad = jnp.einsum(
            "hqk,qhd->khd", score_grad, query_heads, preferred_element_type=jnp.float32
        ).astype(jnp.bfloat16)
        stacked = [each.reshape(length, local_cols) for each in (query_grad, key_grad, value_grad)]
        grads = [
            lax.dot_general(row_tokens, each, first_dims, preferred_element_type=jnp.float32) for each in stacked
        ]
        for each, weight in zip(stacked, weights[:3]):
            input_rows = input_rows + lax.dot_general(each, weight, last_dims, preferred_element_type=jnp.float32)
        attention_grads.append(jnp.stack(grads + [grad_out_weight]))
        head_grads.append(
            jnp.stack(
                [jnp.sum(stacked[0].astype(jnp.float32), axis=0), jnp.sum(stacked[2].astype(jnp.float32), axis=0)]
            )
        )
    return (
        final.astype(jnp.bfloat16),
        input_rows,
        jnp.stack(attention_grads).astype(jnp.bfloat16),
        jnp.stack(dense_grads).astype(jnp.bfloat16),
        jnp.stack(head_grads),
        jnp.stack(dense_bias_grads),
        small_grad,
    )


def plain_step(tokens, segment_ids, cotangent, attention_master, dense_master, head_bias, dense_bias, small_vectors):
    attention_full, dense_full = plain_gather(attention_master.astype(jnp.bfloat16), dense_master.astype(jnp.bfloat16))
    head_full = lax.all_gather(head_bias, "mp", axis=0)
    dense_bias_full = lax.all_gather(dense_bias, "mp", axis=0)
    mine = lax.axis_index("mp")
    row_tokens = lax.dynamic_index_in_dim(tokens, mine, 0, keepdims=False)
    segment_row = lax.dynamic_index_in_dim(segment_ids, mine, 0, keepdims=False)
    upstream = lax.dynamic_index_in_dim(cotangent, mine, 0, keepdims=False).astype(jnp.float32)
    final, input_rows, attention_grad, dense_grad, head_grad, dense_bias_grad, small_grad = plain_layer(
        row_tokens, segment_row, upstream, attention_full, dense_full, head_full, dense_bias_full, small_vectors
    )
    width = tokens.shape[2]
    sums = jnp.concatenate([part.reshape(-1, width) for part in (small_grad, dense_bias_grad, head_grad)])
    attention_share, dense_share, sums = plain_scatter(attention_grad, dense_grad, sums)
    out_rows, grad_rows = (lax.all_gather(rows, "mp", axis=0) for rows in (final, input_rows))
    return out_rows, grad_rows, attention_share, dense_share, sums


def make_local(mesh):
    n_dp, n_mp = mesh.shape["dp"], mesh.shape["mp"]
    square = n_dp == 16 and n_mp == 2

    def local(
        tokens,
        segment_ids,
        cotangent,
        attention_master,
        attention_first,
        attention_second,
        dense_master,
        dense_first,
        dense_second,
        head_bias,
        head_bias_first,
        head_bias_second,
        dense_bias,
        dense_bias_first,
        dense_bias_second,
        small_vectors,
        small_first,
        small_second,
    ):
        states = (
            (attention_master, attention_first, attention_second),
            (dense_master, dense_first, dense_second),
            (head_bias, head_bias_first, head_bias_second),
            (dense_bias, dense_bias_first, dense_bias_second),
            (small_vectors, small_first, small_second),
        )
        step = whole_step if square else plain_step
        results = step(
            tokens, segment_ids, cotangent, attention_master, dense_master, head_bias, dense_bias, small_vectors
        )
        if square:
            return finish_step(results, *states)
        out_rows, grad_rows, attention_share, dense_share, sums = results
        mine = lax.axis_index("mp")
        width, cols, units = tokens.shape[2], head_bias.shape[1], dense_bias.shape[0]
        small_sum = sums[:6]
        dense_bias_sum = lax.dynamic_slice(sums, (6 + 2 * mine, 0), (2, width)).reshape(units)
        head_sum = lax.dynamic_slice(sums, (10 + mine, 0), (1, width)).reshape(2, cols)
        attention_new = adamw(attention_master, attention_share, attention_first, attention_second, 0.03, 0.01)
        dense_new = adamw(dense_master, dense_share, dense_first, dense_second, 0.03, 0.01)
        head_new = adamw(head_bias, head_sum, head_bias_first, head_bias_second, 0.2, 0.0)
        dbias_new = adamw(dense_bias, dense_bias_sum, dense_bias_first, dense_bias_second, 0.2, 0.0)
        small_new = adamw(small_vectors, small_sum, small_first, small_second, 0.2, 0.0)
        return (
            out_rows,
            grad_rows,
            *attention_new,
            attention_new[0].astype(jnp.bfloat16),
            *dense_new,
            dense_new[0].astype(jnp.bfloat16),
            *head_new,
            *dbias_new,
            *small_new,
        )

    return local


def solution(mesh):
    rows, matrix, halves, units = P("dp", None, None), P(None, "dp", "mp"), P(None, "mp"), P("mp")
    return jax.shard_map(
        make_local(mesh),
        mesh=mesh,
        in_specs=(rows, P("dp", None), rows) + (matrix,) * 6 + (halves,) * 3 + (units,) * 3 + (P(),) * 3,
        out_specs=(rows,) * 2 + (matrix,) * 8 + (halves,) * 3 + (units,) * 3 + (P(),) * 3,
        check_vma=False,
    )
```
